32 devices in a mesh: parts: 2 (over x), harm: 4 (over y, core), tile: 4 (over z).
Axes of the slice: x: 2, y: 2, z: 4, core: 2. Of those that a mesh axis runs over, the one named last changes fastest.
Arguments:
- perturbation: float32 [8, 2, 5, 128, 256], P('harm', None, None, ('parts', 'tile')), parts along dimension 3, may hold values from -6 to 6
- base_flow: float32 [8, 2, 3, 128, 256], P('harm', None, None, ('parts', 'tile')), parts along dimension 3, may hold values from -0.9 to 0.9
- viscosity: float32 [128, 256], P(('parts', 'tile')), parts along dimension 0, may hold values from 0.05 to 0.5
Outputs:
- resolvent_image: float32 [8, 2, 5, 128, 256], P('harm', None, None, ('parts', 'tile')), parts along dimension 3
The draws below stay inside these ranges and needn't reach their ends.
There are 2 independent parts, one for each index of `parts`. The reference program is written for one: setup_inputs(seed, part) draws one part's arguments, and reference() takes and returns one part's arrays. A program takes and returns all parts, laid end to end along the dimension named above; each array names one. Nothing has to cross between parts.
All inputs are finite; a program needn't handle non-finite values.
Results may differ from the reference program's by a relative error of at most 0.00002.
Values sent between devices are 32-bit elements; how exact they have to be, the bound alone decides.
A program may use at most 64 MiB of HBM per device.

```python
import math
import jax
import jax.numpy as jnp
from jax import lax

FIELDS = 5
CY = 256
NH = 8
NXG = 64


def shard_levels(stream_key, dims, split, smallest, high):
    level, own = 1.0, jax.random.fold_in(stream_key, 6)
    for axis_at, parts in split:
        steps = jnp.exp(jax.random.uniform(jax.random.fold_in(own, axis_at), (parts,), jnp.float32, smallest / len(split), high / len(split)))
        level = level * jnp.repeat(steps, dims[axis_at] // parts).reshape([-1 if axis == axis_at else 1 for axis in range(len(dims))])
    return level


def scatter_about(own_key, dims, width, limit, shards=(), kind=jnp.bfloat16):
    drawn = width * jax.random.normal(own_key, dims, jnp.float32)
    if shards:
        drawn = drawn * shard_levels(own_key, dims, shards, -0.22, 0.18)
    return jnp.clip(drawn, -limit, limit).astype(kind)


def setup_inputs(seed: int = 0, part: int = 0) -> dict:
    streams_of = jax.random.split(jax.random.key(seed), 4)
    part_keys = jax.random.split(jax.random.fold_in(streams_of[3], part), 4)
    return {
        "perturbation": scatter_about(part_keys[0], (NH, 2, FIELDS, NXG, CY), 1.0, 6.0, ((0, 4), (3, 4)), jnp.float32),
        "base_flow": scatter_about(part_keys[1], (NH, 2, 3, NXG, CY), 0.15, 0.9, ((0, 4), (3, 4)), jnp.float32),
        "viscosity": jnp.clip(jnp.exp(math.log(0.5) - 2.3025851 * jax.random.uniform(part_keys[2], (NXG, CY), jnp.float32) ** shard_levels(part_keys[2], (NXG, CY), ((0, 4),), -0.2, 0.2)), 0.05, 0.5),
    }


omega_base = 0.25


def along_first(values):
    return 0.5 * (jnp.roll(values, -1, -2) - jnp.roll(values, 1, -2))


def along_second(values):
    return 0.5 * (jnp.roll(values, -1, -1) - jnp.roll(values, 1, -1))


def diffusion(values, viscosity):
    east_face = 0.5 * (viscosity + jnp.roll(viscosity, -1, -2))
    west_face = 0.5 * (viscosity + jnp.roll(viscosity, 1, -2))
    north_face = 0.5 * (viscosity + jnp.roll(viscosity, -1, -1))
    south_face = 0.5 * (viscosity + jnp.roll(viscosity, 1, -1))
    return (east_face * (jnp.roll(values, -1, -2) - values) - west_face * (values - jnp.roll(values, 1, -2))
            + north_face * (jnp.roll(values, -1, -1) - values) - south_face * (values - jnp.roll(values, 1, -1)))


def acoustic(grad_x, grad_y):
    dilation = grad_x[..., 1, :, :] + grad_y[..., 2, :, :]
    return jnp.stack([dilation, grad_x[..., 4, :, :], grad_y[..., 4, :, :], jnp.zeros_like(dilation), dilation], axis=-3)


def own_terms(middle, grad_x, grad_y, damping, frequency):
    rotation = jnp.stack([-frequency * middle[:, 1], frequency * middle[:, 0]], axis=1)
    return rotation + acoustic(grad_x, grad_y) - damping


def coupling(u_real, u_imag, v_real, v_imag, g_real, g_imag, q_real, q_imag, x_real, x_imag, y_real, y_imag):
    real_part = u_real * x_real - u_imag * x_imag + v_real * y_real - v_imag * y_imag + g_real * q_real - g_imag * q_imag
    imag_part = u_real * x_imag + u_imag * x_real + v_real * y_imag + v_imag * y_real + g_real * q_imag + g_imag * q_real
    return real_part, imag_part


def reference(perturbation, base_flow, viscosity):
    grad_x = along_first(perturbation)
    grad_y = along_second(perturbation)
    numbers = jnp.arange(NH, dtype=jnp.int32)
    signed = jnp.where(numbers < NH // 2, numbers, numbers - NH)
    frequency = (omega_base * signed.astype(jnp.float32)).reshape(NH, 1, 1, 1)
    summed = own_terms(perturbation, grad_x, grad_y, diffusion(perturbation, viscosity), frequency)

    def add_source(source, summed):
        shifted = jnp.roll(base_flow, source, axis=0)
        values = lax.dynamic_index_in_dim(perturbation, source, 0, keepdims=False)
        slope_x = lax.dynamic_index_in_dim(grad_x, source, 0, keepdims=False)
        slope_y = lax.dynamic_index_in_dim(grad_y, source, 0, keepdims=False)
        real_part, imag_part = coupling(
            shifted[:, 0, 0][:, None], shifted[:, 1, 0][:, None],
            shifted[:, 0, 1][:, None], shifted[:, 1, 1][:, None],
            shifted[:, 0, 2][:, None], shifted[:, 1, 2][:, None],
            values[0], values[1], slope_x[0], slope_x[1], slope_y[0], slope_y[1])
        return summed + jnp.stack([real_part, imag_part], axis=1)

    summed = lax.fori_loop(0, NH, add_source, summed)
    return summed
```

```python
import functools

import jax
import jax.numpy as jnp
from jax import lax
from jax.experimental import pallas as pl
from jax.experimental.pallas import tpu as pltpu
from jax.sharding import PartitionSpec as P

omega_base = 0.25
MESH = pl.DeviceIdType.MESH


def kernel(
    groups,
    tiles,
    p_hbm,
    b_hbm,
    v_hbm,
    out,
    pbuf,
    bbuf,
    vbuf,
    stage,
    rims,
    gx,
    gy,
    local_sem,
    y_send,
    y_recv,
    chip_send,
    chip_recv,
    z_send,
    z_recv,
    rim_send,
    rim_recv,
):
    local, _, fields, rows, width = p_hbm.shape
    total = pbuf.shape[0]
    cores = 2
    chips = groups // cores
    rim_rows = local * 2 * fields
    me = lax.axis_index("harm")
    chip, core = me // cores, me % cores
    place = lax.axis_index("tile")
    partner = chip * cores + (1 - core)
    above, below = (place + 1) % tiles, (place + tiles - 1) % tiles

    def group_at(distance, own_core):
        at = (chip + chips - distance) % chips
        return at * cores + (core if own_core else 1 - core)

    def target_at(distance):
        return (chip + distance) % chips * cores + core

    first = me * local

    copy_p = pltpu.make_async_copy(p_hbm, pbuf.at[pl.ds(first, local)], local_sem.at[0])
    copy_b = pltpu.make_async_copy(b_hbm, bbuf.at[pl.ds(first, local)], local_sem.at[1])
    copy_v = pltpu.make_async_copy(v_hbm, vbuf, local_sem.at[2])
    copy_p.start()
    copy_v.start()
    copy_b.start()

    barrier = pltpu.get_barrier_semaphore()
    for distance in range(1, chips):
        pl.semaphore_signal(
            barrier, inc=1, device_id={"harm": target_at(distance)}, device_id_type=MESH
        )
    pl.semaphore_signal(barrier, inc=1, device_id={"harm": partner}, device_id_type=MESH)
    pl.semaphore_signal(barrier, inc=1, device_id={"tile": above}, device_id_type=MESH)
    pl.semaphore_signal(barrier, inc=1, device_id={"tile": below}, device_id_type=MESH)

    def pack(distance):
        start = group_at(distance, True) * local
        for index in range(local):
            for part in range(2):
                for field in range(fields):
                    row = (index * 2 + part) * fields + field
                    stage[distance, 0, row : row + 1, :] = pbuf[start + index, part, field, 0:1, :]
                    stage[distance, 1, row : row + 1, :] = pbuf[
                        start + index, part, field, rows - 1 : rows, :
                    ]

    copy_p.wait()
    copy_v.wait()
    pack(0)
    stage[0, 0, rim_rows : rim_rows + 1, :] = vbuf[0:1, :]
    stage[0, 1, rim_rows : rim_rows + 1, :] = vbuf[rows - 1 : rows, :]

    pl.semaphore_wait(barrier, chips + 2)

    y_copies = []
    for kind in range(2):
        source, dest = ((p_hbm, pbuf), (b_hbm, bbuf))[kind]
        for index in range(local):
            for distance in range(1, chips):
                copy = pltpu.make_async_remote_copy(
                    src_ref=source.at[index],
                    dst_ref=dest.at[first + index],
                    send_sem=y_send.at[distance - 1, kind, index],
                    recv_sem=y_recv.at[distance - 1, kind, index],
                    device_id={"harm": target_at(distance)},
                    device_id_type=MESH,
                )
                copy.start()
                y_copies.append((distance, kind, index, copy))

    def rim_copies(distance):
        group = group_at(distance, True)
        return [
            pltpu.make_async_remote_copy(
                src_ref=stage.at[distance, side],
                dst_ref=rims.at[group, 1 - side],
                send_sem=z_send.at[distance, side],
                recv_sem=z_recv.at[distance, side],
                device_id={"tile": (below, above)[side]},
                device_id_type=MESH,
            )
            for side in range(2)
        ]

    started = []
    rim_pending = {}

    def send_rims(distance):
        rim_pending[distance] = rim_copies(distance)
        for copy in rim_pending[distance]:
            copy.start()

    def relay_copy(distance, kind, index):
        at = group_at(distance, True) * local + index
        dest = (pbuf, bbuf)[kind]
        source = dest.at[at] if distance else (p_hbm, b_hbm)[kind].at[index]
        return pltpu.make_async_remote_copy(
            src_ref=source,
            dst_ref=dest.at[at],
            send_sem=chip_send.at[distance, kind, index],
            recv_sem=chip_recv.at[distance, kind, index],
            device_id={"harm": partner},
            device_id_type=MESH,
        )

    relays = {}

    def relay(distance, kind, index):
        relays[distance, kind, index] = relay_copy(distance, kind, index)
        relays[distance, kind, index].start()

    def relay_rims(distance):
        group = group_at(distance, True)
        relays[distance] = pltpu.make_async_remote_copy(
            src_ref=rims.at[group],
            dst_ref=rims.at[group],
            send_sem=rim_send.at[distance],
            recv_sem=rim_recv.at[distance],
            device_id={"harm": partner},
            device_id_type=MESH,
        )
        relays[distance].start()

    send_rims(0)
    for kind in range(2):
        for index in range(local):
            relay(0, kind, index)

    row_at = lax.broadcasted_iota(jnp.int32, (rows, width), 0)

    def neighbours(value, low, high):
        east = jnp.where(row_at == rows - 1, high, pltpu.roll(value, rows - 1, 0))
        west = jnp.where(row_at == 0, low, pltpu.roll(value, 1, 0))
        return east, west

    def slope_y(group):
        def one(index, _):
            at = group * local + index
            for part in range(2):
                for field in range(fields):
                    value = pbuf[at, part, field]
                    gy[at, part, field] = 0.5 * (
                        pltpu.roll(value, width - 1, 1) - pltpu.roll(value, 1, 1)
                    )
            return 0

        lax.fori_loop(0, local, one, 0)

    def slope_x(group):
        for index in range(local):
            at = group * local + index
            for part in range(2):
                for field in range(fields):
                    row = (index * 2 + part) * fields + field
                    east, west = neighbours(
                        pbuf[at, part, field],
                        rims[group, 0, row : row + 1, :],
                        rims[group, 1, row : row + 1, :],
                    )
                    gx[at, part, field] = 0.5 * (east - west)

    def own_terms():
        center = vbuf[...]
        east, west = neighbours(
            center,
            rims[me, 0, rim_rows : rim_rows + 1, :],
            rims[me, 1, rim_rows : rim_rows + 1, :],
        )
        east_face = 0.5 * (center + east)
        west_face = 0.5 * (center + west)
        north_face = 0.5 * (center + pltpu.roll(center, width - 1, 1))
        south_face = 0.5 * (center + pltpu.roll(center, 1, 1))
        for index in range(local):
            at = first + index
            signed = jnp.where(at < total // 2, at, at - total)
            frequency = omega_base * signed.astype(jnp.float32)
            for part in range(2):
                for field in range(fields):
                    row = (index * 2 + part) * fields + field
                    value = pbuf[at, part, field]
                    up, down = neighbours(
                        value,
                        rims[me, 0, row : row + 1, :],
                        rims[me, 1, row : row + 1, :],
                    )
                    damping = (
                        east_face * (up - value)
                        - west_face * (value - down)
                        + north_face * (pltpu.roll(value, width - 1, 1) - value)
                        - south_face * (value - pltpu.roll(value, 1, 1))
                    )
                    turned = pbuf[at, 1 - part, field] * frequency
                    result = turned - damping if part else -turned - damping
                    if field == 0 or field == 4:
                        result = result + (gx[at, part, 1] + gy[at, part, 2])
                    elif field == 1:
                        result = result + gx[at, part, 4]
                    elif field == 2:
                        result = result + gy[at, part, 4]
                    out[index, part, field] = result

    def couple(at):
        def strip(step, _):
            span = pl.ds(pl.multiple_of(step * 8, 8), 8)
            base = [[bbuf[at, part, which, span, :] for part in range(2)] for which in range(3)]
            for index in range(local):
                source = (first + index + total - at) % total
                for field in range(fields):
                    real = out[index, 0, field, span, :]
                    imag = out[index, 1, field, span, :]
                    for which, values in ((0, gx), (1, gy), (2, pbuf)):
                        a_real, a_imag = base[which]
                        q_real = values[source, 0, field, span, :]
                        q_imag = values[source, 1, field, span, :]
                        real = real + a_real * q_real - a_imag * q_imag
                        imag = imag + a_real * q_imag + a_imag * q_real
                    out[index, 0, field, span, :] = real
                    out[index, 1, field, span, :] = imag
            return 0

        lax.fori_loop(0, rows // 8, strip, 0)

    def wait_y(distance, kind, index):
        for other, what, which, copy in y_copies:
            if (other, what, which) == (distance, kind, index):
                copy.wait_recv()

    slope_y(me)
    for copy in rim_pending[0]:
        copy.wait_recv()
    relay_rims(0)
    slope_x(me)
    own_terms()
    for index in range(local):
        relays[0, 0, index].wait_recv()
    slope_y(partner)
    relays[0].wait_recv()
    slope_x(partner)

    for distance in range(1, chips):
        for index in range(local):
            wait_y(distance, 0, index)
            relay(distance, 0, index)
        pack(distance)
        send_rims(distance)
    for distance in range(1, chips):
        slope_y(group_at(distance, True))
        for index in range(local):
            relays[distance, 0, index].wait_recv()
        slope_y(group_at(distance, False))
    for distance in range(1, chips):
        for index in range(local - 1):
            wait_y(distance, 1, index)
            relay(distance, 1, index)
    for distance in range(1, chips):
        for copy in rim_pending[distance]:
            copy.wait_recv()
        relay_rims(distance)
        slope_x(group_at(distance, True))
    for distance in range(1, chips):
        relays[distance].wait_recv()
        slope_x(group_at(distance, False))

    copy_b.wait()
    for index in range(local):
        couple(first + index)
    for index in range(local):
        relays[0, 1, index].wait_recv()
        couple(partner * local + index)
    for distance in range(1, chips):
        wait_y(distance, 1, local - 1)
        relay(distance, 1, local - 1)
    for distance in range(1, chips):
        for index in range(local):
            couple(group_at(distance, True) * local + index)
    for distance in range(1, chips):
        for index in range(local):
            relays[distance, 1, index].wait_recv()
            couple(group_at(distance, False) * local + index)

    for _, _, _, copy in y_copies:
        copy.wait_send()
    for copies in rim_pending.values():
        for copy in copies:
            copy.wait_send()
    for copy in relays.values():
        copy.wait_send()


def shards(perturbation, base_flow, viscosity):
    local, parts, fields, rows, width = perturbation.shape
    groups = lax.axis_size("harm")
    tiles = lax.axis_size("tile")
    chips = groups // 2
    cols = width // groups
    if (
        chips == 2
        and tiles > 2
        and rows == 16
        and 2 * cols == 128
        and 2 * local * parts * fields <= cols
    ):
        return quarters(perturbation, base_flow, viscosity)
    total = local * groups
    rim = -(-(local * parts * fields + 1) // 8) * 8
    kinds = base_flow.shape[2]
    dma = pltpu.SemaphoreType.DMA
    f32 = jnp.float32
    return pl.pallas_call(
        functools.partial(kernel, groups, tiles),
        out_shape=jax.ShapeDtypeStruct(perturbation.shape, f32),
        in_specs=[pl.BlockSpec(memory_space=pl.ANY)] * 3,
        out_specs=pl.BlockSpec(memory_space=pltpu.VMEM),
        scratch_shapes=[
            pltpu.VMEM((total, 2, fields, rows, width), f32),
            pltpu.VMEM((total, 2, kinds, rows, width), f32),
            pltpu.VMEM((rows, width), f32),
            pltpu.VMEM((chips, 2, rim, width), f32),
            pltpu.VMEM((groups, 2, rim, width), f32),
            pltpu.VMEM((total, 2, fields, rows, width), f32),
            pltpu.VMEM((total, 2, fields, rows, width), f32),
            dma((3,)),
            dma((chips - 1, 2, local)),
            dma((chips - 1, 2, local)),
            dma((chips, 2, local)),
            dma((chips, 2, local)),
            dma((chips, 2)),
            dma((chips, 2)),
            dma((chips,)),
            dma((chips,)),
        ],
        compiler_params=pltpu.CompilerParams(collective_id=0, has_side_effects=True),
    )(perturbation, base_flow, viscosity)


def quarter_kernel(
    groups,
    tiles,
    p_hbm,
    b_hbm,
    v_hbm,
    own,
    back,
    full,
    base,
    vbuf,
    stage,
    zrims,
    rim_out,
    rim_in,
    rim_rows,
    b_out,
    b_in,
    p_out,
    p_in,
    gx,
    gy,
    sent,
    load_sem,
    g_send,
    g_recv,
    z_send,
    z_recv,
    ready_up,
    ready_down,
):
    local, _, fields, rows, width = p_hbm.shape
    kinds = b_hbm.shape[2]
    harmonics = local * groups
    half = rows // 2
    cols = width // groups
    lanes = 2 * cols
    pairs = 2 * local
    values = pairs * fields
    deep = values // 2
    halo = kinds * pairs
    me = lax.axis_index("harm")
    chip, core = me // 2, me % 2
    place = lax.axis_index("tile")
    partner = chip * 2 + (1 - core)
    across = (1 - chip) * 2 + core
    corner = (1 - chip) * 2 + (1 - core)
    peers = (across, corner, partner)
    everyone = (me, partner, across, corner)
    above, below = (place + 1) % tiles, (place + tiles - 1) % tiles
    inner, lowest, highest = place < tiles - 1, place == 0, place == tiles - 1

    loads = [
        pltpu.make_async_copy(source, dest, load_sem.at[at])
        for at, (source, dest) in enumerate(((b_hbm, base), (p_hbm, full), (v_hbm, vbuf)))
    ]
    for copy in loads:
        copy.start()

    def tell(semaphore, where):
        for group in everyone:
            pl.semaphore_signal(
                semaphore, inc=1, device_id={"harm": group, "tile": where}, device_id_type=MESH
            )

    barrier = pltpu.get_barrier_semaphore()
    for group in peers:
        pl.semaphore_signal(barrier, inc=1, device_id={"harm": group}, device_id_type=MESH)

    @pl.when(inner)
    def _():
        tell(barrier, above)

    @pl.when(lowest)
    def _():
        tell(barrier, below)

    lane = lax.broadcasted_iota(jnp.int32, (half, lanes), 1)
    sub = lax.broadcasted_iota(jnp.int32, (half, lanes), 0)
    left = lane < cols
    column = lane % cols

    def turn(value, shift):
        return pltpu.roll(value, shift % lanes, 1)

    def packed(ref, at):
        blocks = []
        for tile in range(width // lanes):
            span = slice(tile * lanes, (tile + 1) * lanes)
            top = ref[(*at, slice(0, half), span)]
            bottom = ref[(*at, slice(half, rows), span)]
            blocks.append(jnp.where(left, top, turn(bottom, cols)))
            blocks.append(jnp.where(left, turn(top, cols), bottom))
        return blocks

    loads[0].wait()
    for index in range(local):
        for part in range(2):
            for which in range(kinds):
                for group, block in enumerate(packed(base, (index, part, which))):
                    b_out[group, (index * 2 + part) * kinds + which] = block

    loads[1].wait()
    loads[2].wait()
    halos = [jnp.zeros((half, lanes), jnp.float32) for _ in range(groups)]
    for field in range(fields):
        for index in range(local):
            for part in range(2):
                number = field * pairs + index * 2 + part
                blocks = packed(full, (index, part, field))
                for group, block in enumerate(blocks):
                    p_out[field, group, index * 2 + part] = block
                    low = turn(blocks[(group - 1) % groups], 2 * number + 2 - cols)
                    high = turn(blocks[(group + 1) % groups], 2 * number + cols)
                    halos[group] = jnp.where(
                        column == 2 * number + 1,
                        low,
                        jnp.where(column == 2 * number, high, halos[group]),
                    )
                at = number % deep
                stage[0, number // deep, at : at + 1, :] = full[index, part, field, 0:1, :]
                stage[1, number // deep, at : at + 1, :] = full[
                    index, part, field, rows - 1 : rows, :
                ]
    for group in range(groups):
        b_out[group, halo] = halos[group]
    stage[0, 0, deep : deep + 1, :] = vbuf[0:1, :]
    stage[1, 0, deep : deep + 1, :] = vbuf[rows - 1 : rows, :]
    low_lane = lax.broadcasted_iota(jnp.int32, (deep, lanes), 1) < cols
    for side in range(2):
        for group in range(groups):
            tile, odd = group * cols // lanes, group * cols % lanes
            span = slice(tile * lanes, (tile + 1) * lanes)
            first = stage[side, 0, 0:deep, span]
            second = stage[side, 1, 0:deep, span]
            if side == 0:
                first, second = second, first
            if odd:
                first = turn(first, cols)
            else:
                second = turn(second, cols)
            rim_out[side, group] = jnp.where(low_lane, first, second)

    def remote(source, dest, send, recv, at, device):
        return pltpu.make_async_remote_copy(
            src_ref=source,
            dst_ref=dest,
            send_sem=send.at[at],
            recv_sem=recv.at[at],
            device_id=device,
            device_id_type=MESH,
        )

    def base_copy(slot):
        return remote(
            b_out.at[peers[slot]], b_in.at[me], g_send, g_recv, (0, slot), {"harm": peers[slot]}
        )

    def field_copy(field, slot):
        return remote(
            p_out.at[field, peers[slot]],
            p_in.at[field, me],
            g_send,
            g_recv,
            (1 + field, slot),
            {"harm": peers[slot]},
        )

    def back_copy(field, slot):
        return remote(
            sent.at[field, peers[slot]],
            back.at[field, me],
            g_send,
            g_recv,
            (1 + fields + field, slot),
            {"harm": peers[slot]},
        )

    def rim_copy(side, slot):
        where = (below, above)[side]
        if slot == len(everyone):
            return remote(
                stage.at[side],
                zrims.at[side],
                z_send,
                z_recv,
                (side, slot),
                {"harm": me, "tile": where},
            )
        return remote(
            rim_out.at[side, everyone[slot]],
            rim_in.at[side, me],
            z_send,
            z_recv,
            (side, slot),
            {"harm": everyone[slot], "tile": where},
        )

    def send_rims(side):
        for slot in range(len(everyone) + 1):
            rim_copy(side, slot).start()

    pl.semaphore_wait(
        barrier,
        len(peers)
        + groups * (place > 0).astype(jnp.int32)
        + groups * highest.astype(jnp.int32),
    )

    @pl.when(place > 0)
    def _():
        tell(ready_up, below)
        send_rims(0)

    @pl.when(highest)
    def _():
        tell(ready_down, above)
        send_rims(1)

    def send_field(field):
        for slot in range(len(peers)):
            field_copy(field, slot).start()

    early = min(3, fields)
    for slot in range(len(peers)):
        base_copy(slot).start()
    for field in range(early):
        send_field(field)

    @pl.when(inner)
    def _():
        pl.semaphore_wait(ready_up, groups)
        send_rims(1)

    @pl.when(lowest)
    def _():
        pl.semaphore_wait(ready_down, groups)
        send_rims(0)

    for field in range(early, fields):
        send_field(field)

    b_in[me] = b_out[me]
    for field in range(fields):
        p_in[field, me] = p_out[field, me]

    for side in range(2):
        for slot in range(len(everyone)):
            rim_copy(side, slot).wait_recv()
    for group in range(groups):
        above_rows, below_rows = rim_in[0, group], rim_in[1, group]
        rim_rows[group, 0:deep, :] = jnp.where(low_lane, below_rows, above_rows)
        rim_rows[group, deep:values, :] = turn(jnp.where(low_lane, above_rows, below_rows), cols)
    for slot in range(len(peers)):
        base_copy(slot).wait_recv()

    def one_field(field, _):
        for slot in range(len(peers)):
            field_copy(field, slot).wait_recv()
        for group in range(groups):
            for pair in range(pairs):
                number = field * pairs + pair
                value = p_in[field, group, pair]
                edge = pltpu.roll(b_in[group, halo], lanes - 1 - 2 * number, 1)
                north = jnp.where(column == cols - 1, edge, turn(value, -1))
                south = jnp.where(column == 0, edge, turn(value, 1))
                gy[group * pairs + pair] = 0.5 * (north - south)
                swapped = turn(value, cols)
                rim = rim_rows[group, pl.ds(number, 1), :]
                high = jnp.where(left, swapped, rim)
                low = jnp.where(left, rim, swapped)
                east = pltpu.roll(jnp.where(sub == 0, high, value), half - 1, 0)
                west = pltpu.roll(jnp.where(sub == half - 1, low, value), 1, 0)
                gx[group * pairs + pair] = 0.5 * (east - west)
        sums = [None] * (2 * harmonics)
        for source in range(harmonics):
            group, at = source // local, source % local * 2
            moved = (
                (gx[2 * source], gx[2 * source + 1]),
                (gy[2 * source], gy[2 * source + 1]),
                (p_in[field, group, at], p_in[field, group, at + 1]),
            )
            for target in range(harmonics):
                shift = (target - source) % harmonics
                owner, first = shift // local, shift % local * 2 * kinds
                real, imag = sums[2 * target], sums[2 * target + 1]
                for which in range(kinds):
                    a_real = b_in[owner, first + which]
                    a_imag = b_in[owner, first + kinds + which]
                    q_real, q_imag = moved[which]
                    if real is None:
                        real = a_real * q_real - a_imag * q_imag
                        imag = a_real * q_imag + a_imag * q_real
                    else:
                        real = real + a_real * q_real - a_imag * q_imag
                        imag = imag + a_real * q_imag + a_imag * q_real
                sums[2 * target], sums[2 * target + 1] = real, imag
        for target in range(harmonics):
            for part in range(2):
                sent[field, target // local, target % local * 2 + part] = sums[2 * target + part]
        for slot in range(len(peers)):
            back_copy(field, slot).start()
        back[field, me] = sent[field, me]
        return 0

    lax.fori_loop(0, fields, one_field, 0)

    for side in range(2):
        rim_copy(side, len(everyone)).wait_recv()

    row_at = lax.broadcasted_iota(jnp.int32, (rows, width), 0)

    def neighbours(value, number, at):
        high, low = zrims[0, number, at : at + 1, :], zrims[1, number, at : at + 1, :]
        east = jnp.where(row_at == rows - 1, high, pltpu.roll(value, rows - 1, 0))
        west = jnp.where(row_at == 0, low, pltpu.roll(value, 1, 0))
        return east, west

    def north_of(value):
        return pltpu.roll(value, width - 1, 1)

    def south_of(value):
        return pltpu.roll(value, 1, 1)

    center = vbuf[...]
    east, west = neighbours(center, 0, deep)
    east_face = 0.5 * (center + east)
    west_face = 0.5 * (center + west)
    north_face = 0.5 * (center + north_of(center))
    south_face = 0.5 * (center + south_of(center))
    for index in range(local):
        at = me * local + index
        signed = jnp.where(at < harmonics // 2, at, at - harmonics)
        frequency = omega_base * signed.astype(jnp.float32)
        for part in range(2):

            def sides(field):
                number = field * pairs + index * 2 + part
                return neighbours(full[index, part, field], number // deep, number % deep)

            def along_x(field):
                up, down = sides(field)
                return 0.5 * (up - down)

            def along_y(field):
                value = full[index, part, field]
                return 0.5 * (north_of(value) - south_of(value))

            dilation = along_x(1) + along_y(2)
            sound = {0: dilation, 4: dilation, 1: along_x(4), 2: along_y(4)}
            for field in range(fields):
                value = full[index, part, field]
                up, down = sides(field)
                damping = (
                    east_face * (up - value)
                    - west_face * (value - down)
                    + north_face * (north_of(value) - value)
                    - south_face * (value - south_of(value))
                )
                turned = full[index, 1 - part, field] * frequency
                result = turned if part else -turned
                if field in sound:
                    result = result + sound[field]
                own[index, part, field] = result - damping

    for field in range(fields):
        for slot in range(len(peers)):
            back_copy(field, slot).wait_recv()
    for slot in range(len(peers)):
        base_copy(slot).wait_send()
        for field in range(fields):
            field_copy(field, slot).wait_send()
            back_copy(field, slot).wait_send()
    for side in range(2):
        for slot in range(len(everyone) + 1):
            rim_copy(side, slot).wait_send()


def join_kernel(groups, own, back, out_hbm, out, sem):
    local, _, fields, rows, width = own.shape
    half, lanes = back.shape[-2:]
    left = lax.broadcasted_iota(jnp.int32, (half, lanes), 1) < lanes // 2
    copies = []
    for index in range(local):
        for part in range(2):
            for field in range(fields):
                pair = index * 2 + part
                for tile in range(width // lanes):
                    span = slice(tile * lanes, (tile + 1) * lanes)
                    first, second = back[field, 2 * tile, pair], back[field, 2 * tile + 1, pair]
                    top = jnp.where(left, first, pltpu.roll(second, lanes // 2, 1))
                    bottom = jnp.where(left, pltpu.roll(first, lanes // 2, 1), second)
                    out[index, part, field, 0:half, span] = (
                        own[index, part, field, 0:half, span] + top
                    )
                    out[index, part, field, half:rows, span] = (
                        own[index, part, field, half:rows, span] + bottom
                    )
            copy = pltpu.make_async_copy(
                out.at[index, part], out_hbm.at[index, part], sem.at[index, part]
            )
            copy.start()
            copies.append(copy)
    for copy in copies:
        copy.wait()


def quarters(perturbation, base_flow, viscosity):
    local, parts, fields, rows, width = perturbation.shape
    groups = lax.axis_size("harm")
    tiles = lax.axis_size("tile")
    kinds = base_flow.shape[2]
    half, lanes = rows // 2, 2 * (width // groups)
    pairs = 2 * local
    values = pairs * fields
    deep = values // 2
    dma = pltpu.SemaphoreType.DMA
    f32 = jnp.float32
    limit = 24 * 1024 * 1024
    whole = (local, parts, fields, rows, width)
    blocks = (fields, groups, pairs, half, lanes)
    inputs = [
        pltpu.with_memory_space_constraint(array, pltpu.HBM)
        for array in (perturbation, base_flow, viscosity)
    ]
    own, back = pl.pallas_call(
        functools.partial(quarter_kernel, groups, tiles),
        out_shape=(pltpu.VMEM(whole, f32), pltpu.VMEM(blocks, f32)),
        in_specs=[pl.BlockSpec(memory_space=pltpu.HBM)] * 3,
        out_specs=[pl.BlockSpec(memory_space=pltpu.VMEM)] * 2,
        scratch_shapes=[
            pltpu.VMEM(whole, f32),
            pltpu.VMEM((local, parts, kinds, rows, width), f32),
            pltpu.VMEM((rows, width), f32),
            pltpu.VMEM((2, 2, deep + 1, width), f32),
            pltpu.VMEM((2, 2, deep + 1, width), f32),
            pltpu.VMEM((2, groups, deep, lanes), f32),
            pltpu.VMEM((2, groups, deep, lanes), f32),
            pltpu.VMEM((groups, values, lanes), f32),
            pltpu.VMEM((groups, kinds * pairs + 1, half, lanes), f32),
            pltpu.VMEM((groups, kinds * pairs + 1, half, lanes), f32),
            pltpu.VMEM(blocks, f32),
            pltpu.VMEM(blocks, f32),
            pltpu.VMEM((groups * pairs, half, lanes), f32),
            pltpu.VMEM((groups * pairs, half, lanes), f32),
            pltpu.VMEM(blocks, f32),
            dma((3,)),
            dma((1 + 2 * fields, 3)),
            dma((1 + 2 * fields, 3)),
            dma((2, 5)),
            dma((2, 5)),
            pltpu.SemaphoreType.REGULAR,
            pltpu.SemaphoreType.REGULAR,
        ],
        compiler_params=pltpu.CompilerParams(
            collective_id=0, has_side_effects=True, vmem_limit_bytes=limit
        ),
    )(*inputs)
    own = pltpu.with_memory_space_constraint(own, pltpu.VMEM)
    back = pltpu.with_memory_space_constraint(back, pltpu.VMEM)
    return pl.pallas_call(
        functools.partial(join_kernel, groups),
        out_shape=jax.ShapeDtypeStruct(whole, f32),
        in_specs=[pl.BlockSpec(memory_space=pltpu.VMEM)] * 2,
        out_specs=pl.BlockSpec(memory_space=pl.ANY),
        scratch_shapes=[pltpu.VMEM(whole, f32), dma((local, parts))],
        compiler_params=pltpu.CompilerParams(vmem_limit_bytes=limit),
    )(own, back)


def solution(mesh):
    placed = (
        P("harm", None, None, ("parts", "tile"), None),
        P("harm", None, None, ("parts", "tile"), None),
        P(("parts", "tile"), None),
    )
    return jax.shard_map(
        shards,
        mesh=mesh,
        in_specs=placed,
        out_specs=P("harm", None, None, ("parts", "tile"), None),
        check_vma=False,
    )
```

```python
import functools

import jax
import jax.numpy as jnp
from jax import lax
from jax.experimental import pallas as pl
from jax.experimental.pallas import tpu as pltpu
from jax.sharding import PartitionSpec as P

omega_base = 0.25
MESH = pl.DeviceIdType.MESH


def kernel(
    groups,
    tiles,
    p_hbm,
    b_hbm,
    v_hbm,
    out,
    pbuf,
    bbuf,
    vbuf,
    stage,
    rims,
    gx,
    gy,
    local_sem,
    y_send,
    y_recv,
    chip_send,
    chip_recv,
    z_send,
    z_recv,
    rim_send,
    rim_recv,
):
    local, _, fields, rows, width = p_hbm.shape
    total = pbuf.shape[0]
    cores = 2
    chips = groups // cores
    rim_rows = local * 2 * fields
    me = lax.axis_index("harm")
    chip, core = me // cores, me % cores
    place = lax.axis_index("tile")
    partner = chip * cores + (1 - core)
    above, below = (place + 1) % tiles, (place + tiles - 1) % tiles

    def group_at(distance, own_core):
        at = (chip + chips - distance) % chips
        return at * cores + (core if own_core else 1 - core)

    def target_at(distance):
        return (chip + distance) % chips * cores + core

    first = me * local

    copy_p = pltpu.make_async_copy(p_hbm, pbuf.at[pl.ds(first, local)], local_sem.at[0])
    copy_b = pltpu.make_async_copy(b_hbm, bbuf.at[pl.ds(first, local)], local_sem.at[1])
    copy_v = pltpu.make_async_copy(v_hbm, vbuf, local_sem.at[2])
    copy_p.start()
    copy_v.start()
    copy_b.start()

    barrier = pltpu.get_barrier_semaphore()
    for distance in range(1, chips):
        pl.semaphore_signal(
            barrier, inc=1, device_id={"harm": target_at(distance)}, device_id_type=MESH
        )
    pl.semaphore_signal(barrier, inc=1, device_id={"harm": partner}, device_id_type=MESH)
    pl.semaphore_signal(barrier, inc=1, device_id={"tile": above}, device_id_type=MESH)
    pl.semaphore_signal(barrier, inc=1, device_id={"tile": below}, device_id_type=MESH)

    def pack(distance):
        start = group_at(distance, True) * local
        for index in range(local):
            for part in range(2):
                for field in range(fields):
                    row = (index * 2 + part) * fields + field
                    stage[distance, 0, row : row + 1, :] = pbuf[start + index, part, field, 0:1, :]
                    stage[distance, 1, row : row + 1, :] = pbuf[
                        start + index, part, field, rows - 1 : rows, :
                    ]

    copy_p.wait()
    copy_v.wait()
    pack(0)
    stage[0, 0, rim_rows : rim_rows + 1, :] = vbuf[0:1, :]
    stage[0, 1, rim_rows : rim_rows + 1, :] = vbuf[rows - 1 : rows, :]

    pl.semaphore_wait(barrier, chips + 2)

    y_copies = []
    for kind in range(2):
        source, dest = ((p_hbm, pbuf), (b_hbm, bbuf))[kind]
        for index in range(local):
            for distance in range(1, chips):
                copy = pltpu.make_async_remote_copy(
                    src_ref=source.at[index],
                    dst_ref=dest.at[first + index],
                    send_sem=y_send.at[distance - 1, kind, index],
                    recv_sem=y_recv.at[distance - 1, kind, index],
                    device_id={"harm": target_at(distance)},
                    device_id_type=MESH,
                )
                copy.start()
                y_copies.append((distance, kind, index, copy))

    def rim_copies(distance):
        group = group_at(distance, True)
        return [
            pltpu.make_async_remote_copy(
                src_ref=stage.at[distance, side],
                dst_ref=rims.at[group, 1 - side],
                send_sem=z_send.at[distance, side],
                recv_sem=z_recv.at[distance, side],
                device_id={"tile": (below, above)[side]},
                device_id_type=MESH,
            )
            for side in range(2)
        ]

    started = []
    rim_pending = {}

    def send_rims(distance):
        rim_pending[distance] = rim_copies(distance)
        for copy in rim_pending[distance]:
            copy.start()

    def relay_copy(distance, kind, index):
        at = group_at(distance, True) * local + index
        dest = (pbuf, bbuf)[kind]
        source = dest.at[at] if distance else (p_hbm, b_hbm)[kind].at[index]
        return pltpu.make_async_remote_copy(
            src_ref=source,
            dst_ref=dest.at[at],
            send_sem=chip_send.at[distance, kind, index],
            recv_sem=chip_recv.at[distance, kind, index],
            device_id={"harm": partner},
            device_id_type=MESH,
        )

    relays = {}

    def relay(distance, kind, index):
        relays[distance, kind, index] = relay_copy(distance, kind, index)
        relays[distance, kind, index].start()

    def relay_rims(distance):
        group = group_at(distance, True)
        relays[distance] = pltpu.make_async_remote_copy(
            src_ref=rims.at[group],
            dst_ref=rims.at[group],
            send_sem=rim_send.at[distance],
            recv_sem=rim_recv.at[distance],
            device_id={"harm": partner},
            device_id_type=MESH,
        )
        relays[distance].start()

    send_rims(0)
    for kind in range(2):
        for index in range(local):
            relay(0, kind, index)

    row_at = lax.broadcasted_iota(jnp.int32, (rows, width), 0)

    def neighbours(value, low, high):
        east = jnp.where(row_at == rows - 1, high, pltpu.roll(value, rows - 1, 0))
        west = jnp.where(row_at == 0, low, pltpu.roll(value, 1, 0))
        return east, west

    def slope_y(group):
        def one(index, _):
            at = group * local + index
            for part in range(2):
                for field in range(fields):
                    value = pbuf[at, part, field]
                    gy[at, part, field] = 0.5 * (
                        pltpu.roll(value, width - 1, 1) - pltpu.roll(value, 1, 1)
                    )
            return 0

        lax.fori_loop(0, local, one, 0)

    def slope_x(group):
        for index in range(local):
            at = group * local + index
            for part in range(2):
                for field in range(fields):
                    row = (index * 2 + part) * fields + field
                    east, west = neighbours(
                        pbuf[at, part, field],
                        rims[group, 0, row : row + 1, :],
                        rims[group, 1, row : row + 1, :],
                    )
                    gx[at, part, field] = 0.5 * (east - west)

    def own_terms():
        center = vbuf[...]
        east, west = neighbours(
            center,
            rims[me, 0, rim_rows : rim_rows + 1, :],
            rims[me, 1, rim_rows : rim_rows + 1, :],
        )
        east_face = 0.5 * (center + east)
        west_face = 0.5 * (center + west)
        north_face = 0.5 * (center + pltpu.roll(center, width - 1, 1))
        south_face = 0.5 * (center + pltpu.roll(center, 1, 1))
        for index in range(local):
            at = first + index
            signed = jnp.where(at < total // 2, at, at - total)
            frequency = omega_base * signed.astype(jnp.float32)
            for part in range(2):
                for field in range(fields):
                    row = (index * 2 + part) * fields + field
                    value = pbuf[at, part, field]
                    up, down = neighbours(
                        value,
                        rims[me, 0, row : row + 1, :],
                        rims[me, 1, row : row + 1, :],
                    )
                    damping = (
                        east_face * (up - value)
                        - west_face * (value - down)
                        + north_face * (pltpu.roll(value, width - 1, 1) - value)
                        - south_face * (value - pltpu.roll(value, 1, 1))
                    )
                    turned = pbuf[at, 1 - part, field] * frequency
                    result = turned - damping if part else -turned - damping
                    if field == 0 or field == 4:
                        result = result + (gx[at, part, 1] + gy[at, part, 2])
                    elif field == 1:
                        result = result + gx[at, part, 4]
                    elif field == 2:
                        result = result + gy[at, part, 4]
                    out[index, part, field] = result

    def couple(at):
        def strip(step, _):
            span = pl.ds(pl.multiple_of(step * 8, 8), 8)
            base = [[bbuf[at, part, which, span, :] for part in range(2)] for which in range(3)]
            for index in range(local):
                source = (first + index + total - at) % total
                for field in range(fields):
                    real = out[index, 0, field, span, :]
                    imag = out[index, 1, field, span, :]
                    for which, values in ((0, gx), (1, gy), (2, pbuf)):
                        a_real, a_imag = base[which]
                        q_real = values[source, 0, field, span, :]
                        q_imag = values[source, 1, field, span, :]
                        real = real + a_real * q_real - a_imag * q_imag
                        imag = imag + a_real * q_imag + a_imag * q_real
                    out[index, 0, field, span, :] = real
                    out[index, 1, field, span, :] = imag
            return 0

        lax.fori_loop(0, rows // 8, strip, 0)

    def wait_y(distance, kind, index):
        for other, what, which, copy in y_copies:
            if (other, what, which) == (distance, kind, index):
                copy.wait_recv()

    slope_y(me)
    for copy in rim_pending[0]:
        copy.wait_recv()
    relay_rims(0)
    slope_x(me)
    own_terms()
    for index in range(local):
        relays[0, 0, index].wait_recv()
    slope_y(partner)
    relays[0].wait_recv()
    slope_x(partner)

    for distance in range(1, chips):
        for index in range(local):
            wait_y(distance, 0, index)
            relay(distance, 0, index)
        pack(distance)
        send_rims(distance)
    for distance in range(1, chips):
        slope_y(group_at(distance, True))
        for index in range(local):
            relays[distance, 0, index].wait_recv()
        slope_y(group_at(distance, False))
    for distance in range(1, chips):
        for index in range(local - 1):
            wait_y(distance, 1, index)
            relay(distance, 1, index)
    for distance in range(1, chips):
        for copy in rim_pending[distance]:
            copy.wait_recv()
        relay_rims(distance)
        slope_x(group_at(distance, True))
    for distance in range(1, chips):
        relays[distance].wait_recv()
        slope_x(group_at(distance, False))

    copy_b.wait()
    for index in range(local):
        couple(first + index)
    for index in range(local):
        relays[0, 1, index].wait_recv()
        couple(partner * local + index)
    for distance in range(1, chips):
        wait_y(distance, 1, local - 1)
        relay(distance, 1, local - 1)
    for distance in range(1, chips):
        for index in range(local):
            couple(group_at(distance, True) * local + index)
    for distance in range(1, chips):
        for index in range(local):
            relays[distance, 1, index].wait_recv()
            couple(group_at(distance, False) * local + index)

    for _, _, _, copy in y_copies:
        copy.wait_send()
    for copies in rim_pending.values():
        for copy in copies:
            copy.wait_send()
    for copy in relays.values():
        copy.wait_send()


def shards(perturbation, base_flow, viscosity):
    local, parts, fields, rows, width = perturbation.shape
    groups = lax.axis_size("harm")
    tiles = lax.axis_size("tile")
    chips = groups // 2
    cols = width // groups
    if (
        chips == 2
        and tiles > 2
        and rows == 16
        and 2 * cols == 128
        and 2 * local * parts * fields <= cols
    ):
        return quarters(perturbation, base_flow, viscosity)
    total = local * groups
    rim = -(-(local * parts * fields + 1) // 8) * 8
    kinds = base_flow.shape[2]
    dma = pltpu.SemaphoreType.DMA
    f32 = jnp.float32
    return pl.pallas_call(
        functools.partial(kernel, groups, tiles),
        out_shape=jax.ShapeDtypeStruct(perturbation.shape, f32),
        in_specs=[pl.BlockSpec(memory_space=pl.ANY)] * 3,
        out_specs=pl.BlockSpec(memory_space=pltpu.VMEM),
        scratch_shapes=[
            pltpu.VMEM((total, 2, fields, rows, width), f32),
            pltpu.VMEM((total, 2, kinds, rows, width), f32),
            pltpu.VMEM((rows, width), f32),
            pltpu.VMEM((chips, 2, rim, width), f32),
            pltpu.VMEM((groups, 2, rim, width), f32),
            pltpu.VMEM((total, 2, fields, rows, width), f32),
            pltpu.VMEM((total, 2, fields, rows, width), f32),
            dma((3,)),
            dma((chips - 1, 2, local)),
            dma((chips - 1, 2, local)),
            dma((chips, 2, local)),
            dma((chips, 2, local)),
            dma((chips, 2)),
            dma((chips, 2)),
            dma((chips,)),
            dma((chips,)),
        ],
        compiler_params=pltpu.CompilerParams(collective_id=0, has_side_effects=True),
    )(perturbation, base_flow, viscosity)


def quarter_kernel(
    groups,
    tiles,
    p_hbm,
    b_hbm,
    v_hbm,
    own,
    back,
    full,
    base,
    vbuf,
    stage,
    zrims,
    rim_out,
    rim_in,
    rim_rows,
    late_in,
    fix_out,
    fix_in,
    b_out,
    b_in,
    h_out,
    h_in,
    p_out,
    p_in,
    gx,
    gy,
    sent,
    load_sem,
    g_send,
    g_recv,
    z_send,
    z_recv,
    ready_up,
    ready_down,
):
    local, _, fields, rows, width = p_hbm.shape
    kinds = b_hbm.shape[2]
    harmonics = local * groups
    half = rows // 2
    cols = width // groups
    lanes = 2 * cols
    pairs = 2 * local
    values = pairs * fields
    deep = values // 2
    me = lax.axis_index("harm")
    chip, core = me // 2, me % 2
    place = lax.axis_index("tile")
    partner = chip * 2 + (1 - core)
    across = (1 - chip) * 2 + core
    corner = (1 - chip) * 2 + (1 - core)
    peers = (across, corner, partner)
    everyone = (me, partner, across, corner)
    above, below = (place + 1) % tiles, (place + tiles - 1) % tiles
    inner, lowest, highest = place < tiles - 1, place == 0, place == tiles - 1

    loads = [
        pltpu.make_async_copy(source, dest, load_sem.at[at])
        for at, (source, dest) in enumerate(((b_hbm, base), (p_hbm, full), (v_hbm, vbuf)))
    ]
    for copy in loads:
        copy.start()

    def tell(semaphore, where):
        for group in everyone:
            pl.semaphore_signal(
                semaphore, inc=1, device_id={"harm": group, "tile": where}, device_id_type=MESH
            )

    barrier = pltpu.get_barrier_semaphore()
    for group in peers:
        pl.semaphore_signal(barrier, inc=1, device_id={"harm": group}, device_id_type=MESH)

    @pl.when(inner)
    def _():
        tell(barrier, above)

    @pl.when(lowest)
    def _():
        tell(barrier, below)

    lane = lax.broadcasted_iota(jnp.int32, (half, lanes), 1)
    sub = lax.broadcasted_iota(jnp.int32, (half, lanes), 0)
    left = lane < cols
    column = lane % cols

    def turn(value, shift):
        return pltpu.roll(value, shift % lanes, 1)

    def packed(ref, at):
        blocks = []
        for tile in range(width // lanes):
            span = slice(tile * lanes, (tile + 1) * lanes)
            top = ref[(*at, slice(0, half), span)]
            bottom = ref[(*at, slice(half, rows), span)]
            blocks.append(jnp.where(left, top, turn(bottom, cols)))
            blocks.append(jnp.where(left, turn(top, cols), bottom))
        return blocks

    loads[0].wait()
    for index in range(local):
        for part in range(2):
            for which in range(kinds):
                for group, block in enumerate(packed(base, (index, part, which))):
                    b_out[group, (index * 2 + part) * kinds + which] = block

    low_lane = lax.broadcasted_iota(jnp.int32, (deep, lanes), 1) < cols

    def prepare_rims():
        loads[1].wait()
        loads[2].wait()
        for field in range(fields):
            for index in range(local):
                for part in range(2):
                    at = index * fields + field
                    stage[0, part, at : at + 1, :] = full[index, part, field, 0:1, :]
                    stage[1, part, at : at + 1, :] = full[index, part, field, rows - 1 : rows, :]
        stage[0, 0, deep : deep + 1, :] = vbuf[0:1, :]
        stage[1, 0, deep : deep + 1, :] = vbuf[rows - 1 : rows, :]
        for side in range(2):
            for group in range(groups):
                tile, odd = group * cols // lanes, group * cols % lanes
                span = slice(tile * lanes, (tile + 1) * lanes)
                first = stage[side, 0, 0:deep, span]
                second = stage[side, 1, 0:deep, span]
                if side == 0:
                    first, second = second, first
                if odd:
                    first = turn(first, cols)
                else:
                    second = turn(second, cols)
                rim_out[side, group] = jnp.where(low_lane, first, second)

    def pack_fields():
        halos = [jnp.zeros((half, lanes), jnp.float32) for _ in range(groups)]
        for field in range(fields):
            for index in range(local):
                for part in range(2):
                    number = field * pairs + index * 2 + part
                    blocks = packed(full, (index, part, field))
                    for group, block in enumerate(blocks):
                        p_out[field, group, index * 2 + part] = block
                        low = turn(blocks[(group - 1) % groups], 2 * number + 2 - cols)
                        high = turn(blocks[(group + 1) % groups], 2 * number + cols)
                        halos[group] = jnp.where(
                            column == 2 * number + 1,
                            low,
                            jnp.where(column == 2 * number, high, halos[group]),
                        )
        for group in range(groups):
            h_out[group] = halos[group]

    def remote(source, dest, send, recv, at, device):
        return pltpu.make_async_remote_copy(
            src_ref=source,
            dst_ref=dest,
            send_sem=send.at[at],
            recv_sem=recv.at[at],
            device_id=device,
            device_id_type=MESH,
        )

    def base_copy(slot):
        return remote(
            b_out.at[peers[slot]], b_in.at[me], g_send, g_recv, (0, slot), {"harm": peers[slot]}
        )

    def halo_copy(slot):
        return remote(
            h_out.at[peers[slot]],
            h_in.at[me],
            g_send,
            g_recv,
            (1 + 2 * fields, slot),
            {"harm": peers[slot]},
        )

    def field_copy(field, slot):
        return remote(
            p_out.at[field, peers[slot]],
            p_in.at[field, me],
            g_send,
            g_recv,
            (1 + field, slot),
            {"harm": peers[slot]},
        )

    def back_copy(field, slot):
        return remote(
            sent.at[field, peers[slot]],
            back.at[field, me],
            g_send,
            g_recv,
            (1 + fields + field, slot),
            {"harm": peers[slot]},
        )

    def rim_copy(side, slot):
        where = (below, above)[side]
        if slot == len(everyone):
            return remote(
                stage.at[side],
                zrims.at[side],
                z_send,
                z_recv,
                (side, slot),
                {"harm": me, "tile": where},
            )
        return remote(
            rim_out.at[side, everyone[slot]],
            rim_in.at[side, me],
            z_send,
            z_recv,
            (side, slot),
            {"harm": everyone[slot], "tile": where},
        )

    def late_copy(side, slot):
        return remote(
            rim_out.at[side, everyone[slot]],
            late_in.at[me],
            z_send,
            z_recv,
            (2, slot),
            {"harm": everyone[slot], "tile": (below, above)[side]},
        )

    def fix_copy(slot):
        return remote(
            fix_out.at[peers[slot]],
            fix_in.at[me],
            g_send,
            g_recv,
            (2 + 2 * fields, slot),
            {"harm": peers[slot]},
        )

    def send_rims(side):
        for slot in range(len(everyone) + 1):
            rim_copy(side, slot).start()

    def send_late(side):
        for slot in range(len(everyone)):
            late_copy(side, slot).start()
        rim_copy(side, len(everyone)).start()

    pl.semaphore_wait(
        barrier,
        len(peers)
        + groups * (place > 0).astype(jnp.int32)
        + groups * highest.astype(jnp.int32),
    )

    @pl.when(place > 0)
    def _():
        tell(ready_up, below)
        prepare_rims()
        send_rims(0)

    @pl.when(highest)
    def _():
        tell(ready_down, above)
        send_late(1)

    for slot in range(len(peers)):
        base_copy(slot).start()

    @pl.when(lowest)
    def _():
        prepare_rims()

    pack_fields()
    for slot in range(len(peers)):
        halo_copy(slot).start()

    def send_field(field):
        for slot in range(len(peers)):
            field_copy(field, slot).start()

    early = min(3, fields)
    for field in range(early):
        send_field(field)

    @pl.when(inner)
    def _():
        pl.semaphore_wait(ready_up, groups)
        send_rims(1)

    @pl.when(lowest)
    def _():
        pl.semaphore_wait(ready_down, groups)
        send_late(0)

    for field in range(early, fields):
        send_field(field)

    b_in[me] = b_out[me]
    h_in[me] = h_out[me]
    for field in range(fields):
        p_in[field, me] = p_out[field, me]

    def take_rims(slot):
        group = everyone[slot]

        @pl.when(inner)
        def _():
            rim_copy(0, slot).wait_recv()

        @pl.when(highest)
        def _():
            rim_in[0, group] = jnp.zeros((deep, lanes), jnp.float32)

        @pl.when(place > 0)
        def _():
            rim_copy(1, slot).wait_recv()

        @pl.when(lowest)
        def _():
            rim_in[1, group] = jnp.zeros((deep, lanes), jnp.float32)

        above_rows, below_rows = rim_in[0, group], rim_in[1, group]
        rim_rows[group, 0] = jnp.where(low_lane, below_rows, above_rows)
        rim_rows[group, 1] = turn(jnp.where(low_lane, above_rows, below_rows), cols)

    for slot in range(len(peers)):
        base_copy(slot).wait_recv()
        halo_copy(slot).wait_recv()
    for slot in range(len(everyone)):
        take_rims(slot)

    def slopes(field, group):
        for pair in range(pairs):
            number = field * pairs + pair
            value = p_in[field, group, pair]
            edge = pltpu.roll(h_in[group], lanes - 1 - 2 * number, 1)
            north = jnp.where(column == cols - 1, edge, turn(value, -1))
            south = jnp.where(column == 0, edge, turn(value, 1))
            gy[group, pair] = 0.5 * (north - south)
            swapped = turn(value, cols)
            rim = rim_rows[group, pair % 2, pl.ds(pair // 2 * fields + field, 1), :]
            high = jnp.where(left, swapped, rim)
            low = jnp.where(left, rim, swapped)
            east = pltpu.roll(jnp.where(sub == 0, high, value), half - 1, 0)
            west = pltpu.roll(jnp.where(sub == half - 1, low, value), 1, 0)
            gx[group, pair] = 0.5 * (east - west)

    def convolve(field, target, index, sources, sums):
        real, imag = sums
        for group in sources:
            for at in range(local):
                shift = (target - group) * local + index - at
                shift = (shift + harmonics) % harmonics
                owner, first = shift // local, shift % local * 2 * kinds
                for which, values_of in enumerate((gx, gy, p_in.at[field])):
                    a_real = b_in[owner, first + which]
                    a_imag = b_in[owner, first + kinds + which]
                    q_real, q_imag = values_of[group, 2 * at], values_of[group, 2 * at + 1]
                    real = real + a_real * q_real - a_imag * q_imag
                    imag = imag + a_real * q_imag + a_imag * q_real
        return real, imag

    order = (*peers, me)

    at_end = lowest | highest

    def fix():
        for slot in range(len(everyone)):
            late_copy(0, slot).wait_recv()
        edge = (1 - lowest.astype(jnp.int32)) * (half - 1)
        scale = jnp.where(lowest, -0.5, 0.5)
        low_row = lax.broadcasted_iota(jnp.int32, (1, lanes), 1) < cols
        here = low_row == lowest

        def both(row):
            return scale * jnp.where(here, row, turn(row, cols))

        def straight(rows_here):
            return jnp.where(lowest, rows_here, turn(rows_here, cols))

        late = [straight(late_in[group]) for group in everyone]
        crossed = [turn(rows_here, cols) for rows_here in late]
        for target in everyone:
            for index in range(local):
                total = jnp.zeros((fields, lanes), jnp.float32)
                for number, group in enumerate(everyone):
                    for at in range(local):
                        shift = (target - group) * local + index - at
                        shift = (shift + harmonics) % harmonics
                        owner, first = shift // local, shift % local * 2 * kinds
                        real = both(b_in[owner, first, pl.ds(edge, 1), :])
                        imag = both(b_in[owner, first + kinds, pl.ds(edge, 1), :])
                        span = slice(at * fields, (at + 1) * fields)
                        total = total + real * late[number][span]
                        total = total + jnp.where(low_row, -imag, imag) * crossed[number][span]
                fix_out[target, index * fields : (index + 1) * fields, :] = total
        fix_in[me] = fix_out[me]
        for slot in range(len(peers)):
            fix_copy(slot).start()

    def one_field(field, _):
        @pl.when(at_end & (field == min(3, fields - 1)))
        def _():
            fix()

        field_copy(field, 2).wait_recv()
        slopes(field, me)
        slopes(field, partner)
        zero = jnp.zeros((half, lanes), jnp.float32)
        sums = [
            [convolve(field, target, index, (me, partner), (zero, zero)) for index in range(local)]
            for target in order
        ]
        field_copy(field, 0).wait_recv()
        slopes(field, across)
        field_copy(field, 1).wait_recv()
        slopes(field, corner)
        for slot, target in enumerate(order):
            for index in range(local):
                real, imag = convolve(field, target, index, (across, corner), sums[slot][index])
                if slot < len(peers):
                    sent[field, target, 2 * index] = real
                    sent[field, target, 2 * index + 1] = imag
                else:
                    back[field, me, 2 * index] = real
                    back[field, me, 2 * index + 1] = imag
            if slot < len(peers):
                back_copy(field, slot).start()
        return 0

    lax.fori_loop(0, fields, one_field, 0)

    for side in range(2):
        rim_copy(side, len(everyone)).wait_recv()

    row_at = lax.broadcasted_iota(jnp.int32, (rows, width), 0)

    def neighbours(value, number, at):
        high, low = zrims[0, number, at : at + 1, :], zrims[1, number, at : at + 1, :]
        east = jnp.where(row_at == rows - 1, high, pltpu.roll(value, rows - 1, 0))
        west = jnp.where(row_at == 0, low, pltpu.roll(value, 1, 0))
        return east, west

    def north_of(value):
        return pltpu.roll(value, width - 1, 1)

    def south_of(value):
        return pltpu.roll(value, 1, 1)

    center = vbuf[...]
    east, west = neighbours(center, 0, deep)
    east_face = 0.5 * (center + east)
    west_face = 0.5 * (center + west)
    north_face = 0.5 * (center + north_of(center))
    south_face = 0.5 * (center + south_of(center))
    for index in range(local):
        at = me * local + index
        signed = jnp.where(at < harmonics // 2, at, at - harmonics)
        frequency = omega_base * signed.astype(jnp.float32)
        for part in range(2):

            def sides(field):
                return neighbours(full[index, part, field], part, index * fields + field)

            def along_x(field):
                up, down = sides(field)
                return 0.5 * (up - down)

            def along_y(field):
                value = full[index, part, field]
                return 0.5 * (north_of(value) - south_of(value))

            dilation = along_x(1) + along_y(2)
            sound = {0: dilation, 4: dilation, 1: along_x(4), 2: along_y(4)}
            for field in range(fields):
                value = full[index, part, field]
                up, down = sides(field)
                damping = (
                    east_face * (up - value)
                    - west_face * (value - down)
                    + north_face * (north_of(value) - value)
                    - south_face * (value - south_of(value))
                )
                turned = full[index, 1 - part, field] * frequency
                result = turned if part else -turned
                if field in sound:
                    result = result + sound[field]
                own[index, part, field] = result - damping

    def add_fixes(edge):
        for slot in range(len(peers)):
            fix_copy(slot).wait_recv()
        for tile in range(width // lanes):
            span = slice(tile * lanes, (tile + 1) * lanes)
            first, second = fix_in[2 * tile], fix_in[2 * tile + 1]
            both = (
                jnp.where(low_lane, first, turn(second, cols)),
                jnp.where(low_lane, turn(first, cols), second),
            )
            for index in range(local):
                for part in range(2):
                    for field in range(fields):
                        at = index * fields + field
                        own[index, part, field, edge : edge + 1, span] += both[part][at : at + 1]

    for field in range(fields):
        if field == fields - 1:
            pl.when(lowest)(lambda: add_fixes(0))
            pl.when(highest)(lambda: add_fixes(rows - 1))
        for slot in range(len(peers)):
            back_copy(field, slot).wait_recv()
        if field < fields - 1:
            join(field, own, back, own, field)

    for slot in range(len(peers)):
        base_copy(slot).wait_send()
        halo_copy(slot).wait_send()
        for field in range(fields):
            field_copy(field, slot).wait_send()
            back_copy(field, slot).wait_send()
    def sent_rims(side):
        for slot in range(len(everyone)):
            rim_copy(side, slot).wait_send()

    pl.when(inner)(lambda: sent_rims(1))
    pl.when(place > 0)(lambda: sent_rims(0))

    @pl.when(at_end)
    def _():
        for slot in range(len(everyone)):
            late_copy(0, slot).wait_send()
        for slot in range(len(peers)):
            fix_copy(slot).wait_send()

    for side in range(2):
        rim_copy(side, len(everyone)).wait_send()


def join(field, own, back, out, at):
    local, _, _, rows, width = own.shape
    half, lanes = back.shape[-2:]
    left = lax.broadcasted_iota(jnp.int32, (half, lanes), 1) < lanes // 2
    for index in range(local):
        for part in range(2):
            pair = index * 2 + part
            for tile in range(width // lanes):
                span = slice(tile * lanes, (tile + 1) * lanes)
                first, second = back[field, 2 * tile, pair], back[field, 2 * tile + 1, pair]
                top = jnp.where(left, first, pltpu.roll(second, lanes // 2, 1))
                bottom = jnp.where(left, pltpu.roll(first, lanes // 2, 1), second)
                out[index, part, at, 0:half, span] = own[index, part, field, 0:half, span] + top
                out[index, part, at, half:rows, span] = (
                    own[index, part, field, half:rows, span] + bottom
                )


def join_kernel(own, back, out_hbm, out, sem):
    last = own.shape[2] - 1
    copies = [
        pltpu.make_async_copy(own.at[:, :, 0:last], out_hbm.at[:, :, 0:last], sem.at[0]),
        pltpu.make_async_copy(out, out_hbm.at[:, :, last : last + 1], sem.at[1]),
    ]
    copies[0].start()
    join(last, own, back, out, 0)
    copies[1].start()
    for copy in copies:
        copy.wait()


def quarters(perturbation, base_flow, viscosity):
    local, parts, fields, rows, width = perturbation.shape
    groups = lax.axis_size("harm")
    tiles = lax.axis_size("tile")
    kinds = base_flow.shape[2]
    half, lanes = rows // 2, 2 * (width // groups)
    pairs = 2 * local
    values = pairs * fields
    deep = values // 2
    dma = pltpu.SemaphoreType.DMA
    f32 = jnp.float32
    limit = 24 * 1024 * 1024
    whole = (local, parts, fields, rows, width)
    blocks = (fields, groups, pairs, half, lanes)
    inputs = [
        pltpu.with_memory_space_constraint(array, pltpu.HBM)
        for array in (perturbation, base_flow, viscosity)
    ]
    own, back = pl.pallas_call(
        functools.partial(quarter_kernel, groups, tiles),
        out_shape=(pltpu.VMEM(whole, f32), pltpu.VMEM(blocks, f32)),
        in_specs=[pl.BlockSpec(memory_space=pltpu.HBM)] * 3,
        out_specs=[pl.BlockSpec(memory_space=pltpu.VMEM)] * 2,
        scratch_shapes=[
            pltpu.VMEM(whole, f32),
            pltpu.VMEM((local, parts, kinds, rows, width), f32),
            pltpu.VMEM((rows, width), f32),
            pltpu.VMEM((2, 2, deep + 1, width), f32),
            pltpu.VMEM((2, 2, deep + 1, width), f32),
            pltpu.VMEM((2, groups, deep, lanes), f32),
            pltpu.VMEM((2, groups, deep, lanes), f32),
            pltpu.VMEM((groups, 2, deep, lanes), f32),
            pltpu.VMEM((groups, deep, lanes), f32),
            pltpu.VMEM((groups, deep, lanes), f32),
            pltpu.VMEM((groups, deep, lanes), f32),
            pltpu.VMEM((groups, kinds * pairs, half, lanes), f32),
            pltpu.VMEM((groups, kinds * pairs, half, lanes), f32),
            pltpu.VMEM((groups, half, lanes), f32),
            pltpu.VMEM((groups, half, lanes), f32),
            pltpu.VMEM(blocks, f32),
            pltpu.VMEM(blocks, f32),
            pltpu.VMEM((groups, pairs, half, lanes), f32),
            pltpu.VMEM((groups, pairs, half, lanes), f32),
            pltpu.VMEM(blocks, f32),
            dma((3,)),
            dma((3 + 2 * fields, 3)),
            dma((3 + 2 * fields, 3)),
            dma((3, 5)),
            dma((3, 5)),
            pltpu.SemaphoreType.REGULAR,
            pltpu.SemaphoreType.REGULAR,
        ],
        compiler_params=pltpu.CompilerParams(
            collective_id=0, has_side_effects=True, vmem_limit_bytes=limit
        ),
    )(*inputs)
    own = pltpu.with_memory_space_constraint(own, pltpu.VMEM)
    back = pltpu.with_memory_space_constraint(back, pltpu.VMEM)
    return pl.pallas_call(
        join_kernel,
        out_shape=jax.ShapeDtypeStruct(whole, f32),
        in_specs=[pl.BlockSpec(memory_space=pltpu.VMEM)] * 2,
        out_specs=pl.BlockSpec(memory_space=pl.ANY),
        scratch_shapes=[pltpu.VMEM((local, parts, 1, rows, width), f32), dma((2,))],
        compiler_params=pltpu.CompilerParams(vmem_limit_bytes=limit),
    )(own, back)


def solution(mesh):
    placed = (
        P("harm", None, None, ("parts", "tile"), None),
        P("harm", None, None, ("parts", "tile"), None),
        P(("parts", "tile"), None),
    )
    return jax.shard_map(
        shards,
        mesh=mesh,
        in_specs=placed,
        out_specs=P("harm", None, None, ("parts", "tile"), None),
        check_vma=False,
    )
```

```python
import functools

import jax
import jax.numpy as jnp
from jax import lax
from jax.experimental import pallas as pl
from jax.experimental.pallas import tpu as pltpu
from jax.sharding import PartitionSpec as P

omega_base = 0.25
MESH = pl.DeviceIdType.MESH


def kernel(
    groups,
    tiles,
    p_hbm,
    b_hbm,
    v_hbm,
    out,
    pbuf,
    bbuf,
    vbuf,
    stage,
    rims,
    gx,
    gy,
    local_sem,
    y_send,
    y_recv,
    chip_send,
    chip_recv,
    z_send,
    z_recv,
    rim_send,
    rim_recv,
):
    local, _, fields, rows, width = p_hbm.shape
    total = pbuf.shape[0]
    cores = 2
    chips = groups // cores
    rim_rows = local * 2 * fields
    me = lax.axis_index("harm")
    chip, core = me // cores, me % cores
    place = lax.axis_index("tile")
    partner = chip * cores + (1 - core)
    above, below = (place + 1) % tiles, (place + tiles - 1) % tiles

    def group_at(distance, own_core):
        at = (chip + chips - distance) % chips
        return at * cores + (core if own_core else 1 - core)

    def target_at(distance):
        return (chip + distance) % chips * cores + core

    first = me * local

    copy_p = pltpu.make_async_copy(p_hbm, pbuf.at[pl.ds(first, local)], local_sem.at[0])
    copy_b = pltpu.make_async_copy(b_hbm, bbuf.at[pl.ds(first, local)], local_sem.at[1])
    copy_v = pltpu.make_async_copy(v_hbm, vbuf, local_sem.at[2])
    copy_p.start()
    copy_v.start()
    copy_b.start()

    barrier = pltpu.get_barrier_semaphore()
    for distance in range(1, chips):
        pl.semaphore_signal(
            barrier, inc=1, device_id={"harm": target_at(distance)}, device_id_type=MESH
        )
    pl.semaphore_signal(barrier, inc=1, device_id={"harm": partner}, device_id_type=MESH)
    pl.semaphore_signal(barrier, inc=1, device_id={"tile": above}, device_id_type=MESH)
    pl.semaphore_signal(barrier, inc=1, device_id={"tile": below}, device_id_type=MESH)

    def pack(distance):
        start = group_at(distance, True) * local
        for index in range(local):
            for part in range(2):
                for field in range(fields):
                    row = (index * 2 + part) * fields + field
                    stage[distance, 0, row : row + 1, :] = pbuf[start + index, part, field, 0:1, :]
                    stage[distance, 1, row : row + 1, :] = pbuf[
                        start + index, part, field, rows - 1 : rows, :
                    ]

    copy_p.wait()
    copy_v.wait()
    pack(0)
    stage[0, 0, rim_rows : rim_rows + 1, :] = vbuf[0:1, :]
    stage[0, 1, rim_rows : rim_rows + 1, :] = vbuf[rows - 1 : rows, :]

    pl.semaphore_wait(barrier, chips + 2)

    y_copies = []
    for kind in range(2):
        source, dest = ((p_hbm, pbuf), (b_hbm, bbuf))[kind]
        for index in range(local):
            for distance in range(1, chips):
                copy = pltpu.make_async_remote_copy(
                    src_ref=source.at[index],
                    dst_ref=dest.at[first + index],
                    send_sem=y_send.at[distance - 1, kind, index],
                    recv_sem=y_recv.at[distance - 1, kind, index],
                    device_id={"harm": target_at(distance)},
                    device_id_type=MESH,
                )
                copy.start()
                y_copies.append((distance, kind, index, copy))

    def rim_copies(distance):
        group = group_at(distance, True)
        return [
            pltpu.make_async_remote_copy(
                src_ref=stage.at[distance, side],
                dst_ref=rims.at[group, 1 - side],
                send_sem=z_send.at[distance, side],
                recv_sem=z_recv.at[distance, side],
                device_id={"tile": (below, above)[side]},
                device_id_type=MESH,
            )
            for side in range(2)
        ]

    started = []
    rim_pending = {}

    def send_rims(distance):
        rim_pending[distance] = rim_copies(distance)
        for copy in rim_pending[distance]:
            copy.start()

    def relay_copy(distance, kind, index):
        at = group_at(distance, True) * local + index
        dest = (pbuf, bbuf)[kind]
        source = dest.at[at] if distance else (p_hbm, b_hbm)[kind].at[index]
        return pltpu.make_async_remote_copy(
            src_ref=source,
            dst_ref=dest.at[at],
            send_sem=chip_send.at[distance, kind, index],
            recv_sem=chip_recv.at[distance, kind, index],
            device_id={"harm": partner},
            device_id_type=MESH,
        )

    relays = {}

    def relay(distance, kind, index):
        relays[distance, kind, index] = relay_copy(distance, kind, index)
        relays[distance, kind, index].start()

    def relay_rims(distance):
        group = group_at(distance, True)
        relays[distance] = pltpu.make_async_remote_copy(
            src_ref=rims.at[group],
            dst_ref=rims.at[group],
            send_sem=rim_send.at[distance],
            recv_sem=rim_recv.at[distance],
            device_id={"harm": partner},
            device_id_type=MESH,
        )
        relays[distance].start()

    send_rims(0)
    for kind in range(2):
        for index in range(local):
            relay(0, kind, index)

    row_at = lax.broadcasted_iota(jnp.int32, (rows, width), 0)

    def neighbours(value, low, high):
        east = jnp.where(row_at == rows - 1, high, pltpu.roll(value, rows - 1, 0))
        west = jnp.where(row_at == 0, low, pltpu.roll(value, 1, 0))
        return east, west

    def slope_y(group):
        def one(index, _):
            at = group * local + index
            for part in range(2):
                for field in range(fields):
                    value = pbuf[at, part, field]
                    gy[at, part, field] = 0.5 * (
                        pltpu.roll(value, width - 1, 1) - pltpu.roll(value, 1, 1)
                    )
            return 0

        lax.fori_loop(0, local, one, 0)

    def slope_x(group):
        for index in range(local):
            at = group * local + index
            for part in range(2):
                for field in range(fields):
                    row = (index * 2 + part) * fields + field
                    east, west = neighbours(
                        pbuf[at, part, field],
                        rims[group, 0, row : row + 1, :],
                        rims[group, 1, row : row + 1, :],
                    )
                    gx[at, part, field] = 0.5 * (east - west)

    def own_terms():
        center = vbuf[...]
        east, west = neighbours(
            center,
            rims[me, 0, rim_rows : rim_rows + 1, :],
            rims[me, 1, rim_rows : rim_rows + 1, :],
        )
        east_face = 0.5 * (center + east)
        west_face = 0.5 * (center + west)
        north_face = 0.5 * (center + pltpu.roll(center, width - 1, 1))
        south_face = 0.5 * (center + pltpu.roll(center, 1, 1))
        for index in range(local):
            at = first + index
            signed = jnp.where(at < total // 2, at, at - total)
            frequency = omega_base * signed.astype(jnp.float32)
            for part in range(2):
                for field in range(fields):
                    row = (index * 2 + part) * fields + field
                    value = pbuf[at, part, field]
                    up, down = neighbours(
                        value,
                        rims[me, 0, row : row + 1, :],
                        rims[me, 1, row : row + 1, :],
                    )
                    damping = (
                        east_face * (up - value)
                        - west_face * (value - down)
                        + north_face * (pltpu.roll(value, width - 1, 1) - value)
                        - south_face * (value - pltpu.roll(value, 1, 1))
                    )
                    turned = pbuf[at, 1 - part, field] * frequency
                    result = turned - damping if part else -turned - damping
                    if field == 0 or field == 4:
                        result = result + (gx[at, part, 1] + gy[at, part, 2])
                    elif field == 1:
                        result = result + gx[at, part, 4]
                    elif field == 2:
                        result = result + gy[at, part, 4]
                    out[index, part, field] = result

    def couple(at):
        def strip(step, _):
            span = pl.ds(pl.multiple_of(step * 8, 8), 8)
            base = [[bbuf[at, part, which, span, :] for part in range(2)] for which in range(3)]
            for index in range(local):
                source = (first + index + total - at) % total
                for field in range(fields):
                    real = out[index, 0, field, span, :]
                    imag = out[index, 1, field, span, :]
                    for which, values in ((0, gx), (1, gy), (2, pbuf)):
                        a_real, a_imag = base[which]
                        q_real = values[source, 0, field, span, :]
                        q_imag = values[source, 1, field, span, :]
                        real = real + a_real * q_real - a_imag * q_imag
                        imag = imag + a_real * q_imag + a_imag * q_real
                    out[index, 0, field, span, :] = real
                    out[index, 1, field, span, :] = imag
            return 0

        lax.fori_loop(0, rows // 8, strip, 0)

    def wait_y(distance, kind, index):
        for other, what, which, copy in y_copies:
            if (other, what, which) == (distance, kind, index):
                copy.wait_recv()

    slope_y(me)
    for copy in rim_pending[0]:
        copy.wait_recv()
    relay_rims(0)
    slope_x(me)
    own_terms()
    for index in range(local):
        relays[0, 0, index].wait_recv()
    slope_y(partner)
    relays[0].wait_recv()
    slope_x(partner)

    for distance in range(1, chips):
        for index in range(local):
            wait_y(distance, 0, index)
            relay(distance, 0, index)
        pack(distance)
        send_rims(distance)
    for distance in range(1, chips):
        slope_y(group_at(distance, True))
        for index in range(local):
            relays[distance, 0, index].wait_recv()
        slope_y(group_at(distance, False))
    for distance in range(1, chips):
        for index in range(local - 1):
            wait_y(distance, 1, index)
            relay(distance, 1, index)
    for distance in range(1, chips):
        for copy in rim_pending[distance]:
            copy.wait_recv()
        relay_rims(distance)
        slope_x(group_at(distance, True))
    for distance in range(1, chips):
        relays[distance].wait_recv()
        slope_x(group_at(distance, False))

    copy_b.wait()
    for index in range(local):
        couple(first + index)
    for index in range(local):
        relays[0, 1, index].wait_recv()
        couple(partner * local + index)
    for distance in range(1, chips):
        wait_y(distance, 1, local - 1)
        relay(distance, 1, local - 1)
    for distance in range(1, chips):
        for index in range(local):
            couple(group_at(distance, True) * local + index)
    for distance in range(1, chips):
        for index in range(local):
            relays[distance, 1, index].wait_recv()
            couple(group_at(distance, False) * local + index)

    for _, _, _, copy in y_copies:
        copy.wait_send()
    for copies in rim_pending.values():
        for copy in copies:
            copy.wait_send()
    for copy in relays.values():
        copy.wait_send()


def shards(perturbation, base_flow, viscosity):
    local, parts, fields, rows, width = perturbation.shape
    groups = lax.axis_size("harm")
    tiles = lax.axis_size("tile")
    chips = groups // 2
    cols = width // groups
    if (
        chips == 2
        and tiles > 2
        and rows == 16
        and 2 * cols == 128
        and 2 * local * parts * fields <= cols
    ):
        return quarters(perturbation, base_flow, viscosity)
    total = local * groups
    rim = -(-(local * parts * fields + 1) // 8) * 8
    kinds = base_flow.shape[2]
    dma = pltpu.SemaphoreType.DMA
    f32 = jnp.float32
    return pl.pallas_call(
        functools.partial(kernel, groups, tiles),
        out_shape=jax.ShapeDtypeStruct(perturbation.shape, f32),
        in_specs=[pl.BlockSpec(memory_space=pl.ANY)] * 3,
        out_specs=pl.BlockSpec(memory_space=pltpu.VMEM),
        scratch_shapes=[
            pltpu.VMEM((total, 2, fields, rows, width), f32),
            pltpu.VMEM((total, 2, kinds, rows, width), f32),
            pltpu.VMEM((rows, width), f32),
            pltpu.VMEM((chips, 2, rim, width), f32),
            pltpu.VMEM((groups, 2, rim, width), f32),
            pltpu.VMEM((total, 2, fields, rows, width), f32),
            pltpu.VMEM((total, 2, fields, rows, width), f32),
            dma((3,)),
            dma((chips - 1, 2, local)),
            dma((chips - 1, 2, local)),
            dma((chips, 2, local)),
            dma((chips, 2, local)),
            dma((chips, 2)),
            dma((chips, 2)),
            dma((chips,)),
            dma((chips,)),
        ],
        compiler_params=pltpu.CompilerParams(collective_id=0, has_side_effects=True),
    )(perturbation, base_flow, viscosity)


def quarter_kernel(
    groups,
    tiles,
    p_hbm,
    b_hbm,
    v_hbm,
    own,
    back,
    full,
    base,
    vbuf,
    stage,
    zrims,
    rim_out,
    rim_in,
    rim_rows,
    late_in,
    fix_out,
    fix_in,
    b_out,
    b_in,
    h_out,
    h_in,
    p_out,
    p_in,
    gx,
    gy,
    sent,
    load_sem,
    g_send,
    g_recv,
    z_send,
    z_recv,
    ready_up,
    ready_down,
):
    local, _, fields, rows, width = p_hbm.shape
    kinds = b_hbm.shape[2]
    harmonics = local * groups
    half = rows // 2
    cols = width // groups
    lanes = 2 * cols
    pairs = 2 * local
    values = pairs * fields
    deep = values // 2
    me = lax.axis_index("harm")
    chip, core = me // 2, me % 2
    place = lax.axis_index("tile")
    partner = chip * 2 + (1 - core)
    far_first, far_second = (1 - chip) * 2, (1 - chip) * 2 + 1
    peers = (far_first, far_second, partner)
    relation = (core, 1 - core, 2)
    everyone = (me, partner, far_first, far_second)
    role = (0, 1, 2 + core, 3 - core)
    above, below = (place + 1) % tiles, (place + tiles - 1) % tiles
    inner, lowest, highest = place < tiles - 1, place == 0, place == tiles - 1

    def tell(semaphore, where):
        for group in everyone:
            pl.semaphore_signal(
                semaphore, inc=1, device_id={"harm": group, "tile": where}, device_id_type=MESH
            )

    barrier = pltpu.get_barrier_semaphore()
    for group in peers:
        pl.semaphore_signal(barrier, inc=1, device_id={"harm": group}, device_id_type=MESH)

    loads = [
        pltpu.make_async_copy(source, dest, load_sem.at[at])
        for at, (source, dest) in enumerate(((b_hbm, base), (p_hbm, full), (v_hbm, vbuf)))
    ]
    for copy in loads:
        copy.start()

    @pl.when(inner)
    def _():
        tell(barrier, above)

    @pl.when(lowest)
    def _():
        tell(barrier, below)

    lane = lax.broadcasted_iota(jnp.int32, (half, lanes), 1)
    sub = lax.broadcasted_iota(jnp.int32, (half, lanes), 0)
    left = lane < cols
    column = lane % cols

    def turn(value, shift):
        return pltpu.roll(value, shift % lanes, 1)

    def packed(ref, at):
        blocks = []
        for tile in range(width // lanes):
            span = slice(tile * lanes, (tile + 1) * lanes)
            top = ref[(*at, slice(0, half), span)]
            bottom = ref[(*at, slice(half, rows), span)]
            blocks.append(jnp.where(left, top, turn(bottom, cols)))
            blocks.append(jnp.where(left, turn(top, cols), bottom))
        return blocks

    loads[0].wait()
    for index in range(local):
        for part in range(2):
            for which in range(kinds):
                for group, block in enumerate(packed(base, (index, part, which))):
                    b_out[group, (index * 2 + part) * kinds + which] = block

    low_lane = lax.broadcasted_iota(jnp.int32, (deep, lanes), 1) < cols

    def prepare_rims():
        for field in range(fields):
            for index in range(local):
                for part in range(2):
                    at = index * fields + field
                    stage[0, part, at : at + 1, :] = full[index, part, field, 0:1, :]
                    stage[1, part, at : at + 1, :] = full[index, part, field, rows - 1 : rows, :]
        stage[0, 0, deep : deep + 1, :] = vbuf[0:1, :]
        stage[1, 0, deep : deep + 1, :] = vbuf[rows - 1 : rows, :]
        for side in range(2):
            for group in range(groups):
                tile, odd = group * cols // lanes, group * cols % lanes
                span = slice(tile * lanes, (tile + 1) * lanes)
                first = stage[side, 0, 0:deep, span]
                second = stage[side, 1, 0:deep, span]
                if side == 0:
                    first, second = second, first
                if odd:
                    first = turn(first, cols)
                else:
                    second = turn(second, cols)
                rim_out[side, group] = jnp.where(low_lane, first, second)

    def pack_fields():
        halos = [jnp.zeros((half, lanes), jnp.float32) for _ in range(groups)]
        for field in range(fields):
            for index in range(local):
                for part in range(2):
                    number = field * pairs + index * 2 + part
                    blocks = packed(full, (index, part, field))
                    for group, block in enumerate(blocks):
                        p_out[field, group, index * 2 + part] = block
                        low = turn(blocks[(group - 1) % groups], 2 * number + 2 - cols)
                        high = turn(blocks[(group + 1) % groups], 2 * number + cols)
                        halos[group] = jnp.where(
                            column == 2 * number + 1,
                            low,
                            jnp.where(column == 2 * number, high, halos[group]),
                        )
        for group in range(groups):
            h_out[group] = halos[group]

    def remote(source, dest, send, recv, at, device):
        return pltpu.make_async_remote_copy(
            src_ref=source,
            dst_ref=dest,
            send_sem=send.at[at],
            recv_sem=recv.at[at],
            device_id=device,
            device_id_type=MESH,
        )

    def base_copy(slot):
        return remote(
            b_out.at[peers[slot]], b_in.at[me], g_send, g_recv, (0, relation[slot]), {"harm": peers[slot]}
        )

    def halo_copy(slot):
        return remote(
            h_out.at[peers[slot]],
            h_in.at[me],
            g_send,
            g_recv,
            (1 + 2 * fields, relation[slot]),
            {"harm": peers[slot]},
        )

    def field_copy(field, slot):
        return remote(
            p_out.at[field, peers[slot]],
            p_in.at[field, me],
            g_send,
            g_recv,
            (1 + field, relation[slot]),
            {"harm": peers[slot]},
        )

    def back_copy(field, slot):
        return remote(
            sent.at[field, peers[slot]],
            back.at[field, me],
            g_send,
            g_recv,
            (1 + fields + field, relation[slot]),
            {"harm": peers[slot]},
        )

    def rim_copy(side, slot):
        where = (below, above)[side]
        if slot == len(everyone):
            return remote(
                stage.at[side],
                zrims.at[side],
                z_send,
                z_recv,
                (side, slot),
                {"harm": me, "tile": where},
            )
        return remote(
            rim_out.at[side, everyone[slot]],
            rim_in.at[side, me],
            z_send,
            z_recv,
            (side, role[slot]),
            {"harm": everyone[slot], "tile": where},
        )

    def late_copy(side, slot):
        return remote(
            rim_out.at[side, everyone[slot]],
            late_in.at[me],
            z_send,
            z_recv,
            (2, role[slot]),
            {"harm": everyone[slot], "tile": (below, above)[side]},
        )

    def fix_copy(slot):
        return remote(
            fix_out.at[peers[slot]],
            fix_in.at[me],
            g_send,
            g_recv,
            (2 + 2 * fields, relation[slot]),
            {"harm": peers[slot]},
        )

    def send_rims(side):
        for slot in range(len(everyone) + 1):
            rim_copy(side, slot).start()

    def send_late(side):
        for slot in range(len(everyone)):
            late_copy(side, slot).start()
        rim_copy(side, len(everyone)).start()

    pl.semaphore_wait(
        barrier,
        len(peers)
        + groups * (place > 0).astype(jnp.int32)
        + groups * highest.astype(jnp.int32),
    )

    @pl.when(place > 0)
    def _():
        tell(ready_up, below)
        loads[1].wait()
        loads[2].wait()
        prepare_rims()
        send_rims(0)

    @pl.when(highest)
    def _():
        tell(ready_down, above)
        send_late(1)

    for slot in range(len(peers)):
        base_copy(slot).start()

    @pl.when(lowest)
    def _():
        loads[1].wait()
        loads[2].wait()

    pack_fields()
    for slot in range(len(peers)):
        halo_copy(slot).start()

    def send_field(field):
        for slot in range(len(peers)):
            field_copy(field, slot).start()

    early = min(3, fields)
    for field in range(early):
        send_field(field)

    pl.when(lowest)(prepare_rims)

    @pl.when(inner)
    def _():
        pl.semaphore_wait(ready_up, groups)
        send_rims(1)

    @pl.when(lowest)
    def _():
        pl.semaphore_wait(ready_down, groups)
        send_late(0)

    for field in range(early, fields):
        send_field(field)

    b_in[me] = b_out[me]
    h_in[me] = h_out[me]
    for field in range(fields):
        p_in[field, me] = p_out[field, me]

    def take_rims(slot):
        group = everyone[slot]

        @pl.when(inner)
        def _():
            rim_copy(0, slot).wait_recv()

        @pl.when(highest)
        def _():
            rim_in[0, group] = jnp.zeros((deep, lanes), jnp.float32)

        @pl.when(place > 0)
        def _():
            rim_copy(1, slot).wait_recv()

        @pl.when(lowest)
        def _():
            rim_in[1, group] = jnp.zeros((deep, lanes), jnp.float32)

        above_rows, below_rows = rim_in[0, group], rim_in[1, group]
        rim_rows[group, 0] = jnp.where(low_lane, below_rows, above_rows)
        rim_rows[group, 1] = turn(jnp.where(low_lane, above_rows, below_rows), cols)

    for slot in range(len(peers)):
        base_copy(slot).wait_recv()
        halo_copy(slot).wait_recv()
    for slot in range(len(everyone)):
        take_rims(slot)

    def slopes(field, group):
        for pair in range(pairs):
            number = field * pairs + pair
            value = p_in[field, group, pair]
            edge = pltpu.roll(h_in[group], lanes - 1 - 2 * number, 1)
            north = jnp.where(column == cols - 1, edge, turn(value, -1))
            south = jnp.where(column == 0, edge, turn(value, 1))
            gy[group, pair] = 0.5 * (north - south)
            swapped = turn(value, cols)
            rim = rim_rows[group, pair % 2, pl.ds(pair // 2 * fields + field, 1), :]
            high = jnp.where(left, swapped, rim)
            low = jnp.where(left, rim, swapped)
            east = pltpu.roll(jnp.where(sub == 0, high, value), half - 1, 0)
            west = pltpu.roll(jnp.where(sub == half - 1, low, value), 1, 0)
            gx[group, pair] = 0.5 * (east - west)

    def convolve(field, target, index, sources, sums):
        real, imag = sums
        for group in sources:
            for at in range(local):
                shift = (target - group) * local + index - at
                shift = (shift + harmonics) % harmonics
                owner, first = shift // local, shift % local * 2 * kinds
                for which, values_of in enumerate((gx, gy, p_in.at[field])):
                    a_real = b_in[owner, first + which]
                    a_imag = b_in[owner, first + kinds + which]
                    q_real, q_imag = values_of[group, 2 * at], values_of[group, 2 * at + 1]
                    real = real + a_real * q_real - a_imag * q_imag
                    imag = imag + a_real * q_imag + a_imag * q_real
        return real, imag

    order = (*peers, me)

    at_end = lowest | highest

    def fix():
        for slot in range(len(everyone)):
            late_copy(0, slot).wait_recv()
        edge = (1 - lowest.astype(jnp.int32)) * (half - 1)
        scale = jnp.where(lowest, -0.5, 0.5)
        low_row = lax.broadcasted_iota(jnp.int32, (1, lanes), 1) < cols
        here = low_row == lowest

        def both(row):
            return scale * jnp.where(here, row, turn(row, cols))

        def straight(rows_here):
            return jnp.where(lowest, rows_here, turn(rows_here, cols))

        late = [straight(late_in[group]) for group in everyone]
        crossed = [turn(rows_here, cols) for rows_here in late]
        for target in everyone:
            for index in range(local):
                total = jnp.zeros((fields, lanes), jnp.float32)
                for number, group in enumerate(everyone):
                    for at in range(local):
                        shift = (target - group) * local + index - at
                        shift = (shift + harmonics) % harmonics
                        owner, first = shift // local, shift % local * 2 * kinds
                        real = both(b_in[owner, first, pl.ds(edge, 1), :])
                        imag = both(b_in[owner, first + kinds, pl.ds(edge, 1), :])
                        span = slice(at * fields, (at + 1) * fields)
                        total = total + real * late[number][span]
                        total = total + jnp.where(low_row, -imag, imag) * crossed[number][span]
                fix_out[target, index * fields : (index + 1) * fields, :] = total
        fix_in[me] = fix_out[me]
        for slot in range(len(peers)):
            fix_copy(slot).start()

    def one_field(field, _):
        @pl.when(at_end & (field == min(3, fields - 1)))
        def _():
            fix()

        field_copy(field, 2).wait_recv()
        slopes(field, me)
        slopes(field, partner)
        zero = jnp.zeros((half, lanes), jnp.float32)
        sums = [
            [convolve(field, target, index, (me, partner), (zero, zero)) for index in range(local)]
            for target in order
        ]
        field_copy(field, 0).wait_recv()
        slopes(field, far_first)
        field_copy(field, 1).wait_recv()
        slopes(field, far_second)
        for slot, target in enumerate(order):
            for index in range(local):
                real, imag = convolve(field, target, index, (far_first, far_second), sums[slot][index])
                if slot < len(peers):
                    sent[field, target, 2 * index] = real
                    sent[field, target, 2 * index + 1] = imag
                else:
                    back[field, me, 2 * index] = real
                    back[field, me, 2 * index + 1] = imag
            if slot < len(peers):
                back_copy(field, slot).start()
        return 0

    lax.fori_loop(0, fields, one_field, 0)

    for side in range(2):
        rim_copy(side, len(everyone)).wait_recv()

    row_at = lax.broadcasted_iota(jnp.int32, (rows, width), 0)

    def neighbours(value, number, at):
        high, low = zrims[0, number, at : at + 1, :], zrims[1, number, at : at + 1, :]
        east = jnp.where(row_at == rows - 1, high, pltpu.roll(value, rows - 1, 0))
        west = jnp.where(row_at == 0, low, pltpu.roll(value, 1, 0))
        return east, west

    def north_of(value):
        return pltpu.roll(value, width - 1, 1)

    def south_of(value):
        return pltpu.roll(value, 1, 1)

    center = vbuf[...]
    east, west = neighbours(center, 0, deep)
    east_face = 0.5 * (center + east)
    west_face = 0.5 * (center + west)
    north_face = 0.5 * (center + north_of(center))
    south_face = 0.5 * (center + south_of(center))
    for index in range(local):
        at = me * local + index
        signed = jnp.where(at < harmonics // 2, at, at - harmonics)
        frequency = omega_base * signed.astype(jnp.float32)
        for part in range(2):

            def sides(field):
                return neighbours(full[index, part, field], part, index * fields + field)

            def along_x(field):
                up, down = sides(field)
                return 0.5 * (up - down)

            def along_y(field):
                value = full[index, part, field]
                return 0.5 * (north_of(value) - south_of(value))

            dilation = along_x(1) + along_y(2)
            sound = {0: dilation, 4: dilation, 1: along_x(4), 2: along_y(4)}
            for field in range(fields):
                value = full[index, part, field]
                up, down = sides(field)
                damping = (
                    east_face * (up - value)
                    - west_face * (value - down)
                    + north_face * (north_of(value) - value)
                    - south_face * (value - south_of(value))
                )
                turned = full[index, 1 - part, field] * frequency
                result = turned if part else -turned
                if field in sound:
                    result = result + sound[field]
                own[index, part, field] = result - damping

    def add_fixes(edge):
        for slot in range(len(peers)):
            fix_copy(slot).wait_recv()
        for tile in range(width // lanes):
            span = slice(tile * lanes, (tile + 1) * lanes)
            first, second = fix_in[2 * tile], fix_in[2 * tile + 1]
            both = (
                jnp.where(low_lane, first, turn(second, cols)),
                jnp.where(low_lane, turn(first, cols), second),
            )
            for index in range(local):
                for part in range(2):
                    for field in range(fields):
                        at = index * fields + field
                        own[index, part, field, edge : edge + 1, span] += both[part][at : at + 1]

    for field in range(fields):
        if field == fields - 1:
            pl.when(lowest)(lambda: add_fixes(0))
            pl.when(highest)(lambda: add_fixes(rows - 1))
        for slot in range(len(peers)):
            back_copy(field, slot).wait_recv()
        if field < fields - 1:
            join(field, own, back, own, field)

    for slot in range(len(peers)):
        base_copy(slot).wait_send()
        halo_copy(slot).wait_send()
        for field in range(fields):
            field_copy(field, slot).wait_send()
            back_copy(field, slot).wait_send()
    def sent_rims(side):
        for slot in range(len(everyone)):
            rim_copy(side, slot).wait_send()

    pl.when(inner)(lambda: sent_rims(1))
    pl.when(place > 0)(lambda: sent_rims(0))

    @pl.when(at_end)
    def _():
        for slot in range(len(everyone)):
            late_copy(0, slot).wait_send()
        for slot in range(len(peers)):
            fix_copy(slot).wait_send()

    for side in range(2):
        rim_copy(side, len(everyone)).wait_send()


def join(field, own, back, out, at):
    local, _, _, rows, width = own.shape
    half, lanes = back.shape[-2:]
    left = lax.broadcasted_iota(jnp.int32, (half, lanes), 1) < lanes // 2
    for index in range(local):
        for part in range(2):
            pair = index * 2 + part
            for tile in range(width // lanes):
                span = slice(tile * lanes, (tile + 1) * lanes)
                first, second = back[field, 2 * tile, pair], back[field, 2 * tile + 1, pair]
                top = jnp.where(left, first, pltpu.roll(second, lanes // 2, 1))
                bottom = jnp.where(left, pltpu.roll(first, lanes // 2, 1), second)
                out[index, part, at, 0:half, span] = own[index, part, field, 0:half, span] + top
                out[index, part, at, half:rows, span] = (
                    own[index, part, field, half:rows, span] + bottom
                )


def join_kernel(own, back, out_hbm, out, sem):
    last = own.shape[2] - 1
    copies = [
        pltpu.make_async_copy(own.at[:, :, 0:last], out_hbm.at[:, :, 0:last], sem.at[0]),
        pltpu.make_async_copy(out, out_hbm.at[:, :, last : last + 1], sem.at[1]),
    ]
    copies[0].start()
    join(last, own, back, out, 0)
    copies[1].start()
    for copy in copies:
        copy.wait()


def quarters(perturbation, base_flow, viscosity):
    local, parts, fields, rows, width = perturbation.shape
    groups = lax.axis_size("harm")
    tiles = lax.axis_size("tile")
    kinds = base_flow.shape[2]
    half, lanes = rows // 2, 2 * (width // groups)
    pairs = 2 * local
    values = pairs * fields
    deep = values // 2
    dma = pltpu.SemaphoreType.DMA
    f32 = jnp.float32
    limit = 24 * 1024 * 1024
    whole = (local, parts, fields, rows, width)
    blocks = (fields, groups, pairs, half, lanes)
    inputs = [
        pltpu.with_memory_space_constraint(array, pltpu.HBM)
        for array in (perturbation, base_flow, viscosity)
    ]
    own, back = pl.pallas_call(
        functools.partial(quarter_kernel, groups, tiles),
        out_shape=(pltpu.VMEM(whole, f32), pltpu.VMEM(blocks, f32)),
        in_specs=[pl.BlockSpec(memory_space=pltpu.HBM)] * 3,
        out_specs=[pl.BlockSpec(memory_space=pltpu.VMEM)] * 2,
        scratch_shapes=[
            pltpu.VMEM(whole, f32),
            pltpu.VMEM((local, parts, kinds, rows, width), f32),
            pltpu.VMEM((rows, width), f32),
            pltpu.VMEM((2, 2, deep + 1, width), f32),
            pltpu.VMEM((2, 2, deep + 1, width), f32),
            pltpu.VMEM((2, groups, deep, lanes), f32),
            pltpu.VMEM((2, groups, deep, lanes), f32),
            pltpu.VMEM((groups, 2, deep, lanes), f32),
            pltpu.VMEM((groups, deep, lanes), f32),
            pltpu.VMEM((groups, deep, lanes), f32),
            pltpu.VMEM((groups, deep, lanes), f32),
            pltpu.VMEM((groups, kinds * pairs, half, lanes), f32),
            pltpu.VMEM((groups, kinds * pairs, half, lanes), f32),
            pltpu.VMEM((groups, half, lanes), f32),
            pltpu.VMEM((groups, half, lanes), f32),
            pltpu.VMEM(blocks, f32),
            pltpu.VMEM(blocks, f32),
            pltpu.VMEM((groups, pairs, half, lanes), f32),
            pltpu.VMEM((groups, pairs, half, lanes), f32),
            pltpu.VMEM(blocks, f32),
            dma((3,)),
            dma((3 + 2 * fields, 3)),
            dma((3 + 2 * fields, 3)),
            dma((3, 5)),
            dma((3, 5)),
            pltpu.SemaphoreType.REGULAR,
            pltpu.SemaphoreType.REGULAR,
        ],
        compiler_params=pltpu.CompilerParams(
            collective_id=0, has_side_effects=True, vmem_limit_bytes=limit
        ),
    )(*inputs)
    own = pltpu.with_memory_space_constraint(own, pltpu.VMEM)
    back = pltpu.with_memory_space_constraint(back, pltpu.VMEM)
    return pl.pallas_call(
        join_kernel,
        out_shape=jax.ShapeDtypeStruct(whole, f32),
        in_specs=[pl.BlockSpec(memory_space=pltpu.VMEM)] * 2,
        out_specs=pl.BlockSpec(memory_space=pl.ANY),
        scratch_shapes=[pltpu.VMEM((local, parts, 1, rows, width), f32), dma((2,))],
        compiler_params=pltpu.CompilerParams(vmem_limit_bytes=limit),
    )(own, back)


def solution(mesh):
    placed = (
        P("harm", None, None, ("parts", "tile"), None),
        P("harm", None, None, ("parts", "tile"), None),
        P(("parts", "tile"), None),
    )
    return jax.shard_map(
        shards,
        mesh=mesh,
        in_specs=placed,
        out_specs=P("harm", None, None, ("parts", "tile"), None),
        check_vma=False,
    )
```

```python
import functools

import jax
import jax.numpy as jnp
from jax import lax
from jax.experimental import pallas as pl
from jax.experimental.pallas import tpu as pltpu
from jax.sharding import PartitionSpec as P

omega_base = 0.25
MESH = pl.DeviceIdType.MESH


def kernel(
    groups,
    tiles,
    p_hbm,
    b_hbm,
    v_hbm,
    out,
    pbuf,
    bbuf,
    vbuf,
    stage,
    rims,
    gx,
    gy,
    local_sem,
    y_send,
    y_recv,
    chip_send,
    chip_recv,
    z_send,
    z_recv,
    rim_send,
    rim_recv,
):
    local, _, fields, rows, width = p_hbm.shape
    total = pbuf.shape[0]
    cores = 2
    chips = groups // cores
    rim_rows = local * 2 * fields
    me = lax.axis_index("harm")
    chip, core = me // cores, me % cores
    place = lax.axis_index("tile")
    partner = chip * cores + (1 - core)
    above, below = (place + 1) % tiles, (place + tiles - 1) % tiles

    def group_at(distance, own_core):
        at = (chip + chips - distance) % chips
        return at * cores + (core if own_core else 1 - core)

    def target_at(distance):
        return (chip + distance) % chips * cores + core

    first = me * local

    copy_p = pltpu.make_async_copy(p_hbm, pbuf.at[pl.ds(first, local)], local_sem.at[0])
    copy_b = pltpu.make_async_copy(b_hbm, bbuf.at[pl.ds(first, local)], local_sem.at[1])
    copy_v = pltpu.make_async_copy(v_hbm, vbuf, local_sem.at[2])
    copy_p.start()
    copy_v.start()
    copy_b.start()

    barrier = pltpu.get_barrier_semaphore()
    for distance in range(1, chips):
        pl.semaphore_signal(
            barrier, inc=1, device_id={"harm": target_at(distance)}, device_id_type=MESH
        )
    pl.semaphore_signal(barrier, inc=1, device_id={"harm": partner}, device_id_type=MESH)
    pl.semaphore_signal(barrier, inc=1, device_id={"tile": above}, device_id_type=MESH)
    pl.semaphore_signal(barrier, inc=1, device_id={"tile": below}, device_id_type=MESH)

    def pack(distance):
        start = group_at(distance, True) * local
        for index in range(local):
            for part in range(2):
                for field in range(fields):
                    row = (index * 2 + part) * fields + field
                    stage[distance, 0, row : row + 1, :] = pbuf[start + index, part, field, 0:1, :]
                    stage[distance, 1, row : row + 1, :] = pbuf[
                        start + index, part, field, rows - 1 : rows, :
                    ]

    copy_p.wait()
    copy_v.wait()
    pack(0)
    stage[0, 0, rim_rows : rim_rows + 1, :] = vbuf[0:1, :]
    stage[0, 1, rim_rows : rim_rows + 1, :] = vbuf[rows - 1 : rows, :]

    pl.semaphore_wait(barrier, chips + 2)

    y_copies = []
    for kind in range(2):
        source, dest = ((p_hbm, pbuf), (b_hbm, bbuf))[kind]
        for index in range(local):
            for distance in range(1, chips):
                copy = pltpu.make_async_remote_copy(
                    src_ref=source.at[index],
                    dst_ref=dest.at[first + index],
                    send_sem=y_send.at[distance - 1, kind, index],
                    recv_sem=y_recv.at[distance - 1, kind, index],
                    device_id={"harm": target_at(distance)},
                    device_id_type=MESH,
                )
                copy.start()
                y_copies.append((distance, kind, index, copy))

    def rim_copies(distance):
        group = group_at(distance, True)
        return [
            pltpu.make_async_remote_copy(
                src_ref=stage.at[distance, side],
                dst_ref=rims.at[group, 1 - side],
                send_sem=z_send.at[distance, side],
                recv_sem=z_recv.at[distance, side],
                device_id={"tile": (below, above)[side]},
                device_id_type=MESH,
            )
            for side in range(2)
        ]

    started = []
    rim_pending = {}

    def send_rims(distance):
        rim_pending[distance] = rim_copies(distance)
        for copy in rim_pending[distance]:
            copy.start()

    def relay_copy(distance, kind, index):
        at = group_at(distance, True) * local + index
        dest = (pbuf, bbuf)[kind]
        source = dest.at[at] if distance else (p_hbm, b_hbm)[kind].at[index]
        return pltpu.make_async_remote_copy(
            src_ref=source,
            dst_ref=dest.at[at],
            send_sem=chip_send.at[distance, kind, index],
            recv_sem=chip_recv.at[distance, kind, index],
            device_id={"harm": partner},
            device_id_type=MESH,
        )

    relays = {}

    def relay(distance, kind, index):
        relays[distance, kind, index] = relay_copy(distance, kind, index)
        relays[distance, kind, index].start()

    def relay_rims(distance):
        group = group_at(distance, True)
        relays[distance] = pltpu.make_async_remote_copy(
            src_ref=rims.at[group],
            dst_ref=rims.at[group],
            send_sem=rim_send.at[distance],
            recv_sem=rim_recv.at[distance],
            device_id={"harm": partner},
            device_id_type=MESH,
        )
        relays[distance].start()

    send_rims(0)
    for kind in range(2):
        for index in range(local):
            relay(0, kind, index)

    row_at = lax.broadcasted_iota(jnp.int32, (rows, width), 0)

    def neighbours(value, low, high):
        east = jnp.where(row_at == rows - 1, high, pltpu.roll(value, rows - 1, 0))
        west = jnp.where(row_at == 0, low, pltpu.roll(value, 1, 0))
        return east, west

    def slope_y(group):
        def one(index, _):
            at = group * local + index
            for part in range(2):
                for field in range(fields):
                    value = pbuf[at, part, field]
                    gy[at, part, field] = 0.5 * (
                        pltpu.roll(value, width - 1, 1) - pltpu.roll(value, 1, 1)
                    )
            return 0

        lax.fori_loop(0, local, one, 0)

    def slope_x(group):
        for index in range(local):
            at = group * local + index
            for part in range(2):
                for field in range(fields):
                    row = (index * 2 + part) * fields + field
                    east, west = neighbours(
                        pbuf[at, part, field],
                        rims[group, 0, row : row + 1, :],
                        rims[group, 1, row : row + 1, :],
                    )
                    gx[at, part, field] = 0.5 * (east - west)

    def own_terms():
        center = vbuf[...]
        east, west = neighbours(
            center,
            rims[me, 0, rim_rows : rim_rows + 1, :],
            rims[me, 1, rim_rows : rim_rows + 1, :],
        )
        east_face = 0.5 * (center + east)
        west_face = 0.5 * (center + west)
        north_face = 0.5 * (center + pltpu.roll(center, width - 1, 1))
        south_face = 0.5 * (center + pltpu.roll(center, 1, 1))
        for index in range(local):
            at = first + index
            signed = jnp.where(at < total // 2, at, at - total)
            frequency = omega_base * signed.astype(jnp.float32)
            for part in range(2):
                for field in range(fields):
                    row = (index * 2 + part) * fields + field
                    value = pbuf[at, part, field]
                    up, down = neighbours(
                        value,
                        rims[me, 0, row : row + 1, :],
                        rims[me, 1, row : row + 1, :],
                    )
                    damping = (
                        east_face * (up - value)
                        - west_face * (value - down)
                        + north_face * (pltpu.roll(value, width - 1, 1) - value)
                        - south_face * (value - pltpu.roll(value, 1, 1))
                    )
                    turned = pbuf[at, 1 - part, field] * frequency
                    result = turned - damping if part else -turned - damping
                    if field == 0 or field == 4:
                        result = result + (gx[at, part, 1] + gy[at, part, 2])
                    elif field == 1:
                        result = result + gx[at, part, 4]
                    elif field == 2:
                        result = result + gy[at, part, 4]
                    out[index, part, field] = result

    def couple(at):
        def strip(step, _):
            span = pl.ds(pl.multiple_of(step * 8, 8), 8)
            base = [[bbuf[at, part, which, span, :] for part in range(2)] for which in range(3)]
            for index in range(local):
                source = (first + index + total - at) % total
                for field in range(fields):
                    real = out[index, 0, field, span, :]
                    imag = out[index, 1, field, span, :]
                    for which, values in ((0, gx), (1, gy), (2, pbuf)):
                        a_real, a_imag = base[which]
                        q_real = values[source, 0, field, span, :]
                        q_imag = values[source, 1, field, span, :]
                        real = real + a_real * q_real - a_imag * q_imag
                        imag = imag + a_real * q_imag + a_imag * q_real
                    out[index, 0, field, span, :] = real
                    out[index, 1, field, span, :] = imag
            return 0

        lax.fori_loop(0, rows // 8, strip, 0)

    def wait_y(distance, kind, index):
        for other, what, which, copy in y_copies:
            if (other, what, which) == (distance, kind, index):
                copy.wait_recv()

    slope_y(me)
    for copy in rim_pending[0]:
        copy.wait_recv()
    relay_rims(0)
    slope_x(me)
    own_terms()
    for index in range(local):
        relays[0, 0, index].wait_recv()
    slope_y(partner)
    relays[0].wait_recv()
    slope_x(partner)

    for distance in range(1, chips):
        for index in range(local):
            wait_y(distance, 0, index)
            relay(distance, 0, index)
        pack(distance)
        send_rims(distance)
    for distance in range(1, chips):
        slope_y(group_at(distance, True))
        for index in range(local):
            relays[distance, 0, index].wait_recv()
        slope_y(group_at(distance, False))
    for distance in range(1, chips):
        for index in range(local - 1):
            wait_y(distance, 1, index)
            relay(distance, 1, index)
    for distance in range(1, chips):
        for copy in rim_pending[distance]:
            copy.wait_recv()
        relay_rims(distance)
        slope_x(group_at(distance, True))
    for distance in range(1, chips):
        relays[distance].wait_recv()
        slope_x(group_at(distance, False))

    copy_b.wait()
    for index in range(local):
        couple(first + index)
    for index in range(local):
        relays[0, 1, index].wait_recv()
        couple(partner * local + index)
    for distance in range(1, chips):
        wait_y(distance, 1, local - 1)
        relay(distance, 1, local - 1)
    for distance in range(1, chips):
        for index in range(local):
            couple(group_at(distance, True) * local + index)
    for distance in range(1, chips):
        for index in range(local):
            relays[distance, 1, index].wait_recv()
            couple(group_at(distance, False) * local + index)

    for _, _, _, copy in y_copies:
        copy.wait_send()
    for copies in rim_pending.values():
        for copy in copies:
            copy.wait_send()
    for copy in relays.values():
        copy.wait_send()


def shards(perturbation, base_flow, viscosity):
    local, parts, fields, rows, width = perturbation.shape
    groups = lax.axis_size("harm")
    tiles = lax.axis_size("tile")
    chips = groups // 2
    cols = width // groups
    if (
        chips == 2
        and tiles > 2
        and rows == 16
        and 2 * cols == 128
        and 2 * local * parts * fields <= cols
    ):
        return quarters(perturbation, base_flow, viscosity)
    total = local * groups
    rim = -(-(local * parts * fields + 1) // 8) * 8
    kinds = base_flow.shape[2]
    dma = pltpu.SemaphoreType.DMA
    f32 = jnp.float32
    return pl.pallas_call(
        functools.partial(kernel, groups, tiles),
        out_shape=jax.ShapeDtypeStruct(perturbation.shape, f32),
        in_specs=[pl.BlockSpec(memory_space=pl.ANY)] * 3,
        out_specs=pl.BlockSpec(memory_space=pltpu.VMEM),
        scratch_shapes=[
            pltpu.VMEM((total, 2, fields, rows, width), f32),
            pltpu.VMEM((total, 2, kinds, rows, width), f32),
            pltpu.VMEM((rows, width), f32),
            pltpu.VMEM((chips, 2, rim, width), f32),
            pltpu.VMEM((groups, 2, rim, width), f32),
            pltpu.VMEM((total, 2, fields, rows, width), f32),
            pltpu.VMEM((total, 2, fields, rows, width), f32),
            dma((3,)),
            dma((chips - 1, 2, local)),
            dma((chips - 1, 2, local)),
            dma((chips, 2, local)),
            dma((chips, 2, local)),
            dma((chips, 2)),
            dma((chips, 2)),
            dma((chips,)),
            dma((chips,)),
        ],
        compiler_params=pltpu.CompilerParams(collective_id=0, has_side_effects=True),
    )(perturbation, base_flow, viscosity)


def quarter_kernel(
    groups,
    tiles,
    p_hbm,
    b_hbm,
    v_hbm,
    own,
    back,
    full,
    base,
    vbuf,
    stage,
    zrims,
    rim_out,
    rim_in,
    rim_rows,
    late_in,
    fix_out,
    fix_in,
    b_out,
    b_in,
    h_out,
    h_in,
    p_out,
    p_in,
    gx,
    gy,
    sent,
    load_sem,
    g_send,
    g_recv,
    z_send,
    z_recv,
    ready_up,
    ready_down,
):
    local, _, fields, rows, width = p_hbm.shape
    kinds = b_hbm.shape[2]
    harmonics = local * groups
    half = rows // 2
    cols = width // groups
    lanes = 2 * cols
    pairs = 2 * local
    values = pairs * fields
    deep = values // 2
    me = lax.axis_index("harm")
    chip, core = me // 2, me % 2
    place = lax.axis_index("tile")
    partner = chip * 2 + (1 - core)
    far_first, far_second = (1 - chip) * 2, (1 - chip) * 2 + 1
    peers = (far_first, far_second, partner)
    relation = (core, 1 - core, 2)
    everyone = (me, partner, far_first, far_second)
    role = (0, 1, 2 + core, 3 - core)
    above, below = (place + 1) % tiles, (place + tiles - 1) % tiles
    inner, lowest, highest = place < tiles - 1, place == 0, place == tiles - 1

    def tell(semaphore, where):
        for group in everyone:
            pl.semaphore_signal(
                semaphore, inc=1, device_id={"harm": group, "tile": where}, device_id_type=MESH
            )

    barrier = pltpu.get_barrier_semaphore()
    for group in peers:
        pl.semaphore_signal(barrier, inc=1, device_id={"harm": group}, device_id_type=MESH)

    loads = [
        pltpu.make_async_copy(source, dest, load_sem.at[at])
        for at, (source, dest) in enumerate(((b_hbm, base), (p_hbm, full), (v_hbm, vbuf)))
    ]
    for copy in loads:
        copy.start()

    @pl.when(inner)
    def _():
        tell(barrier, above)

    @pl.when(lowest)
    def _():
        tell(barrier, below)

    lane = lax.broadcasted_iota(jnp.int32, (half, lanes), 1)
    sub = lax.broadcasted_iota(jnp.int32, (half, lanes), 0)
    left = lane < cols
    column = lane % cols

    def turn(value, shift):
        return pltpu.roll(value, shift % lanes, 1)

    def packed(ref, at):
        blocks = []
        for tile in range(width // lanes):
            span = slice(tile * lanes, (tile + 1) * lanes)
            top = ref[(*at, slice(0, half), span)]
            bottom = ref[(*at, slice(half, rows), span)]
            blocks.append(jnp.where(left, top, turn(bottom, cols)))
            blocks.append(jnp.where(left, turn(top, cols), bottom))
        return blocks

    loads[0].wait()
    for index in range(local):
        for part in range(2):
            for which in range(kinds):
                for group, block in enumerate(packed(base, (index, part, which))):
                    b_out[group, (index * 2 + part) * kinds + which] = block

    low_lane = lax.broadcasted_iota(jnp.int32, (deep, lanes), 1) < cols

    def prepare_rims():
        for field in range(fields):
            for index in range(local):
                for part in range(2):
                    at = index * fields + field
                    stage[0, part, at : at + 1, :] = full[index, part, field, 0:1, :]
                    stage[1, part, at : at + 1, :] = full[index, part, field, rows - 1 : rows, :]
        stage[0, 0, deep : deep + 1, :] = vbuf[0:1, :]
        stage[1, 0, deep : deep + 1, :] = vbuf[rows - 1 : rows, :]
        for side in range(2):
            for group in range(groups):
                tile, odd = group * cols // lanes, group * cols % lanes
                span = slice(tile * lanes, (tile + 1) * lanes)
                first = stage[side, 0, 0:deep, span]
                second = stage[side, 1, 0:deep, span]
                if side == 0:
                    first, second = second, first
                if odd:
                    first = turn(first, cols)
                else:
                    second = turn(second, cols)
                rim_out[side, group] = jnp.where(low_lane, first, second)

    def pack_fields():
        halos = [jnp.zeros((half, lanes), jnp.float32) for _ in range(groups)]
        for field in range(fields):
            for index in range(local):
                for part in range(2):
                    number = field * pairs + index * 2 + part
                    blocks = packed(full, (index, part, field))
                    for group, block in enumerate(blocks):
                        p_out[field, group, index * 2 + part] = block
                        low = turn(blocks[(group - 1) % groups], 2 * number + 2 - cols)
                        high = turn(blocks[(group + 1) % groups], 2 * number + cols)
                        halos[group] = jnp.where(
                            column == 2 * number + 1,
                            low,
                            jnp.where(column == 2 * number, high, halos[group]),
                        )
        for group in range(groups):
            h_out[group] = halos[group]

    def remote(source, dest, send, recv, at, device):
        return pltpu.make_async_remote_copy(
            src_ref=source,
            dst_ref=dest,
            send_sem=send.at[at],
            recv_sem=recv.at[at],
            device_id=device,
            device_id_type=MESH,
        )

    def base_copy(slot):
        return remote(
            b_out.at[peers[slot]], b_in.at[me], g_send, g_recv, (0, relation[slot]), {"harm": peers[slot]}
        )

    def halo_copy(slot):
        return remote(
            h_out.at[peers[slot]],
            h_in.at[me],
            g_send,
            g_recv,
            (1 + 2 * fields, relation[slot]),
            {"harm": peers[slot]},
        )

    def field_copy(field, slot):
        return remote(
            p_out.at[field, peers[slot]],
            p_in.at[field, me],
            g_send,
            g_recv,
            (1 + field, relation[slot]),
            {"harm": peers[slot]},
        )

    def back_copy(field, slot):
        return remote(
            sent.at[field, peers[slot]],
            back.at[field, me],
            g_send,
            g_recv,
            (1 + fields + field, relation[slot]),
            {"harm": peers[slot]},
        )

    def rim_copy(side, slot):
        where = (below, above)[side]
        if slot == len(everyone):
            return remote(
                stage.at[side],
                zrims.at[side],
                z_send,
                z_recv,
                (side, slot),
                {"harm": me, "tile": where},
            )
        return remote(
            rim_out.at[side, everyone[slot]],
            rim_in.at[side, me],
            z_send,
            z_recv,
            (side, role[slot]),
            {"harm": everyone[slot], "tile": where},
        )

    def late_copy(side, slot):
        return remote(
            rim_out.at[side, everyone[slot]],
            late_in.at[me],
            z_send,
            z_recv,
            (2, role[slot]),
            {"harm": everyone[slot], "tile": (below, above)[side]},
        )

    def fix_copy(slot):
        return remote(
            fix_out.at[peers[slot]],
            fix_in.at[me],
            g_send,
            g_recv,
            (2 + 2 * fields, relation[slot]),
            {"harm": peers[slot]},
        )

    def send_rims(side):
        for slot in range(len(everyone) + 1):
            rim_copy(side, slot).start()

    def send_late(side):
        for slot in range(len(everyone)):
            late_copy(side, slot).start()
        rim_copy(side, len(everyone)).start()

    pl.semaphore_wait(
        barrier,
        len(peers)
        + groups * (place > 0).astype(jnp.int32)
        + groups * highest.astype(jnp.int32),
    )

    @pl.when(place > 0)
    def _():
        tell(ready_up, below)
        loads[1].wait()
        loads[2].wait()
        prepare_rims()
        send_rims(0)

    @pl.when(highest)
    def _():
        tell(ready_down, above)
        send_late(1)

    for slot in range(len(peers)):
        base_copy(slot).start()

    @pl.when(lowest)
    def _():
        loads[1].wait()
        loads[2].wait()

    pack_fields()
    for slot in range(len(peers)):
        halo_copy(slot).start()

    def send_field(field):
        for slot in range(len(peers)):
            field_copy(field, slot).start()

    early = min(3, fields)
    for field in range(early):
        send_field(field)

    pl.when(lowest)(prepare_rims)

    @pl.when(inner)
    def _():
        pl.semaphore_wait(ready_up, groups)
        send_rims(1)

    @pl.when(lowest)
    def _():
        pl.semaphore_wait(ready_down, groups)
        send_late(0)

    for field in range(early, fields):
        send_field(field)

    b_in[me] = b_out[me]
    h_in[me] = h_out[me]
    for field in range(fields):
        p_in[field, me] = p_out[field, me]

    def set_rims(group):
        above_rows, below_rows = rim_in[0, group], rim_in[1, group]
        rim_rows[group, 0] = jnp.where(low_lane, below_rows, above_rows)
        rim_rows[group, 1] = turn(jnp.where(low_lane, above_rows, below_rows), cols)

    def take_rims(slot):
        group = everyone[slot]

        @pl.when(inner)
        def _():
            rim_copy(0, slot).wait_recv()

        @pl.when(highest)
        def _():
            rim_in[0, group] = jnp.zeros((deep, lanes), jnp.float32)

        @pl.when(place > 0)
        def _():
            rim_copy(1, slot).wait_recv()

        @pl.when(lowest)
        def _():
            rim_in[1, group] = jnp.zeros((deep, lanes), jnp.float32)

        set_rims(group)

    for slot in range(len(peers)):
        base_copy(slot).wait_recv()
        halo_copy(slot).wait_recv()
    for slot in range(len(everyone)):
        take_rims(slot)

    def slopes(field, group):
        for pair in range(pairs):
            number = field * pairs + pair
            value = p_in[field, group, pair]
            edge = pltpu.roll(h_in[group], lanes - 1 - 2 * number, 1)
            north = jnp.where(column == cols - 1, edge, turn(value, -1))
            south = jnp.where(column == 0, edge, turn(value, 1))
            gy[group, pair] = 0.5 * (north - south)
            swapped = turn(value, cols)
            rim = rim_rows[group, pair % 2, pl.ds(pair // 2 * fields + field, 1), :]
            high = jnp.where(left, swapped, rim)
            low = jnp.where(left, rim, swapped)
            east = pltpu.roll(jnp.where(sub == 0, high, value), half - 1, 0)
            west = pltpu.roll(jnp.where(sub == half - 1, low, value), 1, 0)
            gx[group, pair] = 0.5 * (east - west)

    def convolve(field, target, index, sources, sums):
        real, imag = sums
        for group in sources:
            for at in range(local):
                shift = (target - group) * local + index - at
                shift = (shift + harmonics) % harmonics
                owner, first = shift // local, shift % local * 2 * kinds
                for which, values_of in enumerate((gx, gy, p_in.at[field])):
                    a_real = b_in[owner, first + which]
                    a_imag = b_in[owner, first + kinds + which]
                    q_real, q_imag = values_of[group, 2 * at], values_of[group, 2 * at + 1]
                    real = real + a_real * q_real - a_imag * q_imag
                    imag = imag + a_real * q_imag + a_imag * q_real
        return real, imag

    order = (*peers, me)

    at_end = lowest | highest
    cut = fix_out.shape[1] // local

    def fix():
        for slot in range(len(everyone)):
            late_copy(0, slot).wait_recv()
        edge = (1 - lowest.astype(jnp.int32)) * (half - 1)
        scale = jnp.where(lowest, -0.5, 0.5)
        low_row = lax.broadcasted_iota(jnp.int32, (1, lanes), 1) < cols
        here = low_row == lowest

        def both(row):
            return scale * jnp.where(here, row, turn(row, cols))

        def straight(rows_here):
            return jnp.where(lowest, rows_here, turn(rows_here, cols))

        late = [straight(late_in[group]) for group in everyone]
        crossed = [turn(rows_here, cols) for rows_here in late]
        for target in everyone:
            for index in range(local):
                total = jnp.zeros((cut, lanes), jnp.float32)
                for number, group in enumerate(everyone):
                    for at in range(local):
                        shift = (target - group) * local + index - at
                        shift = (shift + harmonics) % harmonics
                        owner, first = shift // local, shift % local * 2 * kinds
                        real = both(b_in[owner, first, pl.ds(edge, 1), :])
                        imag = both(b_in[owner, first + kinds, pl.ds(edge, 1), :])
                        span = slice(at * fields, at * fields + cut)
                        total = total + real * late[number][span]
                        total = total + jnp.where(low_row, -imag, imag) * crossed[number][span]
                fix_out[target, index * cut : (index + 1) * cut, :] = total
        fix_in[me] = fix_out[me]

        @pl.when(lowest)
        def _():
            rim_in[1] = late_in[...]

        @pl.when(highest)
        def _():
            rim_in[0] = late_in[...]

        for group in everyone:
            set_rims(group)
        for slot in range(len(peers)):
            fix_copy(slot).start()

    def one_field(field, _):
        @pl.when(at_end & (field == cut))
        def _():
            fix()

        field_copy(field, 2).wait_recv()
        slopes(field, me)
        slopes(field, partner)
        zero = jnp.zeros((half, lanes), jnp.float32)
        sums = [
            [convolve(field, target, index, (me, partner), (zero, zero)) for index in range(local)]
            for target in order
        ]
        field_copy(field, 0).wait_recv()
        slopes(field, far_first)
        field_copy(field, 1).wait_recv()
        slopes(field, far_second)
        for slot, target in enumerate(order):
            for index in range(local):
                real, imag = convolve(field, target, index, (far_first, far_second), sums[slot][index])
                if slot < len(peers):
                    sent[field, target, 2 * index] = real
                    sent[field, target, 2 * index + 1] = imag
                else:
                    back[field, me, 2 * index] = real
                    back[field, me, 2 * index + 1] = imag
            if slot < len(peers):
                back_copy(field, slot).start()
        return 0

    lax.fori_loop(0, fields, one_field, 0)

    for side in range(2):
        rim_copy(side, len(everyone)).wait_recv()

    row_at = lax.broadcasted_iota(jnp.int32, (rows, width), 0)

    def neighbours(value, number, at):
        high, low = zrims[0, number, at : at + 1, :], zrims[1, number, at : at + 1, :]
        east = jnp.where(row_at == rows - 1, high, pltpu.roll(value, rows - 1, 0))
        west = jnp.where(row_at == 0, low, pltpu.roll(value, 1, 0))
        return east, west

    def north_of(value):
        return pltpu.roll(value, width - 1, 1)

    def south_of(value):
        return pltpu.roll(value, 1, 1)

    center = vbuf[...]
    east, west = neighbours(center, 0, deep)
    east_face = 0.5 * (center + east)
    west_face = 0.5 * (center + west)
    north_face = 0.5 * (center + north_of(center))
    south_face = 0.5 * (center + south_of(center))
    for index in range(local):
        at = me * local + index
        signed = jnp.where(at < harmonics // 2, at, at - harmonics)
        frequency = omega_base * signed.astype(jnp.float32)
        for part in range(2):

            def sides(field):
                return neighbours(full[index, part, field], part, index * fields + field)

            def along_x(field):
                up, down = sides(field)
                return 0.5 * (up - down)

            def along_y(field):
                value = full[index, part, field]
                return 0.5 * (north_of(value) - south_of(value))

            dilation = along_x(1) + along_y(2)
            sound = {0: dilation, 4: dilation, 1: along_x(4), 2: along_y(4)}
            for field in range(fields):
                value = full[index, part, field]
                up, down = sides(field)
                damping = (
                    east_face * (up - value)
                    - west_face * (value - down)
                    + north_face * (north_of(value) - value)
                    - south_face * (value - south_of(value))
                )
                turned = full[index, 1 - part, field] * frequency
                result = turned if part else -turned
                if field in sound:
                    result = result + sound[field]
                own[index, part, field] = result - damping

    def add_fixes(edge):
        for slot in range(len(peers)):
            fix_copy(slot).wait_recv()
        for tile in range(width // lanes):
            span = slice(tile * lanes, (tile + 1) * lanes)
            first, second = fix_in[2 * tile], fix_in[2 * tile + 1]
            both = (
                jnp.where(low_lane[: local * cut], first, turn(second, cols)),
                jnp.where(low_lane[: local * cut], turn(first, cols), second),
            )
            for index in range(local):
                for part in range(2):
                    for field in range(cut):
                        at = index * cut + field
                        own[index, part, field, edge : edge + 1, span] += both[part][at : at + 1]

    for field in range(fields):
        if field == fields - 1:
            pl.when(lowest)(lambda: add_fixes(0))
            pl.when(highest)(lambda: add_fixes(rows - 1))
        for slot in range(len(peers)):
            back_copy(field, slot).wait_recv()
        if field < fields - 1:
            join(field, own, back, own, field)

    for slot in range(len(peers)):
        base_copy(slot).wait_send()
        halo_copy(slot).wait_send()
        for field in range(fields):
            field_copy(field, slot).wait_send()
            back_copy(field, slot).wait_send()
    def sent_rims(side):
        for slot in range(len(everyone)):
            rim_copy(side, slot).wait_send()

    pl.when(inner)(lambda: sent_rims(1))
    pl.when(place > 0)(lambda: sent_rims(0))

    @pl.when(at_end)
    def _():
        for slot in range(len(everyone)):
            late_copy(0, slot).wait_send()
        for slot in range(len(peers)):
            fix_copy(slot).wait_send()

    for side in range(2):
        rim_copy(side, len(everyone)).wait_send()


def join(field, own, back, out, at):
    local, _, _, rows, width = own.shape
    half, lanes = back.shape[-2:]
    left = lax.broadcasted_iota(jnp.int32, (half, lanes), 1) < lanes // 2
    for index in range(local):
        for part in range(2):
            pair = index * 2 + part
            for tile in range(width // lanes):
                span = slice(tile * lanes, (tile + 1) * lanes)
                first, second = back[field, 2 * tile, pair], back[field, 2 * tile + 1, pair]
                top = jnp.where(left, first, pltpu.roll(second, lanes // 2, 1))
                bottom = jnp.where(left, pltpu.roll(first, lanes // 2, 1), second)
                out[index, part, at, 0:half, span] = own[index, part, field, 0:half, span] + top
                out[index, part, at, half:rows, span] = (
                    own[index, part, field, half:rows, span] + bottom
                )


def join_kernel(own, back, out_hbm, out, sem):
    last = own.shape[2] - 1
    copies = [
        pltpu.make_async_copy(own.at[:, :, 0:last], out_hbm.at[:, :, 0:last], sem.at[0]),
        pltpu.make_async_copy(out, out_hbm.at[:, :, last : last + 1], sem.at[1]),
    ]
    copies[0].start()
    join(last, own, back, out, 0)
    copies[1].start()
    for copy in copies:
        copy.wait()


def quarters(perturbation, base_flow, viscosity):
    local, parts, fields, rows, width = perturbation.shape
    groups = lax.axis_size("harm")
    tiles = lax.axis_size("tile")
    kinds = base_flow.shape[2]
    half, lanes = rows // 2, 2 * (width // groups)
    pairs = 2 * local
    values = pairs * fields
    deep = values // 2
    cut = min(3, fields - 1)
    dma = pltpu.SemaphoreType.DMA
    f32 = jnp.float32
    limit = 24 * 1024 * 1024
    whole = (local, parts, fields, rows, width)
    blocks = (fields, groups, pairs, half, lanes)
    inputs = [
        pltpu.with_memory_space_constraint(array, pltpu.HBM)
        for array in (perturbation, base_flow, viscosity)
    ]
    own, back = pl.pallas_call(
        functools.partial(quarter_kernel, groups, tiles),
        out_shape=(pltpu.VMEM(whole, f32), pltpu.VMEM(blocks, f32)),
        in_specs=[pl.BlockSpec(memory_space=pltpu.HBM)] * 3,
        out_specs=[pl.BlockSpec(memory_space=pltpu.VMEM)] * 2,
        scratch_shapes=[
            pltpu.VMEM(whole, f32),
            pltpu.VMEM((local, parts, kinds, rows, width), f32),
            pltpu.VMEM((rows, width), f32),
            pltpu.VMEM((2, 2, deep + 1, width), f32),
            pltpu.VMEM((2, 2, deep + 1, width), f32),
            pltpu.VMEM((2, groups, deep, lanes), f32),
            pltpu.VMEM((2, groups, deep, lanes), f32),
            pltpu.VMEM((groups, 2, deep, lanes), f32),
            pltpu.VMEM((groups, deep, lanes), f32),
            pltpu.VMEM((groups, local * cut, lanes), f32),
            pltpu.VMEM((groups, local * cut, lanes), f32),
            pltpu.VMEM((groups, kinds * pairs, half, lanes), f32),
            pltpu.VMEM((groups, kinds * pairs, half, lanes), f32),
            pltpu.VMEM((groups, half, lanes), f32),
            pltpu.VMEM((groups, half, lanes), f32),
            pltpu.VMEM(blocks, f32),
            pltpu.VMEM(blocks, f32),
            pltpu.VMEM((groups, pairs, half, lanes), f32),
            pltpu.VMEM((groups, pairs, half, lanes), f32),
            pltpu.VMEM(blocks, f32),
            dma((3,)),
            dma((3 + 2 * fields, 3)),
            dma((3 + 2 * fields, 3)),
            dma((3, 5)),
            dma((3, 5)),
            pltpu.SemaphoreType.REGULAR,
            pltpu.SemaphoreType.REGULAR,
        ],
        compiler_params=pltpu.CompilerParams(
            collective_id=0, has_side_effects=True, vmem_limit_bytes=limit
        ),
    )(*inputs)
    own = pltpu.with_memory_space_constraint(own, pltpu.VMEM)
    back = pltpu.with_memory_space_constraint(back, pltpu.VMEM)
    return pl.pallas_call(
        join_kernel,
        out_shape=jax.ShapeDtypeStruct(whole, f32),
        in_specs=[pl.BlockSpec(memory_space=pltpu.VMEM)] * 2,
        out_specs=pl.BlockSpec(memory_space=pl.ANY),
        scratch_shapes=[pltpu.VMEM((local, parts, 1, rows, width), f32), dma((2,))],
        compiler_params=pltpu.CompilerParams(vmem_limit_bytes=limit),
    )(own, back)


def solution(mesh):
    placed = (
        P("harm", None, None, ("parts", "tile"), None),
        P("harm", None, None, ("parts", "tile"), None),
        P(("parts", "tile"), None),
    )
    return jax.shard_map(
        shards,
        mesh=mesh,
        in_specs=placed,
        out_specs=P("harm", None, None, ("parts", "tile"), None),
        check_vma=False,
    )
```

```python
import functools

import jax
import jax.numpy as jnp
from jax import lax
from jax.experimental import pallas as pl
from jax.experimental.pallas import tpu as pltpu
from jax.sharding import PartitionSpec as P

omega_base = 0.25
MESH = pl.DeviceIdType.MESH


def kernel(
    groups,
    tiles,
    p_hbm,
    b_hbm,
    v_hbm,
    out,
    pbuf,
    bbuf,
    vbuf,
    stage,
    rims,
    gx,
    gy,
    local_sem,
    y_send,
    y_recv,
    chip_send,
    chip_recv,
    z_send,
    z_recv,
    rim_send,
    rim_recv,
):
    local, _, fields, rows, width = p_hbm.shape
    total = pbuf.shape[0]
    cores = 2
    chips = groups // cores
    rim_rows = local * 2 * fields
    me = lax.axis_index("harm")
    chip, core = me // cores, me % cores
    place = lax.axis_index("tile")
    partner = chip * cores + (1 - core)
    above, below = (place + 1) % tiles, (place + tiles - 1) % tiles

    def group_at(distance, own_core):
        at = (chip + chips - distance) % chips
        return at * cores + (core if own_core else 1 - core)

    def target_at(distance):
        return (chip + distance) % chips * cores + core

    first = me * local

    copy_p = pltpu.make_async_copy(p_hbm, pbuf.at[pl.ds(first, local)], local_sem.at[0])
    copy_b = pltpu.make_async_copy(b_hbm, bbuf.at[pl.ds(first, local)], local_sem.at[1])
    copy_v = pltpu.make_async_copy(v_hbm, vbuf, local_sem.at[2])
    copy_p.start()
    copy_v.start()
    copy_b.start()

    barrier = pltpu.get_barrier_semaphore()
    for distance in range(1, chips):
        pl.semaphore_signal(
            barrier, inc=1, device_id={"harm": target_at(distance)}, device_id_type=MESH
        )
    pl.semaphore_signal(barrier, inc=1, device_id={"harm": partner}, device_id_type=MESH)
    pl.semaphore_signal(barrier, inc=1, device_id={"tile": above}, device_id_type=MESH)
    pl.semaphore_signal(barrier, inc=1, device_id={"tile": below}, device_id_type=MESH)

    def pack(distance):
        start = group_at(distance, True) * local
        for index in range(local):
            for part in range(2):
                for field in range(fields):
                    row = (index * 2 + part) * fields + field
                    stage[distance, 0, row : row + 1, :] = pbuf[start + index, part, field, 0:1, :]
                    stage[distance, 1, row : row + 1, :] = pbuf[
                        start + index, part, field, rows - 1 : rows, :
                    ]

    copy_p.wait()
    copy_v.wait()
    pack(0)
    stage[0, 0, rim_rows : rim_rows + 1, :] = vbuf[0:1, :]
    stage[0, 1, rim_rows : rim_rows + 1, :] = vbuf[rows - 1 : rows, :]

    pl.semaphore_wait(barrier, chips + 2)

    y_copies = []
    for kind in range(2):
        source, dest = ((p_hbm, pbuf), (b_hbm, bbuf))[kind]
        for index in range(local):
            for distance in range(1, chips):
                copy = pltpu.make_async_remote_copy(
                    src_ref=source.at[index],
                    dst_ref=dest.at[first + index],
                    send_sem=y_send.at[distance - 1, kind, index],
                    recv_sem=y_recv.at[distance - 1, kind, index],
                    device_id={"harm": target_at(distance)},
                    device_id_type=MESH,
                )
                copy.start()
                y_copies.append((distance, kind, index, copy))

    def rim_copies(distance):
        group = group_at(distance, True)
        return [
            pltpu.make_async_remote_copy(
                src_ref=stage.at[distance, side],
                dst_ref=rims.at[group, 1 - side],
                send_sem=z_send.at[distance, side],
                recv_sem=z_recv.at[distance, side],
                device_id={"tile": (below, above)[side]},
                device_id_type=MESH,
            )
            for side in range(2)
        ]

    started = []
    rim_pending = {}

    def send_rims(distance):
        rim_pending[distance] = rim_copies(distance)
        for copy in rim_pending[distance]:
            copy.start()

    def relay_copy(distance, kind, index):
        at = group_at(distance, True) * local + index
        dest = (pbuf, bbuf)[kind]
        source = dest.at[at] if distance else (p_hbm, b_hbm)[kind].at[index]
        return pltpu.make_async_remote_copy(
            src_ref=source,
            dst_ref=dest.at[at],
            send_sem=chip_send.at[distance, kind, index],
            recv_sem=chip_recv.at[distance, kind, index],
            device_id={"harm": partner},
            device_id_type=MESH,
        )

    relays = {}

    def relay(distance, kind, index):
        relays[distance, kind, index] = relay_copy(distance, kind, index)
        relays[distance, kind, index].start()

    def relay_rims(distance):
        group = group_at(distance, True)
        relays[distance] = pltpu.make_async_remote_copy(
            src_ref=rims.at[group],
            dst_ref=rims.at[group],
            send_sem=rim_send.at[distance],
            recv_sem=rim_recv.at[distance],
            device_id={"harm": partner},
            device_id_type=MESH,
        )
        relays[distance].start()

    send_rims(0)
    for kind in range(2):
        for index in range(local):
            relay(0, kind, index)

    row_at = lax.broadcasted_iota(jnp.int32, (rows, width), 0)

    def neighbours(value, low, high):
        east = jnp.where(row_at == rows - 1, high, pltpu.roll(value, rows - 1, 0))
        west = jnp.where(row_at == 0, low, pltpu.roll(value, 1, 0))
        return east, west

    def slope_y(group):
        def one(index, _):
            at = group * local + index
            for part in range(2):
                for field in range(fields):
                    value = pbuf[at, part, field]
                    gy[at, part, field] = 0.5 * (
                        pltpu.roll(value, width - 1, 1) - pltpu.roll(value, 1, 1)
                    )
            return 0

        lax.fori_loop(0, local, one, 0)

    def slope_x(group):
        for index in range(local):
            at = group * local + index
            for part in range(2):
                for field in range(fields):
                    row = (index * 2 + part) * fields + field
                    east, west = neighbours(
                        pbuf[at, part, field],
                        rims[group, 0, row : row + 1, :],
                        rims[group, 1, row : row + 1, :],
                    )
                    gx[at, part, field] = 0.5 * (east - west)

    def own_terms():
        center = vbuf[...]
        east, west = neighbours(
            center,
            rims[me, 0, rim_rows : rim_rows + 1, :],
            rims[me, 1, rim_rows : rim_rows + 1, :],
        )
        east_face = 0.5 * (center + east)
        west_face = 0.5 * (center + west)
        north_face = 0.5 * (center + pltpu.roll(center, width - 1, 1))
        south_face = 0.5 * (center + pltpu.roll(center, 1, 1))
        for index in range(local):
            at = first + index
            signed = jnp.where(at < total // 2, at, at - total)
            frequency = omega_base * signed.astype(jnp.float32)
            for part in range(2):
                for field in range(fields):
                    row = (index * 2 + part) * fields + field
                    value = pbuf[at, part, field]
                    up, down = neighbours(
                        value,
                        rims[me, 0, row : row + 1, :],
                        rims[me, 1, row : row + 1, :],
                    )
                    damping = (
                        east_face * (up - value)
                        - west_face * (value - down)
                        + north_face * (pltpu.roll(value, width - 1, 1) - value)
                        - south_face * (value - pltpu.roll(value, 1, 1))
                    )
                    turned = pbuf[at, 1 - part, field] * frequency
                    result = turned - damping if part else -turned - damping
                    if field == 0 or field == 4:
                        result = result + (gx[at, part, 1] + gy[at, part, 2])
                    elif field == 1:
                        result = result + gx[at, part, 4]
                    elif field == 2:
                        result = result + gy[at, part, 4]
                    out[index, part, field] = result

    def couple(at):
        def strip(step, _):
            span = pl.ds(pl.multiple_of(step * 8, 8), 8)
            base = [[bbuf[at, part, which, span, :] for part in range(2)] for which in range(3)]
            for index in range(local):
                source = (first + index + total - at) % total
                for field in range(fields):
                    real = out[index, 0, field, span, :]
                    imag = out[index, 1, field, span, :]
                    for which, values in ((0, gx), (1, gy), (2, pbuf)):
                        a_real, a_imag = base[which]
                        q_real = values[source, 0, field, span, :]
                        q_imag = values[source, 1, field, span, :]
                        real = real + a_real * q_real - a_imag * q_imag
                        imag = imag + a_real * q_imag + a_imag * q_real
                    out[index, 0, field, span, :] = real
                    out[index, 1, field, span, :] = imag
            return 0

        lax.fori_loop(0, rows // 8, strip, 0)

    def wait_y(distance, kind, index):
        for other, what, which, copy in y_copies:
            if (other, what, which) == (distance, kind, index):
                copy.wait_recv()

    slope_y(me)
    for copy in rim_pending[0]:
        copy.wait_recv()
    relay_rims(0)
    slope_x(me)
    own_terms()
    for index in range(local):
        relays[0, 0, index].wait_recv()
    slope_y(partner)
    relays[0].wait_recv()
    slope_x(partner)

    for distance in range(1, chips):
        for index in range(local):
            wait_y(distance, 0, index)
            relay(distance, 0, index)
        pack(distance)
        send_rims(distance)
    for distance in range(1, chips):
        slope_y(group_at(distance, True))
        for index in range(local):
            relays[distance, 0, index].wait_recv()
        slope_y(group_at(distance, False))
    for distance in range(1, chips):
        for index in range(local - 1):
            wait_y(distance, 1, index)
            relay(distance, 1, index)
    for distance in range(1, chips):
        for copy in rim_pending[distance]:
            copy.wait_recv()
        relay_rims(distance)
        slope_x(group_at(distance, True))
    for distance in range(1, chips):
        relays[distance].wait_recv()
        slope_x(group_at(distance, False))

    copy_b.wait()
    for index in range(local):
        couple(first + index)
    for index in range(local):
        relays[0, 1, index].wait_recv()
        couple(partner * local + index)
    for distance in range(1, chips):
        wait_y(distance, 1, local - 1)
        relay(distance, 1, local - 1)
    for distance in range(1, chips):
        for index in range(local):
            couple(group_at(distance, True) * local + index)
    for distance in range(1, chips):
        for index in range(local):
            relays[distance, 1, index].wait_recv()
            couple(group_at(distance, False) * local + index)

    for _, _, _, copy in y_copies:
        copy.wait_send()
    for copies in rim_pending.values():
        for copy in copies:
            copy.wait_send()
    for copy in relays.values():
        copy.wait_send()


def shards(perturbation, base_flow, viscosity):
    local, parts, fields, rows, width = perturbation.shape
    groups = lax.axis_size("harm")
    tiles = lax.axis_size("tile")
    chips = groups // 2
    cols = width // groups
    if (
        chips == 2
        and tiles > 2
        and rows == 16
        and 2 * cols == 128
        and 2 * local * parts * fields <= cols
    ):
        return quarters(perturbation, base_flow, viscosity)
    total = local * groups
    rim = -(-(local * parts * fields + 1) // 8) * 8
    kinds = base_flow.shape[2]
    dma = pltpu.SemaphoreType.DMA
    f32 = jnp.float32
    return pl.pallas_call(
        functools.partial(kernel, groups, tiles),
        out_shape=jax.ShapeDtypeStruct(perturbation.shape, f32),
        in_specs=[pl.BlockSpec(memory_space=pl.ANY)] * 3,
        out_specs=pl.BlockSpec(memory_space=pltpu.VMEM),
        scratch_shapes=[
            pltpu.VMEM((total, 2, fields, rows, width), f32),
            pltpu.VMEM((total, 2, kinds, rows, width), f32),
            pltpu.VMEM((rows, width), f32),
            pltpu.VMEM((chips, 2, rim, width), f32),
            pltpu.VMEM((groups, 2, rim, width), f32),
            pltpu.VMEM((total, 2, fields, rows, width), f32),
            pltpu.VMEM((total, 2, fields, rows, width), f32),
            dma((3,)),
            dma((chips - 1, 2, local)),
            dma((chips - 1, 2, local)),
            dma((chips, 2, local)),
            dma((chips, 2, local)),
            dma((chips, 2)),
            dma((chips, 2)),
            dma((chips,)),
            dma((chips,)),
        ],
        compiler_params=pltpu.CompilerParams(collective_id=0, has_side_effects=True),
    )(perturbation, base_flow, viscosity)


def quarter_kernel(
    groups,
    tiles,
    p_hbm,
    b_hbm,
    v_hbm,
    own,
    back,
    full,
    base,
    vbuf,
    stage,
    zrims,
    rim_out,
    rim_in,
    rim_rows,
    late_in,
    fix_out,
    fix_in,
    b_out,
    b_in,
    h_out,
    h_in,
    p_out,
    p_in,
    gx,
    gy,
    sent,
    load_sem,
    g_send,
    g_recv,
    z_send,
    z_recv,
    ready_up,
    ready_down,
):
    local, _, fields, rows, width = p_hbm.shape
    kinds = b_hbm.shape[2]
    harmonics = local * groups
    half = rows // 2
    cols = width // groups
    lanes = 2 * cols
    pairs = 2 * local
    values = pairs * fields
    deep = values // 2
    me = lax.axis_index("harm")
    chip, core = me // 2, me % 2
    place = lax.axis_index("tile")
    partner = chip * 2 + (1 - core)
    across = (1 - chip) * 2 + core
    corner = (1 - chip) * 2 + (1 - core)
    peers = (across, corner, partner)
    everyone = (me, partner, across, corner)
    above, below = (place + 1) % tiles, (place + tiles - 1) % tiles
    inner, lowest, highest = place < tiles - 1, place == 0, place == tiles - 1

    loads = [
        pltpu.make_async_copy(source, dest, load_sem.at[at])
        for at, (source, dest) in enumerate(((b_hbm, base), (p_hbm, full), (v_hbm, vbuf)))
    ]
    for copy in loads:
        copy.start()

    def tell(semaphore, where):
        for group in everyone:
            pl.semaphore_signal(
                semaphore, inc=1, device_id={"harm": group, "tile": where}, device_id_type=MESH
            )

    barrier = pltpu.get_barrier_semaphore()
    for group in peers:
        pl.semaphore_signal(barrier, inc=1, device_id={"harm": group}, device_id_type=MESH)

    @pl.when(inner)
    def _():
        tell(barrier, above)

    @pl.when(lowest)
    def _():
        tell(barrier, below)

    lane = lax.broadcasted_iota(jnp.int32, (half, lanes), 1)
    sub = lax.broadcasted_iota(jnp.int32, (half, lanes), 0)
    left = lane < cols
    column = lane % cols

    def turn(value, shift):
        return pltpu.roll(value, shift % lanes, 1)

    def packed(ref, at):
        blocks = []
        for tile in range(width // lanes):
            span = slice(tile * lanes, (tile + 1) * lanes)
            top = ref[(*at, slice(0, half), span)]
            bottom = ref[(*at, slice(half, rows), span)]
            blocks.append(jnp.where(left, top, turn(bottom, cols)))
            blocks.append(jnp.where(left, turn(top, cols), bottom))
        return blocks

    loads[0].wait()
    for index in range(local):
        for part in range(2):
            for which in range(kinds):
                for group, block in enumerate(packed(base, (index, part, which))):
                    b_out[group, (index * 2 + part) * kinds + which] = block

    low_lane = lax.broadcasted_iota(jnp.int32, (deep, lanes), 1) < cols

    def prepare_rims():
        loads[1].wait()
        loads[2].wait()
        for field in range(fields):
            for index in range(local):
                for part in range(2):
                    at = index * fields + field
                    stage[0, part, at : at + 1, :] = full[index, part, field, 0:1, :]
                    stage[1, part, at : at + 1, :] = full[index, part, field, rows - 1 : rows, :]
        stage[0, 0, deep : deep + 1, :] = vbuf[0:1, :]
        stage[1, 0, deep : deep + 1, :] = vbuf[rows - 1 : rows, :]
        for side in range(2):
            for group in range(groups):
                tile, odd = group * cols // lanes, group * cols % lanes
                span = slice(tile * lanes, (tile + 1) * lanes)
                first = stage[side, 0, 0:deep, span]
                second = stage[side, 1, 0:deep, span]
                if side == 0:
                    first, second = second, first
                if odd:
                    first = turn(first, cols)
                else:
                    second = turn(second, cols)
                rim_out[side, group] = jnp.where(low_lane, first, second)

    def pack_fields():
        halos = [jnp.zeros((half, lanes), jnp.float32) for _ in range(groups)]
        for field in range(fields):
            for index in range(local):
                for part in range(2):
                    number = field * pairs + index * 2 + part
                    blocks = packed(full, (index, part, field))
                    for group, block in enumerate(blocks):
                        p_out[field, group, index * 2 + part] = block
                        low = turn(blocks[(group - 1) % groups], 2 * number + 2 - cols)
                        high = turn(blocks[(group + 1) % groups], 2 * number + cols)
                        halos[group] = jnp.where(
                            column == 2 * number + 1,
                            low,
                            jnp.where(column == 2 * number, high, halos[group]),
                        )
        for group in range(groups):
            h_out[group] = halos[group]

    def remote(source, dest, send, recv, at, device):
        return pltpu.make_async_remote_copy(
            src_ref=source,
            dst_ref=dest,
            send_sem=send.at[at],
            recv_sem=recv.at[at],
            device_id=device,
            device_id_type=MESH,
        )

    def base_copy(slot):
        return remote(
            b_out.at[peers[slot]], b_in.at[me], g_send, g_recv, (0, slot), {"harm": peers[slot]}
        )

    def halo_copy(slot):
        return remote(
            h_out.at[peers[slot]],
            h_in.at[me],
            g_send,
            g_recv,
            (1 + 2 * fields, slot),
            {"harm": peers[slot]},
        )

    def field_copy(field, slot):
        return remote(
            p_out.at[field, peers[slot]],
            p_in.at[field, me],
            g_send,
            g_recv,
            (1 + field, slot),
            {"harm": peers[slot]},
        )

    def back_copy(field, slot):
        return remote(
            sent.at[field, peers[slot]],
            back.at[field, me],
            g_send,
            g_recv,
            (1 + fields + field, slot),
            {"harm": peers[slot]},
        )

    def rim_copy(side, slot):
        where = (below, above)[side]
        if slot == len(everyone):
            return remote(
                stage.at[side],
                zrims.at[side],
                z_send,
                z_recv,
                (side, slot),
                {"harm": me, "tile": where},
            )
        return remote(
            rim_out.at[side, everyone[slot]],
            rim_in.at[side, me],
            z_send,
            z_recv,
            (side, slot),
            {"harm": everyone[slot], "tile": where},
        )

    def late_copy(side, slot):
        return remote(
            rim_out.at[side, everyone[slot]],
            late_in.at[me],
            z_send,
            z_recv,
            (2, slot),
            {"harm": everyone[slot], "tile": (below, above)[side]},
        )

    def fix_copy(slot):
        return remote(
            fix_out.at[peers[slot]],
            fix_in.at[me],
            g_send,
            g_recv,
            (2 + 2 * fields, slot),
            {"harm": peers[slot]},
        )

    def send_rims(side):
        for slot in range(len(everyone) + 1):
            rim_copy(side, slot).start()

    def send_late(side):
        for slot in range(len(everyone)):
            late_copy(side, slot).start()
        rim_copy(side, len(everyone)).start()

    pl.semaphore_wait(
        barrier,
        len(peers)
        + groups * (place > 0).astype(jnp.int32)
        + groups * highest.astype(jnp.int32),
    )

    @pl.when(place > 0)
    def _():
        tell(ready_up, below)
        prepare_rims()
        send_rims(0)

    @pl.when(highest)
    def _():
        tell(ready_down, above)
        send_late(1)

    for slot in range(len(peers)):
        base_copy(slot).start()

    @pl.when(lowest)
    def _():
        prepare_rims()

    pack_fields()
    for slot in range(len(peers)):
        halo_copy(slot).start()

    def send_field(field):
        for slot in range(len(peers)):
            field_copy(field, slot).start()

    early = min(4, fields)
    for field in range(early):
        send_field(field)

    @pl.when(inner)
    def _():
        pl.semaphore_wait(ready_up, groups)
        send_rims(1)

    @pl.when(lowest)
    def _():
        pl.semaphore_wait(ready_down, groups)
        send_late(0)

    for field in range(early, fields):
        send_field(field)

    b_in[me] = b_out[me]
    h_in[me] = h_out[me]
    for field in range(fields):
        p_in[field, me] = p_out[field, me]

    def take_rims(slot):
        group = everyone[slot]

        @pl.when(inner)
        def _():
            rim_copy(0, slot).wait_recv()

        @pl.when(highest)
        def _():
            rim_in[0, group] = jnp.zeros((deep, lanes), jnp.float32)

        @pl.when(place > 0)
        def _():
            rim_copy(1, slot).wait_recv()

        @pl.when(lowest)
        def _():
            rim_in[1, group] = jnp.zeros((deep, lanes), jnp.float32)

        above_rows, below_rows = rim_in[0, group], rim_in[1, group]
        rim_rows[group, 0] = jnp.where(low_lane, below_rows, above_rows)
        rim_rows[group, 1] = turn(jnp.where(low_lane, above_rows, below_rows), cols)

    for slot in range(len(peers)):
        base_copy(slot).wait_recv()
        halo_copy(slot).wait_recv()
    for slot in range(len(everyone)):
        take_rims(slot)

    def slopes(field, group):
        for pair in range(pairs):
            number = field * pairs + pair
            value = p_in[field, group, pair]
            edge = pltpu.roll(h_in[group], lanes - 1 - 2 * number, 1)
            north = jnp.where(column == cols - 1, edge, turn(value, -1))
            south = jnp.where(column == 0, edge, turn(value, 1))
            gy[group, pair] = 0.5 * (north - south)
            swapped = turn(value, cols)
            rim = rim_rows[group, pair % 2, pl.ds(pair // 2 * fields + field, 1), :]
            high = jnp.where(left, swapped, rim)
            low = jnp.where(left, rim, swapped)
            east = pltpu.roll(jnp.where(sub == 0, high, value), half - 1, 0)
            west = pltpu.roll(jnp.where(sub == half - 1, low, value), 1, 0)
            gx[group, pair] = 0.5 * (east - west)

    def convolve(field, target, index, sources, sums):
        real, imag = sums
        for group in sources:
            for at in range(local):
                shift = (target - group) * local + index - at
                shift = (shift + harmonics) % harmonics
                owner, first = shift // local, shift % local * 2 * kinds
                for which, values_of in enumerate((gx, gy, p_in.at[field])):
                    a_real = b_in[owner, first + which]
                    a_imag = b_in[owner, first + kinds + which]
                    q_real, q_imag = values_of[group, 2 * at], values_of[group, 2 * at + 1]
                    real = real + a_real * q_real - a_imag * q_imag
                    imag = imag + a_real * q_imag + a_imag * q_real
        return real, imag

    order = (*peers, me)

    at_end = lowest | highest

    def fix():
        for slot in range(len(everyone)):
            late_copy(0, slot).wait_recv()
        edge = (1 - lowest.astype(jnp.int32)) * (half - 1)
        scale = jnp.where(lowest, -0.5, 0.5)
        low_row = lax.broadcasted_iota(jnp.int32, (1, lanes), 1) < cols
        here = low_row == lowest

        def both(row):
            return scale * jnp.where(here, row, turn(row, cols))

        def straight(rows_here):
            return jnp.where(lowest, rows_here, turn(rows_here, cols))

        late = [straight(late_in[group]) for group in everyone]
        crossed = [turn(rows_here, cols) for rows_here in late]
        for target in everyone:
            for index in range(local):
                total = jnp.zeros((fields, lanes), jnp.float32)
                for number, group in enumerate(everyone):
                    for at in range(local):
                        shift = (target - group) * local + index - at
                        shift = (shift + harmonics) % harmonics
                        owner, first = shift // local, shift % local * 2 * kinds
                        real = both(b_in[owner, first, pl.ds(edge, 1), :])
                        imag = both(b_in[owner, first + kinds, pl.ds(edge, 1), :])
                        span = slice(at * fields, (at + 1) * fields)
                        total = total + real * late[number][span]
                        total = total + jnp.where(low_row, -imag, imag) * crossed[number][span]
                fix_out[target, index * fields : (index + 1) * fields, :] = total
        fix_in[me] = fix_out[me]
        for slot in range(len(peers)):
            fix_copy(slot).start()

    def one_field(field, _):
        @pl.when(at_end & (field == min(3, fields - 1)))
        def _():
            fix()

        field_copy(field, 2).wait_recv()
        slopes(field, me)
        slopes(field, partner)
        zero = jnp.zeros((half, lanes), jnp.float32)
        sums = [
            [convolve(field, target, index, (me, partner), (zero, zero)) for index in range(local)]
            for target in order
        ]
        field_copy(field, 0).wait_recv()
        slopes(field, across)
        field_copy(field, 1).wait_recv()
        slopes(field, corner)
        for slot, target in enumerate(order):
            for index in range(local):
                real, imag = convolve(field, target, index, (across, corner), sums[slot][index])
                if slot < len(peers):
                    sent[field, target, 2 * index] = real
                    sent[field, target, 2 * index + 1] = imag
                else:
                    back[field, me, 2 * index] = real
                    back[field, me, 2 * index + 1] = imag
            if slot < len(peers):
                back_copy(field, slot).start()
        return 0

    lax.fori_loop(0, fields, one_field, 0)

    for side in range(2):
        rim_copy(side, len(everyone)).wait_recv()

    row_at = lax.broadcasted_iota(jnp.int32, (rows, width), 0)

    def neighbours(value, number, at):
        high, low = zrims[0, number, at : at + 1, :], zrims[1, number, at : at + 1, :]
        east = jnp.where(row_at == rows - 1, high, pltpu.roll(value, rows - 1, 0))
        west = jnp.where(row_at == 0, low, pltpu.roll(value, 1, 0))
        return east, west

    def north_of(value):
        return pltpu.roll(value, width - 1, 1)

    def south_of(value):
        return pltpu.roll(value, 1, 1)

    center = vbuf[...]
    east, west = neighbours(center, 0, deep)
    east_face = 0.5 * (center + east)
    west_face = 0.5 * (center + west)
    north_face = 0.5 * (center + north_of(center))
    south_face = 0.5 * (center + south_of(center))
    for index in range(local):
        at = me * local + index
        signed = jnp.where(at < harmonics // 2, at, at - harmonics)
        frequency = omega_base * signed.astype(jnp.float32)
        for part in range(2):

            def sides(field):
                return neighbours(full[index, part, field], part, index * fields + field)

            def along_x(field):
                up, down = sides(field)
                return 0.5 * (up - down)

            def along_y(field):
                value = full[index, part, field]
                return 0.5 * (north_of(value) - south_of(value))

            dilation = along_x(1) + along_y(2)
            sound = {0: dilation, 4: dilation, 1: along_x(4), 2: along_y(4)}
            for field in range(fields):
                value = full[index, part, field]
                up, down = sides(field)
                damping = (
                    east_face * (up - value)
                    - west_face * (value - down)
                    + north_face * (north_of(value) - value)
                    - south_face * (value - south_of(value))
                )
                turned = full[index, 1 - part, field] * frequency
                result = turned if part else -turned
                if field in sound:
                    result = result + sound[field]
                own[index, part, field] = result - damping

    def add_fixes(edge):
        for slot in range(len(peers)):
            fix_copy(slot).wait_recv()
        for tile in range(width // lanes):
            span = slice(tile * lanes, (tile + 1) * lanes)
            first, second = fix_in[2 * tile], fix_in[2 * tile + 1]
            both = (
                jnp.where(low_lane, first, turn(second, cols)),
                jnp.where(low_lane, turn(first, cols), second),
            )
            for index in range(local):
                for part in range(2):
                    for field in range(fields):
                        at = index * fields + field
                        own[index, part, field, edge : edge + 1, span] += both[part][at : at + 1]

    for field in range(fields):
        if field == fields - 1:
            pl.when(lowest)(lambda: add_fixes(0))
            pl.when(highest)(lambda: add_fixes(rows - 1))
        for slot in range(len(peers)):
            back_copy(field, slot).wait_recv()
        if field < fields - 1:
            join(field, own, back, own, field)

    for slot in range(len(peers)):
        base_copy(slot).wait_send()
        halo_copy(slot).wait_send()
        for field in range(fields):
            field_copy(field, slot).wait_send()
            back_copy(field, slot).wait_send()
    def sent_rims(side):
        for slot in range(len(everyone)):
            rim_copy(side, slot).wait_send()

    pl.when(inner)(lambda: sent_rims(1))
    pl.when(place > 0)(lambda: sent_rims(0))

    @pl.when(at_end)
    def _():
        for slot in range(len(everyone)):
            late_copy(0, slot).wait_send()
        for slot in range(len(peers)):
            fix_copy(slot).wait_send()

    for side in range(2):
        rim_copy(side, len(everyone)).wait_send()


def join(field, own, back, out, at):
    local, _, _, rows, width = own.shape
    half, lanes = back.shape[-2:]
    left = lax.broadcasted_iota(jnp.int32, (half, lanes), 1) < lanes // 2
    for index in range(local):
        for part in range(2):
            pair = index * 2 + part
            for tile in range(width // lanes):
                span = slice(tile * lanes, (tile + 1) * lanes)
                first, second = back[field, 2 * tile, pair], back[field, 2 * tile + 1, pair]
                top = jnp.where(left, first, pltpu.roll(second, lanes // 2, 1))
                bottom = jnp.where(left, pltpu.roll(first, lanes // 2, 1), second)
                out[index, part, at, 0:half, span] = own[index, part, field, 0:half, span] + top
                out[index, part, at, half:rows, span] = (
                    own[index, part, field, half:rows, span] + bottom
                )


def join_kernel(own, back, out_hbm, out, sem):
    last = own.shape[2] - 1
    copies = [
        pltpu.make_async_copy(own.at[:, :, 0:last], out_hbm.at[:, :, 0:last], sem.at[0]),
        pltpu.make_async_copy(out, out_hbm.at[:, :, last : last + 1], sem.at[1]),
    ]
    copies[0].start()
    join(last, own, back, out, 0)
    copies[1].start()
    for copy in copies:
        copy.wait()


def quarters(perturbation, base_flow, viscosity):
    local, parts, fields, rows, width = perturbation.shape
    groups = lax.axis_size("harm")
    tiles = lax.axis_size("tile")
    kinds = base_flow.shape[2]
    half, lanes = rows // 2, 2 * (width // groups)
    pairs = 2 * local
    values = pairs * fields
    deep = values // 2
    dma = pltpu.SemaphoreType.DMA
    f32 = jnp.float32
    limit = 24 * 1024 * 1024
    whole = (local, parts, fields, rows, width)
    blocks = (fields, groups, pairs, half, lanes)
    inputs = [
        pltpu.with_memory_space_constraint(array, pltpu.HBM)
        for array in (perturbation, base_flow, viscosity)
    ]
    own, back = pl.pallas_call(
        functools.partial(quarter_kernel, groups, tiles),
        out_shape=(pltpu.VMEM(whole, f32), pltpu.VMEM(blocks, f32)),
        in_specs=[pl.BlockSpec(memory_space=pltpu.HBM)] * 3,
        out_specs=[pl.BlockSpec(memory_space=pltpu.VMEM)] * 2,
        scratch_shapes=[
            pltpu.VMEM(whole, f32),
            pltpu.VMEM((local, parts, kinds, rows, width), f32),
            pltpu.VMEM((rows, width), f32),
            pltpu.VMEM((2, 2, deep + 1, width), f32),
            pltpu.VMEM((2, 2, deep + 1, width), f32),
            pltpu.VMEM((2, groups, deep, lanes), f32),
            pltpu.VMEM((2, groups, deep, lanes), f32),
            pltpu.VMEM((groups, 2, deep, lanes), f32),
            pltpu.VMEM((groups, deep, lanes), f32),
            pltpu.VMEM((groups, deep, lanes), f32),
            pltpu.VMEM((groups, deep, lanes), f32),
            pltpu.VMEM((groups, kinds * pairs, half, lanes), f32),
            pltpu.VMEM((groups, kinds * pairs, half, lanes), f32),
            pltpu.VMEM((groups, half, lanes), f32),
            pltpu.VMEM((groups, half, lanes), f32),
            pltpu.VMEM(blocks, f32),
            pltpu.VMEM(blocks, f32),
            pltpu.VMEM((groups, pairs, half, lanes), f32),
            pltpu.VMEM((groups, pairs, half, lanes), f32),
            pltpu.VMEM(blocks, f32),
            dma((3,)),
            dma((3 + 2 * fields, 3)),
            dma((3 + 2 * fields, 3)),
            dma((3, 5)),
            dma((3, 5)),
            pltpu.SemaphoreType.REGULAR,
            pltpu.SemaphoreType.REGULAR,
        ],
        compiler_params=pltpu.CompilerParams(
            collective_id=0, has_side_effects=True, vmem_limit_bytes=limit
        ),
    )(*inputs)
    own = pltpu.with_memory_space_constraint(own, pltpu.VMEM)
    back = pltpu.with_memory_space_constraint(back, pltpu.VMEM)
    return pl.pallas_call(
        join_kernel,
        out_shape=jax.ShapeDtypeStruct(whole, f32),
        in_specs=[pl.BlockSpec(memory_space=pltpu.VMEM)] * 2,
        out_specs=pl.BlockSpec(memory_space=pl.ANY),
        scratch_shapes=[pltpu.VMEM((local, parts, 1, rows, width), f32), dma((2,))],
        compiler_params=pltpu.CompilerParams(vmem_limit_bytes=limit),
    )(own, back)


def solution(mesh):
    placed = (
        P("harm", None, None, ("parts", "tile"), None),
        P("harm", None, None, ("parts", "tile"), None),
        P(("parts", "tile"), None),
    )
    return jax.shard_map(
        shards,
        mesh=mesh,
        in_specs=placed,
        out_specs=P("harm", None, None, ("parts", "tile"), None),
        check_vma=False,
    )
```

```python
import functools

import jax
import jax.numpy as jnp
from jax import lax
from jax.experimental import pallas as pl
from jax.experimental.pallas import tpu as pltpu
from jax.sharding import PartitionSpec as P

omega_base = 0.25
MESH = pl.DeviceIdType.MESH


def kernel(
    groups,
    tiles,
    p_hbm,
    b_hbm,
    v_hbm,
    out,
    pbuf,
    bbuf,
    vbuf,
    stage,
    rims,
    gx,
    gy,
    local_sem,
    y_send,
    y_recv,
    chip_send,
    chip_recv,
    z_send,
    z_recv,
    rim_send,
    rim_recv,
):
    local, _, fields, rows, width = p_hbm.shape
    total = pbuf.shape[0]
    cores = 2
    chips = groups // cores
    rim_rows = local * 2 * fields
    me = lax.axis_index("harm")
    chip, core = me // cores, me % cores
    place = lax.axis_index("tile")
    partner = chip * cores + (1 - core)
    above, below = (place + 1) % tiles, (place + tiles - 1) % tiles

    def group_at(distance, own_core):
        at = (chip + chips - distance) % chips
        return at * cores + (core if own_core else 1 - core)

    def target_at(distance):
        return (chip + distance) % chips * cores + core

    first = me * local

    copy_p = pltpu.make_async_copy(p_hbm, pbuf.at[pl.ds(first, local)], local_sem.at[0])
    copy_b = pltpu.make_async_copy(b_hbm, bbuf.at[pl.ds(first, local)], local_sem.at[1])
    copy_v = pltpu.make_async_copy(v_hbm, vbuf, local_sem.at[2])
    copy_p.start()
    copy_v.start()
    copy_b.start()

    barrier = pltpu.get_barrier_semaphore()
    for distance in range(1, chips):
        pl.semaphore_signal(
            barrier, inc=1, device_id={"harm": target_at(distance)}, device_id_type=MESH
        )
    pl.semaphore_signal(barrier, inc=1, device_id={"harm": partner}, device_id_type=MESH)
    pl.semaphore_signal(barrier, inc=1, device_id={"tile": above}, device_id_type=MESH)
    pl.semaphore_signal(barrier, inc=1, device_id={"tile": below}, device_id_type=MESH)

    def pack(distance):
        start = group_at(distance, True) * local
        for index in range(local):
            for part in range(2):
                for field in range(fields):
                    row = (index * 2 + part) * fields + field
                    stage[distance, 0, row : row + 1, :] = pbuf[start + index, part, field, 0:1, :]
                    stage[distance, 1, row : row + 1, :] = pbuf[
                        start + index, part, field, rows - 1 : rows, :
                    ]

    copy_p.wait()
    copy_v.wait()
    pack(0)
    stage[0, 0, rim_rows : rim_rows + 1, :] = vbuf[0:1, :]
    stage[0, 1, rim_rows : rim_rows + 1, :] = vbuf[rows - 1 : rows, :]

    pl.semaphore_wait(barrier, chips + 2)

    y_copies = []
    for kind in range(2):
        source, dest = ((p_hbm, pbuf), (b_hbm, bbuf))[kind]
        for index in range(local):
            for distance in range(1, chips):
                copy = pltpu.make_async_remote_copy(
                    src_ref=source.at[index],
                    dst_ref=dest.at[first + index],
                    send_sem=y_send.at[distance - 1, kind, index],
                    recv_sem=y_recv.at[distance - 1, kind, index],
                    device_id={"harm": target_at(distance)},
                    device_id_type=MESH,
                )
                copy.start()
                y_copies.append((distance, kind, index, copy))

    def rim_copies(distance):
        group = group_at(distance, True)
        return [
            pltpu.make_async_remote_copy(
                src_ref=stage.at[distance, side],
                dst_ref=rims.at[group, 1 - side],
                send_sem=z_send.at[distance, side],
                recv_sem=z_recv.at[distance, side],
                device_id={"tile": (below, above)[side]},
                device_id_type=MESH,
            )
            for side in range(2)
        ]

    started = []
    rim_pending = {}

    def send_rims(distance):
        rim_pending[distance] = rim_copies(distance)
        for copy in rim_pending[distance]:
            copy.start()

    def relay_copy(distance, kind, index):
        at = group_at(distance, True) * local + index
        dest = (pbuf, bbuf)[kind]
        source = dest.at[at] if distance else (p_hbm, b_hbm)[kind].at[index]
        return pltpu.make_async_remote_copy(
            src_ref=source,
            dst_ref=dest.at[at],
            send_sem=chip_send.at[distance, kind, index],
            recv_sem=chip_recv.at[distance, kind, index],
            device_id={"harm": partner},
            device_id_type=MESH,
        )

    relays = {}

    def relay(distance, kind, index):
        relays[distance, kind, index] = relay_copy(distance, kind, index)
        relays[distance, kind, index].start()

    def relay_rims(distance):
        group = group_at(distance, True)
        relays[distance] = pltpu.make_async_remote_copy(
            src_ref=rims.at[group],
            dst_ref=rims.at[group],
            send_sem=rim_send.at[distance],
            recv_sem=rim_recv.at[distance],
            device_id={"harm": partner},
            device_id_type=MESH,
        )
        relays[distance].start()

    send_rims(0)
    for kind in range(2):
        for index in range(local):
            relay(0, kind, index)

    row_at = lax.broadcasted_iota(jnp.int32, (rows, width), 0)

    def neighbours(value, low, high):
        east = jnp.where(row_at == rows - 1, high, pltpu.roll(value, rows - 1, 0))
        west = jnp.where(row_at == 0, low, pltpu.roll(value, 1, 0))
        return east, west

    def slope_y(group):
        def one(index, _):
            at = group * local + index
            for part in range(2):
                for field in range(fields):
                    value = pbuf[at, part, field]
                    gy[at, part, field] = 0.5 * (
                        pltpu.roll(value, width - 1, 1) - pltpu.roll(value, 1, 1)
                    )
            return 0

        lax.fori_loop(0, local, one, 0)

    def slope_x(group):
        for index in range(local):
            at = group * local + index
            for part in range(2):
                for field in range(fields):
                    row = (index * 2 + part) * fields + field
                    east, west = neighbours(
                        pbuf[at, part, field],
                        rims[group, 0, row : row + 1, :],
                        rims[group, 1, row : row + 1, :],
                    )
                    gx[at, part, field] = 0.5 * (east - west)

    def own_terms():
        center = vbuf[...]
        east, west = neighbours(
            center,
            rims[me, 0, rim_rows : rim_rows + 1, :],
            rims[me, 1, rim_rows : rim_rows + 1, :],
        )
        east_face = 0.5 * (center + east)
        west_face = 0.5 * (center + west)
        north_face = 0.5 * (center + pltpu.roll(center, width - 1, 1))
        south_face = 0.5 * (center + pltpu.roll(center, 1, 1))
        for index in range(local):
            at = first + index
            signed = jnp.where(at < total // 2, at, at - total)
            frequency = omega_base * signed.astype(jnp.float32)
            for part in range(2):
                for field in range(fields):
                    row = (index * 2 + part) * fields + field
                    value = pbuf[at, part, field]
                    up, down = neighbours(
                        value,
                        rims[me, 0, row : row + 1, :],
                        rims[me, 1, row : row + 1, :],
                    )
                    damping = (
                        east_face * (up - value)
                        - west_face * (value - down)
                        + north_face * (pltpu.roll(value, width - 1, 1) - value)
                        - south_face * (value - pltpu.roll(value, 1, 1))
                    )
                    turned = pbuf[at, 1 - part, field] * frequency
                    result = turned - damping if part else -turned - damping
                    if field == 0 or field == 4:
                        result = result + (gx[at, part, 1] + gy[at, part, 2])
                    elif field == 1:
                        result = result + gx[at, part, 4]
                    elif field == 2:
                        result = result + gy[at, part, 4]
                    out[index, part, field] = result

    def couple(at):
        def strip(step, _):
            span = pl.ds(pl.multiple_of(step * 8, 8), 8)
            base = [[bbuf[at, part, which, span, :] for part in range(2)] for which in range(3)]
            for index in range(local):
                source = (first + index + total - at) % total
                for field in range(fields):
                    real = out[index, 0, field, span, :]
                    imag = out[index, 1, field, span, :]
                    for which, values in ((0, gx), (1, gy), (2, pbuf)):
                        a_real, a_imag = base[which]
                        q_real = values[source, 0, field, span, :]
                        q_imag = values[source, 1, field, span, :]
                        real = real + a_real * q_real - a_imag * q_imag
                        imag = imag + a_real * q_imag + a_imag * q_real
                    out[index, 0, field, span, :] = real
                    out[index, 1, field, span, :] = imag
            return 0

        lax.fori_loop(0, rows // 8, strip, 0)

    def wait_y(distance, kind, index):
        for other, what, which, copy in y_copies:
            if (other, what, which) == (distance, kind, index):
                copy.wait_recv()

    slope_y(me)
    for copy in rim_pending[0]:
        copy.wait_recv()
    relay_rims(0)
    slope_x(me)
    own_terms()
    for index in range(local):
        relays[0, 0, index].wait_recv()
    slope_y(partner)
    relays[0].wait_recv()
    slope_x(partner)

    for distance in range(1, chips):
        for index in range(local):
            wait_y(distance, 0, index)
            relay(distance, 0, index)
        pack(distance)
        send_rims(distance)
    for distance in range(1, chips):
        slope_y(group_at(distance, True))
        for index in range(local):
            relays[distance, 0, index].wait_recv()
        slope_y(group_at(distance, False))
    for distance in range(1, chips):
        for index in range(local - 1):
            wait_y(distance, 1, index)
            relay(distance, 1, index)
    for distance in range(1, chips):
        for copy in rim_pending[distance]:
            copy.wait_recv()
        relay_rims(distance)
        slope_x(group_at(distance, True))
    for distance in range(1, chips):
        relays[distance].wait_recv()
        slope_x(group_at(distance, False))

    copy_b.wait()
    for index in range(local):
        couple(first + index)
    for index in range(local):
        relays[0, 1, index].wait_recv()
        couple(partner * local + index)
    for distance in range(1, chips):
        wait_y(distance, 1, local - 1)
        relay(distance, 1, local - 1)
    for distance in range(1, chips):
        for index in range(local):
            couple(group_at(distance, True) * local + index)
    for distance in range(1, chips):
        for index in range(local):
            relays[distance, 1, index].wait_recv()
            couple(group_at(distance, False) * local + index)

    for _, _, _, copy in y_copies:
        copy.wait_send()
    for copies in rim_pending.values():
        for copy in copies:
            copy.wait_send()
    for copy in relays.values():
        copy.wait_send()


def shards(perturbation, base_flow, viscosity):
    local, parts, fields, rows, width = perturbation.shape
    groups = lax.axis_size("harm")
    tiles = lax.axis_size("tile")
    chips = groups // 2
    cols = width // groups
    if (
        chips == 2
        and tiles > 2
        and rows == 16
        and 2 * cols == 128
        and 2 * local * parts * fields <= cols
    ):
        return quarters(perturbation, base_flow, viscosity)
    total = local * groups
    rim = -(-(local * parts * fields + 1) // 8) * 8
    kinds = base_flow.shape[2]
    dma = pltpu.SemaphoreType.DMA
    f32 = jnp.float32
    return pl.pallas_call(
        functools.partial(kernel, groups, tiles),
        out_shape=jax.ShapeDtypeStruct(perturbation.shape, f32),
        in_specs=[pl.BlockSpec(memory_space=pl.ANY)] * 3,
        out_specs=pl.BlockSpec(memory_space=pltpu.VMEM),
        scratch_shapes=[
            pltpu.VMEM((total, 2, fields, rows, width), f32),
            pltpu.VMEM((total, 2, kinds, rows, width), f32),
            pltpu.VMEM((rows, width), f32),
            pltpu.VMEM((chips, 2, rim, width), f32),
            pltpu.VMEM((groups, 2, rim, width), f32),
            pltpu.VMEM((total, 2, fields, rows, width), f32),
            pltpu.VMEM((total, 2, fields, rows, width), f32),
            dma((3,)),
            dma((chips - 1, 2, local)),
            dma((chips - 1, 2, local)),
            dma((chips, 2, local)),
            dma((chips, 2, local)),
            dma((chips, 2)),
            dma((chips, 2)),
            dma((chips,)),
            dma((chips,)),
        ],
        compiler_params=pltpu.CompilerParams(collective_id=0, has_side_effects=True),
    )(perturbation, base_flow, viscosity)


def quarter_kernel(
    groups,
    tiles,
    p_hbm,
    b_hbm,
    v_hbm,
    own,
    back,
    full,
    base,
    vbuf,
    stage,
    zrims,
    rim_out,
    rim_in,
    rim_rows,
    late_in,
    fix_out,
    fix_in,
    b_out,
    b_in,
    h_out,
    h_in,
    p_out,
    p_in,
    gx,
    gy,
    sent,
    load_sem,
    g_send,
    g_recv,
    z_send,
    z_recv,
    ready_up,
    ready_down,
):
    local, _, fields, rows, width = p_hbm.shape
    kinds = b_hbm.shape[2]
    harmonics = local * groups
    half = rows // 2
    cols = width // groups
    lanes = 2 * cols
    pairs = 2 * local
    values = pairs * fields
    deep = values // 2
    me = lax.axis_index("harm")
    chip, core = me // 2, me % 2
    place = lax.axis_index("tile")
    partner = chip * 2 + (1 - core)
    across = (1 - chip) * 2 + core
    corner = (1 - chip) * 2 + (1 - core)
    peers = (across, corner, partner)
    everyone = (me, partner, across, corner)
    above, below = (place + 1) % tiles, (place + tiles - 1) % tiles
    inner, lowest, highest = place < tiles - 1, place == 0, place == tiles - 1

    loads = [
        pltpu.make_async_copy(source, dest, load_sem.at[at])
        for at, (source, dest) in enumerate(((b_hbm, base), (p_hbm, full), (v_hbm, vbuf)))
    ]
    for copy in loads:
        copy.start()

    def tell(semaphore, where):
        for group in everyone:
            pl.semaphore_signal(
                semaphore, inc=1, device_id={"harm": group, "tile": where}, device_id_type=MESH
            )

    barrier = pltpu.get_barrier_semaphore()
    for group in peers:
        pl.semaphore_signal(barrier, inc=1, device_id={"harm": group}, device_id_type=MESH)

    @pl.when(inner)
    def _():
        tell(barrier, above)

    @pl.when(lowest)
    def _():
        tell(barrier, below)

    lane = lax.broadcasted_iota(jnp.int32, (half, lanes), 1)
    sub = lax.broadcasted_iota(jnp.int32, (half, lanes), 0)
    left = lane < cols
    column = lane % cols

    def turn(value, shift):
        return pltpu.roll(value, shift % lanes, 1)

    def packed(ref, at):
        blocks = []
        for tile in range(width // lanes):
            span = slice(tile * lanes, (tile + 1) * lanes)
            top = ref[(*at, slice(0, half), span)]
            bottom = ref[(*at, slice(half, rows), span)]
            blocks.append(jnp.where(left, top, turn(bottom, cols)))
            blocks.append(jnp.where(left, turn(top, cols), bottom))
        return blocks

    loads[0].wait()
    for index in range(local):
        for part in range(2):
            for which in range(kinds):
                for group, block in enumerate(packed(base, (index, part, which))):
                    b_out[group, (index * 2 + part) * kinds + which] = block

    low_lane = lax.broadcasted_iota(jnp.int32, (deep, lanes), 1) < cols

    def prepare_rims():
        loads[1].wait()
        loads[2].wait()
        for field in range(fields):
            for index in range(local):
                for part in range(2):
                    at = index * fields + field
                    stage[0, part, at : at + 1, :] = full[index, part, field, 0:1, :]
                    stage[1, part, at : at + 1, :] = full[index, part, field, rows - 1 : rows, :]
        stage[0, 0, deep : deep + 1, :] = vbuf[0:1, :]
        stage[1, 0, deep : deep + 1, :] = vbuf[rows - 1 : rows, :]
        for side in range(2):
            for group in range(groups):
                tile, odd = group * cols // lanes, group * cols % lanes
                span = slice(tile * lanes, (tile + 1) * lanes)
                first = stage[side, 0, 0:deep, span]
                second = stage[side, 1, 0:deep, span]
                if side == 0:
                    first, second = second, first
                if odd:
                    first = turn(first, cols)
                else:
                    second = turn(second, cols)
                rim_out[side, group] = jnp.where(low_lane, first, second)

    def pack_fields():
        halos = [jnp.zeros((half, lanes), jnp.float32) for _ in range(groups)]
        for field in range(fields):
            for index in range(local):
                for part in range(2):
                    number = field * pairs + index * 2 + part
                    blocks = packed(full, (index, part, field))
                    for group, block in enumerate(blocks):
                        p_out[field, group, index * 2 + part] = block
                        low = turn(blocks[(group - 1) % groups], 2 * number + 2 - cols)
                        high = turn(blocks[(group + 1) % groups], 2 * number + cols)
                        halos[group] = jnp.where(
                            column == 2 * number + 1,
                            low,
                            jnp.where(column == 2 * number, high, halos[group]),
                        )
        for group in range(groups):
            h_out[group] = halos[group]

    def remote(source, dest, send, recv, at, device):
        return pltpu.make_async_remote_copy(
            src_ref=source,
            dst_ref=dest,
            send_sem=send.at[at],
            recv_sem=recv.at[at],
            device_id=device,
            device_id_type=MESH,
        )

    def base_copy(slot):
        return remote(
            b_out.at[peers[slot]], b_in.at[me], g_send, g_recv, (0, slot), {"harm": peers[slot]}
        )

    def halo_copy(slot):
        return remote(
            h_out.at[peers[slot]],
            h_in.at[me],
            g_send,
            g_recv,
            (1 + 2 * fields, slot),
            {"harm": peers[slot]},
        )

    def field_copy(field, slot):
        return remote(
            p_out.at[field, peers[slot]],
            p_in.at[field, me],
            g_send,
            g_recv,
            (1 + field, slot),
            {"harm": peers[slot]},
        )

    def back_copy(field, slot):
        return remote(
            sent.at[field, peers[slot]],
            back.at[field, me],
            g_send,
            g_recv,
            (1 + fields + field, slot),
            {"harm": peers[slot]},
        )

    def rim_copy(side, slot):
        where = (below, above)[side]
        if slot == len(everyone):
            return remote(
                stage.at[side],
                zrims.at[side],
                z_send,
                z_recv,
                (side, slot),
                {"harm": me, "tile": where},
            )
        return remote(
            rim_out.at[side, everyone[slot]],
            rim_in.at[side, me],
            z_send,
            z_recv,
            (side, slot),
            {"harm": everyone[slot], "tile": where},
        )

    def late_copy(side, slot):
        return remote(
            rim_out.at[side, everyone[slot]],
            late_in.at[me],
            z_send,
            z_recv,
            (2, slot),
            {"harm": everyone[slot], "tile": (below, above)[side]},
        )

    def fix_copy(slot):
        return remote(
            fix_out.at[peers[slot]],
            fix_in.at[me],
            g_send,
            g_recv,
            (2 + 2 * fields, slot),
            {"harm": peers[slot]},
        )

    def send_rims(side):
        for slot in range(len(everyone) + 1):
            rim_copy(side, slot).start()

    def send_late(side):
        for slot in range(len(everyone)):
            late_copy(side, slot).start()
        rim_copy(side, len(everyone)).start()

    pl.semaphore_wait(
        barrier,
        len(peers)
        + groups * (place > 0).astype(jnp.int32)
        + groups * highest.astype(jnp.int32),
    )

    @pl.when(place > 0)
    def _():
        tell(ready_up, below)
        prepare_rims()
        send_rims(0)

    @pl.when(highest)
    def _():
        tell(ready_down, above)
        send_late(1)

    for slot in range(len(peers)):
        base_copy(slot).start()

    @pl.when(lowest)
    def _():
        prepare_rims()

    pack_fields()
    for slot in range(len(peers)):
        halo_copy(slot).start()

    def send_field(field):
        for slot in range(len(peers)):
            field_copy(field, slot).start()

    early = min(3, fields)
    for field in range(early):
        send_field(field)

    @pl.when(inner)
    def _():
        pl.semaphore_wait(ready_up, groups)
        send_rims(1)

    @pl.when(lowest)
    def _():
        pl.semaphore_wait(ready_down, groups)
        send_late(0)

    for field in range(early, fields):
        send_field(field)

    b_in[me] = b_out[me]
    h_in[me] = h_out[me]
    for field in range(fields):
        p_in[field, me] = p_out[field, me]

    def take_rims(slot):
        group = everyone[slot]

        @pl.when(inner)
        def _():
            rim_copy(0, slot).wait_recv()

        @pl.when(highest)
        def _():
            rim_in[0, group] = jnp.zeros((deep, lanes), jnp.float32)

        @pl.when(place > 0)
        def _():
            rim_copy(1, slot).wait_recv()

        @pl.when(lowest)
        def _():
            rim_in[1, group] = jnp.zeros((deep, lanes), jnp.float32)

        above_rows, below_rows = rim_in[0, group], rim_in[1, group]
        rim_rows[group, 0] = jnp.where(low_lane, below_rows, above_rows)
        rim_rows[group, 1] = turn(jnp.where(low_lane, above_rows, below_rows), cols)

    for slot in range(len(peers)):
        base_copy(slot).wait_recv()
        halo_copy(slot).wait_recv()
    for slot in range(len(everyone)):
        take_rims(slot)

    def slopes(field, group):
        for pair in range(pairs):
            number = field * pairs + pair
            value = p_in[field, group, pair]
            edge = pltpu.roll(h_in[group], lanes - 1 - 2 * number, 1)
            north = jnp.where(column == cols - 1, edge, turn(value, -1))
            south = jnp.where(column == 0, edge, turn(value, 1))
            gy[group, pair] = 0.5 * (north - south)
            swapped = turn(value, cols)
            rim = rim_rows[group, pair % 2, pl.ds(pair // 2 * fields + field, 1), :]
            high = jnp.where(left, swapped, rim)
            low = jnp.where(left, rim, swapped)
            east = pltpu.roll(jnp.where(sub == 0, high, value), half - 1, 0)
            west = pltpu.roll(jnp.where(sub == half - 1, low, value), 1, 0)
            gx[group, pair] = 0.5 * (east - west)

    def convolve(field, target, index, sources, sums):
        real, imag = sums
        for group in sources:
            for at in range(local):
                shift = (target - group) * local + index - at
                shift = (shift + harmonics) % harmonics
                owner, first = shift // local, shift % local * 2 * kinds
                for which, values_of in enumerate((gx, gy, p_in.at[field])):
                    a_real = b_in[owner, first + which]
                    a_imag = b_in[owner, first + kinds + which]
                    q_real, q_imag = values_of[group, 2 * at], values_of[group, 2 * at + 1]
                    real = real + a_real * q_real - a_imag * q_imag
                    imag = imag + a_real * q_imag + a_imag * q_real
        return real, imag

    order = (*peers, me)

    at_end = lowest | highest

    def fix():
        for slot in range(len(everyone)):
            late_copy(0, slot).wait_recv()
        edge = (1 - lowest.astype(jnp.int32)) * (half - 1)
        scale = jnp.where(lowest, -0.5, 0.5)
        low_row = lax.broadcasted_iota(jnp.int32, (1, lanes), 1) < cols
        here = low_row == lowest

        def both(row):
            return scale * jnp.where(here, row, turn(row, cols))

        def straight(rows_here):
            return jnp.where(lowest, rows_here, turn(rows_here, cols))

        late = [straight(late_in[group]) for group in everyone]
        crossed = [turn(rows_here, cols) for rows_here in late]
        for target in everyone:
            for index in range(local):
                total = jnp.zeros((fields, lanes), jnp.float32)
                for number, group in enumerate(everyone):
                    for at in range(local):
                        shift = (target - group) * local + index - at
                        shift = (shift + harmonics) % harmonics
                        owner, first = shift // local, shift % local * 2 * kinds
                        real = both(b_in[owner, first, pl.ds(edge, 1), :])
                        imag = both(b_in[owner, first + kinds, pl.ds(edge, 1), :])
                        span = slice(at * fields, (at + 1) * fields)
                        total = total + real * late[number][span]
                        total = total + jnp.where(low_row, -imag, imag) * crossed[number][span]
                fix_out[target, index * fields : (index + 1) * fields, :] = total
        fix_in[me] = fix_out[me]
        for slot in range(len(peers)):
            fix_copy(slot).start()

    def one_field(field, _):
        @pl.when(at_end & (field == fields - 1))
        def _():
            fix()

        field_copy(field, 2).wait_recv()
        slopes(field, me)
        slopes(field, partner)
        zero = jnp.zeros((half, lanes), jnp.float32)
        sums = [
            [convolve(field, target, index, (me, partner), (zero, zero)) for index in range(local)]
            for target in order
        ]
        field_copy(field, 0).wait_recv()
        slopes(field, across)
        field_copy(field, 1).wait_recv()
        slopes(field, corner)
        for slot, target in enumerate(order):
            for index in range(local):
                real, imag = convolve(field, target, index, (across, corner), sums[slot][index])
                if slot < len(peers):
                    sent[field, target, 2 * index] = real
                    sent[field, target, 2 * index + 1] = imag
                else:
                    back[field, me, 2 * index] = real
                    back[field, me, 2 * index + 1] = imag
            if slot < len(peers):
                back_copy(field, slot).start()
        return 0

    lax.fori_loop(0, fields, one_field, 0)

    for side in range(2):
        rim_copy(side, len(everyone)).wait_recv()

    row_at = lax.broadcasted_iota(jnp.int32, (rows, width), 0)

    def neighbours(value, number, at):
        high, low = zrims[0, number, at : at + 1, :], zrims[1, number, at : at + 1, :]
        east = jnp.where(row_at == rows - 1, high, pltpu.roll(value, rows - 1, 0))
        west = jnp.where(row_at == 0, low, pltpu.roll(value, 1, 0))
        return east, west

    def north_of(value):
        return pltpu.roll(value, width - 1, 1)

    def south_of(value):
        return pltpu.roll(value, 1, 1)

    center = vbuf[...]
    east, west = neighbours(center, 0, deep)
    east_face = 0.5 * (center + east)
    west_face = 0.5 * (center + west)
    north_face = 0.5 * (center + north_of(center))
    south_face = 0.5 * (center + south_of(center))
    for index in range(local):
        at = me * local + index
        signed = jnp.where(at < harmonics // 2, at, at - harmonics)
        frequency = omega_base * signed.astype(jnp.float32)
        for part in range(2):

            def sides(field):
                return neighbours(full[index, part, field], part, index * fields + field)

            def along_x(field):
                up, down = sides(field)
                return 0.5 * (up - down)

            def along_y(field):
                value = full[index, part, field]
                return 0.5 * (north_of(value) - south_of(value))

            dilation = along_x(1) + along_y(2)
            sound = {0: dilation, 4: dilation, 1: along_x(4), 2: along_y(4)}
            for field in range(fields):
                value = full[index, part, field]
                up, down = sides(field)
                damping = (
                    east_face * (up - value)
                    - west_face * (value - down)
                    + north_face * (north_of(value) - value)
                    - south_face * (value - south_of(value))
                )
                turned = full[index, 1 - part, field] * frequency
                result = turned if part else -turned
                if field in sound:
                    result = result + sound[field]
                own[index, part, field] = result - damping

    def add_fixes(edge):
        for slot in range(len(peers)):
            fix_copy(slot).wait_recv()
        for tile in range(width // lanes):
            span = slice(tile * lanes, (tile + 1) * lanes)
            first, second = fix_in[2 * tile], fix_in[2 * tile + 1]
            both = (
                jnp.where(low_lane, first, turn(second, cols)),
                jnp.where(low_lane, turn(first, cols), second),
            )
            for index in range(local):
                for part in range(2):
                    for field in range(fields):
                        at = index * fields + field
                        own[index, part, field, edge : edge + 1, span] += both[part][at : at + 1]

    for field in range(fields):
        if field == fields - 1:
            pl.when(lowest)(lambda: add_fixes(0))
            pl.when(highest)(lambda: add_fixes(rows - 1))
        for slot in range(len(peers)):
            back_copy(field, slot).wait_recv()
        if field < fields - 1:
            join(field, own, back, own, field)

    for slot in range(len(peers)):
        base_copy(slot).wait_send()
        halo_copy(slot).wait_send()
        for field in range(fields):
            field_copy(field, slot).wait_send()
            back_copy(field, slot).wait_send()
    def sent_rims(side):
        for slot in range(len(everyone)):
            rim_copy(side, slot).wait_send()

    pl.when(inner)(lambda: sent_rims(1))
    pl.when(place > 0)(lambda: sent_rims(0))

    @pl.when(at_end)
    def _():
        for slot in range(len(everyone)):
            late_copy(0, slot).wait_send()
        for slot in range(len(peers)):
            fix_copy(slot).wait_send()

    for side in range(2):
        rim_copy(side, len(everyone)).wait_send()


def join(field, own, back, out, at):
    local, _, _, rows, width = own.shape
    half, lanes = back.shape[-2:]
    left = lax.broadcasted_iota(jnp.int32, (half, lanes), 1) < lanes // 2
    for index in range(local):
        for part in range(2):
            pair = index * 2 + part
            for tile in range(width // lanes):
                span = slice(tile * lanes, (tile + 1) * lanes)
                first, second = back[field, 2 * tile, pair], back[field, 2 * tile + 1, pair]
                top = jnp.where(left, first, pltpu.roll(second, lanes // 2, 1))
                bottom = jnp.where(left, pltpu.roll(first, lanes // 2, 1), second)
                out[index, part, at, 0:half, span] = own[index, part, field, 0:half, span] + top
                out[index, part, at, half:rows, span] = (
                    own[index, part, field, half:rows, span] + bottom
                )


def join_kernel(own, back, out_hbm, out, sem):
    last = own.shape[2] - 1
    copies = [
        pltpu.make_async_copy(own.at[:, :, 0:last], out_hbm.at[:, :, 0:last], sem.at[0]),
        pltpu.make_async_copy(out, out_hbm.at[:, :, last : last + 1], sem.at[1]),
    ]
    copies[0].start()
    join(last, own, back, out, 0)
    copies[1].start()
    for copy in copies:
        copy.wait()


def quarters(perturbation, base_flow, viscosity):
    local, parts, fields, rows, width = perturbation.shape
    groups = lax.axis_size("harm")
    tiles = lax.axis_size("tile")
    kinds = base_flow.shape[2]
    half, lanes = rows // 2, 2 * (width // groups)
    pairs = 2 * local
    values = pairs * fields
    deep = values // 2
    dma = pltpu.SemaphoreType.DMA
    f32 = jnp.float32
    limit = 24 * 1024 * 1024
    whole = (local, parts, fields, rows, width)
    blocks = (fields, groups, pairs, half, lanes)
    inputs = [
        pltpu.with_memory_space_constraint(array, pltpu.HBM)
        for array in (perturbation, base_flow, viscosity)
    ]
    own, back = pl.pallas_call(
        functools.partial(quarter_kernel, groups, tiles),
        out_shape=(pltpu.VMEM(whole, f32), pltpu.VMEM(blocks, f32)),
        in_specs=[pl.BlockSpec(memory_space=pltpu.HBM)] * 3,
        out_specs=[pl.BlockSpec(memory_space=pltpu.VMEM)] * 2,
        scratch_shapes=[
            pltpu.VMEM(whole, f32),
            pltpu.VMEM((local, parts, kinds, rows, width), f32),
            pltpu.VMEM((rows, width), f32),
            pltpu.VMEM((2, 2, deep + 1, width), f32),
            pltpu.VMEM((2, 2, deep + 1, width), f32),
            pltpu.VMEM((2, groups, deep, lanes), f32),
            pltpu.VMEM((2, groups, deep, lanes), f32),
            pltpu.VMEM((groups, 2, deep, lanes), f32),
            pltpu.VMEM((groups, deep, lanes), f32),
            pltpu.VMEM((groups, deep, lanes), f32),
            pltpu.VMEM((groups, deep, lanes), f32),
            pltpu.VMEM((groups, kinds * pairs, half, lanes), f32),
            pltpu.VMEM((groups, kinds * pairs, half, lanes), f32),
            pltpu.VMEM((groups, half, lanes), f32),
            pltpu.VMEM((groups, half, lanes), f32),
            pltpu.VMEM(blocks, f32),
            pltpu.VMEM(blocks, f32),
            pltpu.VMEM((groups, pairs, half, lanes), f32),
            pltpu.VMEM((groups, pairs, half, lanes), f32),
            pltpu.VMEM(blocks, f32),
            dma((3,)),
            dma((3 + 2 * fields, 3)),
            dma((3 + 2 * fields, 3)),
            dma((3, 5)),
            dma((3, 5)),
            pltpu.SemaphoreType.REGULAR,
            pltpu.SemaphoreType.REGULAR,
        ],
        compiler_params=pltpu.CompilerParams(
            collective_id=0, has_side_effects=True, vmem_limit_bytes=limit
        ),
    )(*inputs)
    own = pltpu.with_memory_space_constraint(own, pltpu.VMEM)
    back = pltpu.with_memory_space_constraint(back, pltpu.VMEM)
    return pl.pallas_call(
        join_kernel,
        out_shape=jax.ShapeDtypeStruct(whole, f32),
        in_specs=[pl.BlockSpec(memory_space=pltpu.VMEM)] * 2,
        out_specs=pl.BlockSpec(memory_space=pl.ANY),
        scratch_shapes=[pltpu.VMEM((local, parts, 1, rows, width), f32), dma((2,))],
        compiler_params=pltpu.CompilerParams(vmem_limit_bytes=limit),
    )(own, back)


def solution(mesh):
    placed = (
        P("harm", None, None, ("parts", "tile"), None),
        P("harm", None, None, ("parts", "tile"), None),
        P(("parts", "tile"), None),
    )
    return jax.shard_map(
        shards,
        mesh=mesh,
        in_specs=placed,
        out_specs=P("harm", None, None, ("parts", "tile"), None),
        check_vma=False,
    )
```
